512 devices in a mesh: zg: 8 (over x, core), xy: 64 (over y, z).
Axes of the slice: x: 4, y: 8, z: 8, core: 2. Of those that a mesh axis runs over, the one named last changes fastest.
Arguments:
- source: float32 [64, 2048, 128], P('zg', 'xy'), may hold values from -4 to 4
- conductivity: float32 [64, 2048, 128], P('zg', 'xy'), may hold values from 0.5 to 4
- fluid: int32 [64, 2048, 128], P('zg', 'xy'), may hold values from 0 to 1, as said below
- pressure: float32 [64, 2048, 128], P('zg', 'xy'), may hold values from -6 to 6
Outputs:
- relaxed: float32 [64, 2048, 128], P('zg', 'xy')
- coarse: float32 [32, 1024, 64], P('zg', 'xy')
The draws below stay inside these ranges and needn't reach their ends.
Inputs may be any that keep to these rules, and one draw needn't show every extreme that they name: `fluid`: the solid cells of a column, if any, are its lowest ones.
All inputs are finite; a program needn't handle non-finite values.
Results may differ from the reference program's by a relative error of at most 0.000049.
Values sent between devices are 32-bit elements; how exact they have to be, the bound alone decides.
No kernel may reach another device: no remote copies, remote signals or barrier semaphores. Data moves between devices by JAX's collectives and lax.ppermute only.
A program may use at most 64 MiB of HBM per device.

```python
import math
import jax
import jax.numpy as jnp
from jax import lax

NY = 128
NZ = 64
NX = 2048


def draw_source(key, part):
    normal = jax.random.normal(key, (NZ, NX, NY), jnp.float32)
    return jnp.clip(normal, -4.0, 4.0)


def draw_fluid(key, part):
    base = jax.random.fold_in(key, 11)
    key_built = jax.random.fold_in(base, 1)
    key_height = jax.random.fold_in(base, 2)
    block_rows = NX // 2
    block_cols = NY // 2
    built = jax.random.randint(key_built, (block_rows, block_cols), 0, 10) < 3
    height = jax.random.randint(key_height, (block_rows, block_cols), 1, NZ // 4 + 1)
    height = jnp.where(built, height, jnp.zeros_like(height))
    height = jnp.repeat(jnp.repeat(height, 2, axis=0), 2, axis=1)
    levels = jnp.arange(NZ, dtype=jnp.int32)[:, None, None]
    return (levels >= height[None]).astype(jnp.int32)


def level_of(key, shape, cuts, least, high):
    def one(dim, parts):
        steps = jax.random.uniform(jax.random.fold_in(jax.random.fold_in(key, 6), dim), (parts,), jnp.float32, least / len(cuts), high / len(cuts))
        return jnp.repeat(jnp.exp(steps), shape[dim] // parts).reshape((-1,) + (1,) * (len(shape) - dim - 1))

    level = one(*cuts[0])
    for cut in cuts[1:]:
        level = level * one(*cut)
    return level


def normal_values(key, extent, scale, bound, cuts=(), kind=jnp.bfloat16):
    drawn = jax.random.normal(key, extent, jnp.float32) * scale
    if len(cuts) > 0:
        drawn = level_of(key, extent, cuts, -0.22, 0.18) * drawn
    return jnp.clip(drawn, min=-bound, max=bound).astype(kind)


def setup_inputs(seed: int = 0) -> dict:
    keys = jax.random.split(jax.random.key(seed), 5)
    return {
        "source": draw_source(jax.random.fold_in(keys[4], 71), 0),
        "conductivity": jnp.clip(jnp.exp(math.log(4.0) - 2.0794415 * jax.random.uniform(keys[1], (NZ, NX, NY), jnp.float32) ** level_of(keys[1], (NZ, NX, NY), ((0, 8), (1, 64)), -0.2, 0.2)), 0.5, 4.0),
        "fluid": draw_fluid(jax.random.fold_in(keys[4], 71), 0),
        "pressure": normal_values(keys[3], (NZ, NX, NY), 1.0, 6.0, ((0, 8), (1, 64)), jnp.float32),
    }


vertical_ratio = 100.0
absorption = 0.05

def thomas(lower_coef, diagonal, upper_coef, right_side):

    def forward(carried, level_row):
        ratio_prev, value_prev = carried
        sub_coef, mid_coef, sup_coef, src_term = level_row
        pivots = mid_coef - sub_coef * ratio_prev
        ratio_now = sup_coef / pivots
        value_now = (src_term - sub_coef[None] * value_prev) / pivots[None]
        return ((ratio_now, value_now), (ratio_now, value_now))
    initial = (jnp.zeros_like(diagonal[0]), jnp.zeros_like(right_side[0]))
    unused, (ratios, values) = lax.scan(forward, initial, (lower_coef, diagonal, upper_coef, right_side))

    def backward(carried, level_row):
        ratio_now, value_now = level_row
        result = value_now - ratio_now[None] * carried
        return (result, result)
    unused_end, solved = lax.scan(backward, jnp.zeros_like(right_side[0]), (ratios, values), reverse=True)
    return solved

def faces(weighted, padded):
    face_below = vertical_ratio * jnp.sqrt(weighted * padded[:-2, 1:-1, 1:-1])
    face_above = vertical_ratio * jnp.sqrt(weighted * padded[2:, 1:-1, 1:-1])
    face_west = jnp.sqrt(weighted * padded[1:-1, :-2, 1:-1])
    face_east = jnp.sqrt(weighted * padded[1:-1, 2:, 1:-1])
    face_south = jnp.sqrt(weighted * padded[1:-1, 1:-1, :-2])
    face_north = jnp.sqrt(weighted * padded[1:-1, 1:-1, 2:])
    return (face_below, face_above, face_west, face_east, face_south, face_north)

def horizontal(coefs, padded):
    return coefs[2] * padded[:, :-2, 1:-1] + coefs[3] * padded[:, 2:, 1:-1] + coefs[4] * padded[:, 1:-1, :-2] + coefs[5] * padded[:, 1:-1, 2:]

def restrict_axis(values, dimension):
    length = values.shape[dimension] - 2
    pieces = [lax.slice_in_dim(values, offset, offset + length - 1, 2, dimension) for offset in range(4)]
    return 0.125 * (pieces[0] + 3.0 * pieces[1] + 3.0 * pieces[2] + pieces[3])

def restrict(padded):
    for dimension in range(3):
        padded = restrict_axis(padded, dimension)
    return padded

def reference(source, conductivity, fluid, pressure):
    fluid_real = fluid.astype(jnp.float32)
    weighted = conductivity * fluid_real
    coefs = faces(weighted, jnp.pad(weighted, 1))
    diagonal = fluid_real * (absorption + coefs[0] + coefs[1] + coefs[2] + coefs[3] + coefs[4] + coefs[5]) + (1.0 - fluid_real)
    forcing = fluid_real * source
    grid_shape = source.shape
    parity = (lax.broadcasted_iota(jnp.int32, grid_shape, 1) + lax.broadcasted_iota(jnp.int32, grid_shape, 2)) % 2
    for colour in (0, 1):
        padded = jnp.pad(pressure, ((0, 0), (1, 1), (1, 1)))
        right_side = forcing + horizontal(coefs, padded)
        solved = thomas(-coefs[0], diagonal, -coefs[1], right_side[:, None])[:, 0]
        pressure = jnp.where(parity == colour, solved, pressure)
    full = jnp.pad(pressure, 1)
    applied = diagonal * pressure - (horizontal(coefs, full[1:-1]) + coefs[0] * full[:-2, 1:-1, 1:-1] + coefs[1] * full[2:, 1:-1, 1:-1])
    residual = forcing - applied
    coarse = restrict(jnp.pad(residual, 1))
    return (pressure, coarse)
```

```python
import jax
import jax.numpy as jnp
from jax import lax
from jax.experimental import pallas as pl
from jax.experimental.pallas import tpu as pltpu
from jax.sharding import Mesh
from jax.sharding import PartitionSpec as P

INTERPRET = False
vertical_ratio = 100.0
absorption = 0.05

LEV = 16
WIN = 24
LAN = 128
F32 = jnp.float32


def east_of(v):
    return pltpu.roll(v, WIN - 1, 0)


def west_of(v):
    return pltpu.roll(v, 1, 0)


def north_of(v):
    return pltpu.roll(v, LAN - 1, 1)


def south_of(v):
    return pltpu.roll(v, 1, 1)


def iotas():
    row = lax.broadcasted_iota(jnp.int32, (WIN, LAN), 0)
    lane = lax.broadcasted_iota(jnp.int32, (WIN, LAN), 1)
    red = ((row + lane) & 1) == 0
    return row, lane, red


def side_faces(w, last_lane):
    east = jnp.sqrt(w * east_of(w))
    north = jnp.where(last_lane, 0.0, jnp.sqrt(w * north_of(w)))
    return east, north


def horizontal(east, north, p):
    return (
        west_of(east * p)
        + east * east_of(p)
        + south_of(north * p)
        + north * north_of(p)
    )


def weigh_kernel(source, cond, fluid, pressure, out):
    real = fluid[...].astype(F32)
    out[0] = cond[...] * real
    out[1] = real * source[...]
    out[2] = pressure[...]


def edge_kernel(both, out):
    core = lax.axis_index("zk")
    start = pl.multiple_of(core * 24, 8)
    for f in range(3):
        for l in range(LEV):
            out[f, l] = both[l // 8, f, l % 8, pl.ds(start, 8), :]


def first_kernel(both, halo, send, ef, nf, vf, dg, fr, pr, rc, mm, gr, br, bg):
    core = lax.axis_index("zk")
    row, lane, red = iotas()
    last_lane = lane == LAN - 1
    row8 = lax.broadcasted_iota(jnp.int32, (8, LAN), 0)
    from_near = (row8 < 4) == (core == 0)
    own_at = pl.multiple_of(core * 16, 8)
    near_at = pl.multiple_of(16 - 8 * core, 8)

    def window(f, l):
        own = both[l // 8, f, l % 8, pl.ds(own_at, 16), :]
        near = both[l // 8, f, l % 8, pl.ds(near_at, 8), :]
        return jnp.concatenate([own, jnp.where(from_near, near, halo[f, l])], axis=0)

    w = None
    below = None
    for l in range(LEV):
        w_prev, w = w, window(0, l)
        east, north = side_faces(w, last_lane)
        ef[l] = east
        nf[l] = north
        west, south = west_of(east), south_of(north)
        if l > 0:
            below = vertical_ratio * jnp.sqrt(w * w_prev)
            vf[l] = below
        else:
            vf[l] = jnp.zeros_like(w)
            w0 = w
        fluid = jnp.where(w > 0.0, 1.0, 0.0)
        dg[l] = fluid * (absorption + (west + east + south + north)) + (1.0 - fluid)
        f = window(1, l)
        p = window(2, l)
        fr[l] = f
        pr[l] = p
    w15 = w
    bot = None
    for l in range(LEV):
        d = dg[l] + vf[l]
        if l < LEV - 1:
            d = d + vf[l + 1]
        dg[l] = d
        p = pr[l]
        b = fr[l] + horizontal(ef[l], nf[l], p)
        if l == 0:
            top_d, top_b = d, b
            continue
        v = vf[l]
        if l == 1:
            dd, bb, g = d, b, v
        else:
            dd = d - mult * v
            bb = b + mult * bb
            g = mult * g
        if l < LEV - 1:
            rcp = 1.0 / dd
            mult = vf[l + 1] * rcp
            grl = g * rcp
            rc[l] = rcp
            mm[l] = mult
            gr[l] = grl
            br[l] = bb
            top_d = top_d - g * grl
            top_b = top_b + grl * bb
    beta = gr[LEV - 2]
    gamma = mm[LEV - 2]
    bg[0] = jnp.where(red, south_of(gamma), beta)
    for l in range(LEV - 3, 0, -1):
        beta = gr[l] + mm[l] * beta
        gamma = mm[l] * gamma
    bg[1] = jnp.where(red, south_of(gamma), beta)
    packed = jnp.where(red, top_b, south_of(bb))
    for peer in range(4):
        send[peer, 0] = top_d
        send[peer, 1] = g
        send[peer, 2] = dd
        send[peer, 3] = w0
        send[peer, 4] = w15
        send[peer, 5] = packed
    bg[2] = window(0, LEV - 2)
    bg[3] = window(0, 1)


def chain_solve(rj, mj, cj, right):
    acc = [right[0]]
    for j in range(1, 8):
        acc.append(right[j] + mj[j] * acc[j - 1])
    out = [None] * 8
    out[7] = acc[7] * rj[7]
    for j in range(6, -1, -1):
        out[j] = (acc[j] + cj[j + 1] * out[j + 1]) * rj[j]
    return out


def second_kernel(got, ef, nf, vf, fr, pr, rc, mm, gr, br, bg, send, p1, bb_out, chain, u_red):
    chip = lax.axis_index("zc")
    row, lane, red = iotas()
    pivot = None
    rj, mj, cj, right = [], [], [], []
    face = None
    for j in range(8):
        group, last = j // 2, j % 2
        if last == 0:
            up = got[group, 0]
            link = face if group > 0 else None
            if group > 0:
                up = up + face
            packed = got[group, 5]
            right.append(packed)
        else:
            up = got[group, 2]
            link = got[group, 1]
            if group < 3:
                face = vertical_ratio * jnp.sqrt(got[group, 4] * got[group + 1, 3])
                up = up + face
            right.append(north_of(packed))
        if link is None:
            mj.append(None)
            cj.append(None)
            pivot = up
        else:
            m = link * rj[-1]
            mj.append(m)
            cj.append(link)
            pivot = up - m * link
        rj.append(1.0 / pivot)
        chain[0, j] = rj[j]
        if j > 0:
            chain[1, j] = mj[j]
            chain[2, j] = cj[j]
        else:
            chain[1, j] = jnp.zeros((WIN, LAN), F32)
            chain[2, j] = jnp.zeros((WIN, LAN), F32)
    sol = chain_solve(rj, mj, cj, right)
    for j in range(8):
        u_red[j] = sol[j]
    low = u_red[2 * chip]
    high = u_red[2 * chip + 1]
    p1[0] = jnp.where(red, low, pr[0])
    p1[LEV - 1] = jnp.where(red, high, pr[LEV - 1])
    cur = high
    for l in range(LEV - 2, 0, -1):
        cur = br[l] * rc[l] + gr[l] * low + mm[l] * cur
        p1[l] = jnp.where(red, cur, pr[l])
    for l in range(LEV):
        b = fr[l] + horizontal(ef[l], nf[l], p1[l])
        if l == 0:
            top_b = b
            continue
        if l == 1:
            bb = b
        else:
            bb = b + mm[l - 1] * bb
        if l < LEV - 1:
            bb_out[l] = bb
            top_b = top_b + gr[l] * bb
    bb_out[0] = jnp.zeros((WIN, LAN), F32)
    bb_out[LEV - 1] = jnp.zeros((WIN, LAN), F32)
    alpha14 = bb_out[LEV - 2] * rc[LEV - 2]
    alpha = alpha14
    for l in range(LEV - 3, 0, -1):
        alpha = bb_out[l] * rc[l] + mm[l] * alpha
    packed = jnp.where(red, south_of(bb), top_b)
    up_mix = jnp.where(red, p1[LEV - 2], alpha14)
    down_mix = jnp.where(red, p1[1], alpha)
    for peer in range(4):
        send[peer, 0] = packed

        @pl.when(chip < peer)
        def _():
            send[peer, 1] = up_mix
            send[peer, 2] = bg[0]
            send[peer, 3] = bg[2]
            send[peer, 4] = fr[LEV - 1]

        @pl.when(chip >= peer)
        def _():
            send[peer, 1] = down_mix
            send[peer, 2] = bg[1]
            send[peer, 3] = bg[3]
            send[peer, 4] = fr[0]


def third_kernel(got3, got2, ef, nf, vf, dg, fr, rc, mm, gr, bb_in, p1, chain, u_red, weights, out, u_all, full, res):
    chip = lax.axis_index("zc")
    row, lane, red = iotas()
    last_lane = lane == LAN - 1
    rj = [chain[0, j] for j in range(8)]
    mj = [chain[1, j] for j in range(8)]
    cj = [chain[2, j] for j in range(8)]
    right = []
    for group in range(4):
        packed = got3[group, 0]
        right += [packed, north_of(packed)]
    sol = chain_solve(rj, mj, cj, right)
    for j in range(8):
        u_all[j] = jnp.where(red, u_red[j], sol[j])
    low = u_all[2 * chip]
    high = u_all[2 * chip + 1]
    full[2] = low
    full[LEV + 1] = high
    cur = high
    for l in range(LEV - 2, 0, -1):
        cur = bb_in[l] * rc[l] + gr[l] * low + mm[l] * cur
        full[l + 2] = jnp.where(red, p1[l], cur)
    for l in range(LEV):
        out[l] = full[l + 2, 0:16, :]

    for side in (0, 1):
        near_chip = jnp.maximum(chip - 1, 0) if side == 0 else jnp.minimum(chip + 1, 3)
        there = chip > 0 if side == 0 else chip < 3
        mix = got3[near_chip, 1]
        pack = got3[near_chip, 2]
        w_far = got3[near_chip, 3]
        f_near = got3[near_chip, 4]
        w_near = got2[near_chip, 4 if side == 0 else 3]
        w_own = got2[chip, 3 if side == 0 else 4]
        p_low = u_all[2 * near_chip]
        p_high = u_all[2 * near_chip + 1]
        p_far = jnp.where(red, mix, mix + pack * p_low + north_of(pack) * p_high)
        p_near = p_high if side == 0 else p_low
        p_own = low if side == 0 else high
        w_near = jnp.where(there, w_near, 0.0)
        face_own = vertical_ratio * jnp.sqrt(w_near * w_own)
        face_far = vertical_ratio * jnp.sqrt(w_near * w_far)
        east, north = side_faces(w_near, last_lane)
        fluid = jnp.where(w_near > 0.0, 1.0, 0.0)
        diag = fluid * (
            absorption + (west_of(east) + east + south_of(north) + north) + face_own + face_far
        ) + (1.0 - fluid)
        applied = diag * p_near - (horizontal(east, north, p_near) + face_own * p_own + face_far * p_far)
        beyond = jnp.where(there, f_near - applied, 0.0)
        if side == 0:
            res[0] = beyond
            face_low = face_own
            p_below = p_near
        else:
            res[LEV + 1] = beyond
            face_high = face_own
            p_above = p_near
    for l in range(LEV):
        p = full[l + 2]
        d = dg[l]
        if l == 0:
            d = d + face_low
            vert = face_low * p_below + vf[1] * full[3]
        elif l == LEV - 1:
            d = d + face_high
            vert = vf[l] * full[l + 1] + face_high * p_above
        else:
            vert = vf[l] * full[l + 1] + vf[l + 1] * full[l + 3]
        applied = d * p - (horizontal(ef[l], nf[l], p) + vert)
        res[l + 1] = fr[l] - applied
    for big in range(LEV // 2):
        z = 2 * big
        s = 0.125 * (res[z] + 3.0 * res[z + 1] + 3.0 * res[z + 2] + res[z + 3])
        e = east_of(s)
        s = 0.125 * (west_of(s) + 3.0 * s + 3.0 * e + east_of(e))
        res[z] = jnp.dot(s, weights[...], precision=lax.Precision.HIGHEST, preferred_element_type=F32)
        out[LEV + big] = jnp.concatenate(
            [res[z, pl.ds(0, 8, stride=2), :], jnp.zeros((8, LAN), F32)], axis=0
        )


def last_kernel(both, relaxed, coarse):
    core = lax.axis_index("zk")
    for j in range(2):
        for l in range(8):
            relaxed[l, 16 * j : 16 * j + 16, :] = both[j, core * 8 + l]
        for big in range(4):
            coarse[big, 8 * j : 8 * j + 8, :] = both[j, LEV + core * 4 + big, 0:8, 0:64]


def call(kernel, name, shapes, scratch=(), space=pltpu.VMEM):
    vm = pl.BlockSpec(memory_space=pltpu.VMEM)

    def run(*args):
        return pl.pallas_call(
            kernel,
            out_shape=[jax.ShapeDtypeStruct(s, F32) for s in shapes],
            in_specs=[vm] * len(args),
            out_specs=[vm] * len(shapes),
            scratch_shapes=[pltpu.VMEM(s, F32) for s in scratch],
            name=name,
            interpret=INTERPRET,
        )(*args)

    return run


def restriction_matrix():
    fine = lax.broadcasted_iota(jnp.int32, (LAN, LAN), 0)
    big = lax.broadcasted_iota(jnp.int32, (LAN, LAN), 1)
    off = fine - 2 * big + 1
    inner = (off == 1) | (off == 2)
    outer = (off == 0) | (off == 3)
    return jnp.where(inner, 0.375, jnp.where(outer, 0.125, 0.0)).astype(F32)


def shards(source, conductivity, fluid, pressure):
    cell = (WIN, LAN)
    field = (LEV, WIN, LAN)
    (mine,) = call(weigh_kernel, "weigh", [(3, 8, 32, LAN)])(source, conductivity, fluid, pressure)
    both = lax.all_gather(mine, "zk", axis=0, tiled=False)
    (edge,) = call(edge_kernel, "edge", [(3, LEV, 8, LAN)])(both)
    count = lax.axis_size("xy")
    pairs = [(q, count + q - 1) for q in range(1, count)]
    pairs += [(b, a) for a, b in pairs]
    halo = lax.ppermute(edge, ("zk", "xy"), pairs)
    send2, ef, nf, vf, dg, fr, pr, rc, mm, gr, br, bg = call(
        first_kernel, "first", [(4, 6) + cell] + [field] * 10 + [(4,) + cell]
    )(both, halo)
    got2 = lax.all_to_all(send2, "zc", 0, 0, tiled=False)
    send3, p1, bb, chain, u_red = call(
        second_kernel, "second", [(4, 5) + cell, field, field, (3, 8) + cell, (8,) + cell]
    )(got2, ef, nf, vf, fr, pr, rc, mm, gr, br, bg)
    got3 = lax.all_to_all(send3, "zc", 0, 0, tiled=False)
    (done,) = call(
        third_kernel,
        "third",
        [(LEV + LEV // 2, 16, LAN)],
        [(8,) + cell, (LEV + 4,) + cell, (LEV + 2,) + cell],
    )(got3, got2, ef, nf, vf, dg, fr, rc, mm, gr, bb, p1, chain, u_red, restriction_matrix())
    ends = lax.all_gather(done, "zk", axis=0, tiled=False)
    relaxed, coarse = call(last_kernel, "last", [(8, 32, LAN), (4, 16, LAN // 2)])(ends)
    return relaxed, coarse


def solution(mesh):
    finer = Mesh(mesh.devices.reshape(4, 2, mesh.shape["xy"]), ("zc", "zk", "xy"))
    spec = P(("zc", "zk"), "xy", None)
    return jax.shard_map(shards, mesh=finer, in_specs=(spec,) * 4, out_specs=(spec,) * 2, check_vma=False)
```

```python
import jax
import jax.numpy as jnp
from jax import lax
from jax.experimental import pallas as pl
from jax.experimental.pallas import tpu as pltpu
from jax.sharding import Mesh
from jax.sharding import PartitionSpec as P

INTERPRET = False
SCOPED = 4 << 20
vertical_ratio = 100.0
absorption = 0.05

LEV = 16
WIN = 24
LAN = 128
F32 = jnp.float32


def east_of(v):
    return pltpu.roll(v, WIN - 1, 0)


def west_of(v):
    return pltpu.roll(v, 1, 0)


def north_of(v):
    return pltpu.roll(v, LAN - 1, 1)


def south_of(v):
    return pltpu.roll(v, 1, 1)


def iotas():
    row = lax.broadcasted_iota(jnp.int32, (WIN, LAN), 0)
    lane = lax.broadcasted_iota(jnp.int32, (WIN, LAN), 1)
    red = ((row + lane) & 1) == 0
    return row, lane, red


def side_faces(w, last_lane):
    east = jnp.sqrt(w * east_of(w))
    north = jnp.where(last_lane, 0.0, jnp.sqrt(w * north_of(w)))
    return east, north


def horizontal(east, north, p):
    return (
        west_of(east * p)
        + east * east_of(p)
        + south_of(north * p)
        + north * north_of(p)
    )


def weigh_kernel(source, cond, fluid, pressure, out):
    real = fluid[...].astype(F32)
    out[0] = cond[...] * real
    out[1] = real * source[...]
    out[2] = pressure[...]


def edge_kernel(both, out):
    core = lax.axis_index("zk")
    start = pl.multiple_of(core * 24, 8)
    for f in range(3):
        for l in range(LEV):
            out[f, l] = both[l // 8, f, l % 8, pl.ds(start, 8), :]


def first_kernel(both, halo, send, ef, nf, vf, dg, fr, pr, rc, mm, gr, br, bg):
    core = lax.axis_index("zk")
    row, lane, red = iotas()
    last_lane = lane == LAN - 1
    row8 = lax.broadcasted_iota(jnp.int32, (8, LAN), 0)
    from_near = (row8 < 4) == (core == 0)
    own_at = pl.multiple_of(core * 16, 8)
    near_at = pl.multiple_of(16 - 8 * core, 8)

    def window(f, l):
        own = both[l // 8, f, l % 8, pl.ds(own_at, 16), :]
        near = both[l // 8, f, l % 8, pl.ds(near_at, 8), :]
        return jnp.concatenate([own, jnp.where(from_near, near, halo[f, l])], axis=0)

    w = None
    below = None
    for l in range(LEV):
        w_prev, w = w, window(0, l)
        east, north = side_faces(w, last_lane)
        ef[l] = east
        nf[l] = north
        west, south = west_of(east), south_of(north)
        if l > 0:
            below = vertical_ratio * jnp.sqrt(w * w_prev)
            vf[l] = below
        else:
            vf[l] = jnp.zeros_like(w)
            w0 = w
        fluid = jnp.where(w > 0.0, 1.0, 0.0)
        dg[l] = fluid * (absorption + (west + east + south + north)) + (1.0 - fluid)
        f = window(1, l)
        p = window(2, l)
        fr[l] = f
        pr[l] = p
    w15 = w
    bot = None
    for l in range(LEV):
        d = dg[l] + vf[l]
        if l < LEV - 1:
            d = d + vf[l + 1]
        dg[l] = d
        p = pr[l]
        b = fr[l] + horizontal(ef[l], nf[l], p)
        if l == 0:
            top_d, top_b = d, b
            continue
        v = vf[l]
        if l == 1:
            dd, bb, g = d, b, v
        else:
            dd = d - mult * v
            bb = b + mult * bb
            g = mult * g
        if l < LEV - 1:
            rcp = 1.0 / dd
            mult = vf[l + 1] * rcp
            grl = g * rcp
            rc[l] = rcp
            mm[l] = mult
            gr[l] = grl
            br[l] = bb
            top_d = top_d - g * grl
            top_b = top_b + grl * bb
    beta = gr[LEV - 2]
    gamma = mm[LEV - 2]
    bg[0] = jnp.where(red, south_of(gamma), beta)
    for l in range(LEV - 3, 0, -1):
        beta = gr[l] + mm[l] * beta
        gamma = mm[l] * gamma
    bg[1] = jnp.where(red, south_of(gamma), beta)
    packed = jnp.where(red, top_b, south_of(bb))
    for peer in range(4):
        send[peer, 0] = top_d
        send[peer, 1] = g
        send[peer, 2] = dd
        send[peer, 3] = w0
        send[peer, 4] = w15
        send[peer, 5] = packed
    bg[2] = window(0, LEV - 2)
    bg[3] = window(0, 1)


def chain_solve(rj, mj, cj, right):
    acc = [right[0]]
    for j in range(1, 8):
        acc.append(right[j] + mj[j] * acc[j - 1])
    out = [None] * 8
    out[7] = acc[7] * rj[7]
    for j in range(6, -1, -1):
        out[j] = (acc[j] + cj[j + 1] * out[j + 1]) * rj[j]
    return out


def second_kernel(got, ef, nf, vf, fr, pr, rc, mm, gr, br, bg, send, p1, bb_out, chain, u_red):
    chip = lax.axis_index("zc")
    row, lane, red = iotas()
    pivot = None
    rj, mj, cj, right = [], [], [], []
    face = None
    for j in range(8):
        group, last = j // 2, j % 2
        if last == 0:
            up = got[group, 0]
            link = face if group > 0 else None
            if group > 0:
                up = up + face
            packed = got[group, 5]
            right.append(packed)
        else:
            up = got[group, 2]
            link = got[group, 1]
            if group < 3:
                face = vertical_ratio * jnp.sqrt(got[group, 4] * got[group + 1, 3])
                up = up + face
            right.append(north_of(packed))
        if link is None:
            mj.append(None)
            cj.append(None)
            pivot = up
        else:
            m = link * rj[-1]
            mj.append(m)
            cj.append(link)
            pivot = up - m * link
        rj.append(1.0 / pivot)
        chain[0, j] = rj[j]
        if j > 0:
            chain[1, j] = mj[j]
            chain[2, j] = cj[j]
        else:
            chain[1, j] = jnp.zeros((WIN, LAN), F32)
            chain[2, j] = jnp.zeros((WIN, LAN), F32)
    sol = chain_solve(rj, mj, cj, right)
    for j in range(8):
        u_red[j] = sol[j]
    low = u_red[2 * chip]
    high = u_red[2 * chip + 1]
    p1[0] = jnp.where(red, low, pr[0])
    p1[LEV - 1] = jnp.where(red, high, pr[LEV - 1])
    cur = high
    for l in range(LEV - 2, 0, -1):
        cur = br[l] * rc[l] + gr[l] * low + mm[l] * cur
        p1[l] = jnp.where(red, cur, pr[l])
    for l in range(LEV):
        b = fr[l] + horizontal(ef[l], nf[l], p1[l])
        if l == 0:
            top_b = b
            continue
        if l == 1:
            bb = b
        else:
            bb = b + mm[l - 1] * bb
        if l < LEV - 1:
            bb_out[l] = bb
            top_b = top_b + gr[l] * bb
    bb_out[0] = jnp.zeros((WIN, LAN), F32)
    bb_out[LEV - 1] = jnp.zeros((WIN, LAN), F32)
    alpha14 = bb_out[LEV - 2] * rc[LEV - 2]
    alpha = alpha14
    for l in range(LEV - 3, 0, -1):
        alpha = bb_out[l] * rc[l] + mm[l] * alpha
    packed = jnp.where(red, south_of(bb), top_b)
    up_mix = jnp.where(red, p1[LEV - 2], alpha14)
    down_mix = jnp.where(red, p1[1], alpha)
    for peer in range(4):
        send[peer, 0] = packed

        @pl.when(chip < peer)
        def _():
            send[peer, 1] = up_mix
            send[peer, 2] = bg[0]
            send[peer, 3] = bg[2]
            send[peer, 4] = fr[LEV - 1]

        @pl.when(chip >= peer)
        def _():
            send[peer, 1] = down_mix
            send[peer, 2] = bg[1]
            send[peer, 3] = bg[3]
            send[peer, 4] = fr[0]


def third_kernel(got3, got2, ef, nf, vf, dg, fr, rc, mm, gr, bb_in, p1, chain, u_red, weights, out, u_all, full, res):
    chip = lax.axis_index("zc")
    row, lane, red = iotas()
    last_lane = lane == LAN - 1
    rj = [chain[0, j] for j in range(8)]
    mj = [chain[1, j] for j in range(8)]
    cj = [chain[2, j] for j in range(8)]
    right = []
    for group in range(4):
        packed = got3[group, 0]
        right += [packed, north_of(packed)]
    sol = chain_solve(rj, mj, cj, right)
    for j in range(8):
        u_all[j] = jnp.where(red, u_red[j], sol[j])
    low = u_all[2 * chip]
    high = u_all[2 * chip + 1]
    full[2] = low
    full[LEV + 1] = high
    cur = high
    for l in range(LEV - 2, 0, -1):
        cur = bb_in[l] * rc[l] + gr[l] * low + mm[l] * cur
        full[l + 2] = jnp.where(red, p1[l], cur)
    for l in range(LEV):
        out[l] = full[l + 2, 0:16, :]

    for side in (0, 1):
        near_chip = jnp.maximum(chip - 1, 0) if side == 0 else jnp.minimum(chip + 1, 3)
        there = chip > 0 if side == 0 else chip < 3
        mix = got3[near_chip, 1]
        pack = got3[near_chip, 2]
        w_far = got3[near_chip, 3]
        f_near = got3[near_chip, 4]
        w_near = got2[near_chip, 4 if side == 0 else 3]
        w_own = got2[chip, 3 if side == 0 else 4]
        p_low = u_all[2 * near_chip]
        p_high = u_all[2 * near_chip + 1]
        p_far = jnp.where(red, mix, mix + pack * p_low + north_of(pack) * p_high)
        p_near = p_high if side == 0 else p_low
        p_own = low if side == 0 else high
        w_near = jnp.where(there, w_near, 0.0)
        face_own = vertical_ratio * jnp.sqrt(w_near * w_own)
        face_far = vertical_ratio * jnp.sqrt(w_near * w_far)
        east, north = side_faces(w_near, last_lane)
        fluid = jnp.where(w_near > 0.0, 1.0, 0.0)
        diag = fluid * (
            absorption + (west_of(east) + east + south_of(north) + north) + face_own + face_far
        ) + (1.0 - fluid)
        applied = diag * p_near - (horizontal(east, north, p_near) + face_own * p_own + face_far * p_far)
        beyond = jnp.where(there, f_near - applied, 0.0)
        if side == 0:
            res[0] = beyond
            face_low = face_own
            p_below = p_near
        else:
            res[LEV + 1] = beyond
            face_high = face_own
            p_above = p_near
    for l in range(LEV):
        p = full[l + 2]
        d = dg[l]
        if l == 0:
            d = d + face_low
            vert = face_low * p_below + vf[1] * full[3]
        elif l == LEV - 1:
            d = d + face_high
            vert = vf[l] * full[l + 1] + face_high * p_above
        else:
            vert = vf[l] * full[l + 1] + vf[l + 1] * full[l + 3]
        applied = d * p - (horizontal(ef[l], nf[l], p) + vert)
        res[l + 1] = fr[l] - applied
    for big in range(LEV // 2):
        z = 2 * big
        s = 0.125 * (res[z] + 3.0 * res[z + 1] + 3.0 * res[z + 2] + res[z + 3])
        e = east_of(s)
        s = 0.125 * (west_of(s) + 3.0 * s + 3.0 * e + east_of(e))
        res[z] = jnp.dot(s, weights[...], precision=lax.Precision.HIGHEST, preferred_element_type=F32)
        out[LEV + big] = jnp.concatenate(
            [res[z, pl.ds(0, 8, stride=2), :], jnp.zeros((8, LAN), F32)], axis=0
        )


def last_kernel(both, relaxed, coarse):
    core = lax.axis_index("zk")
    for j in range(2):
        for l in range(8):
            relaxed[l, 16 * j : 16 * j + 16, :] = both[j, core * 8 + l]
        for big in range(4):
            coarse[big, 8 * j : 8 * j + 8, :] = both[j, LEV + core * 4 + big, 0:8, 0:64]


def call(kernel, name, shapes, scratch=(), ends=""):
    vm = pl.BlockSpec(memory_space=pltpu.VMEM)

    def run(*args):
        if ends != "first" and not INTERPRET:
            args = [pltpu.with_memory_space_constraint(a, pltpu.VMEM) for a in args]
        plain = ends == "last" or INTERPRET
        return pl.pallas_call(
            kernel,
            out_shape=[jax.ShapeDtypeStruct(s, F32) if plain else pltpu.VMEM(s, F32) for s in shapes],
            in_specs=[vm] * len(args),
            out_specs=[vm] * len(shapes),
            scratch_shapes=[pltpu.VMEM(s, F32) for s in scratch],
            name=name,
            compiler_params=pltpu.CompilerParams(vmem_limit_bytes=SCOPED),
            interpret=INTERPRET,
        )(*args)

    return run


def restriction_matrix():
    fine = lax.broadcasted_iota(jnp.int32, (LAN, LAN), 0)
    big = lax.broadcasted_iota(jnp.int32, (LAN, LAN), 1)
    off = fine - 2 * big + 1
    inner = (off == 1) | (off == 2)
    outer = (off == 0) | (off == 3)
    return jnp.where(inner, 0.375, jnp.where(outer, 0.125, 0.0)).astype(F32)


def shards(source, conductivity, fluid, pressure):
    cell = (WIN, LAN)
    field = (LEV, WIN, LAN)
    (mine,) = call(weigh_kernel, "weigh", [(3, 8, 32, LAN)], ends="first")(source, conductivity, fluid, pressure)
    both = lax.all_gather(mine, "zk", axis=0, tiled=False)
    (edge,) = call(edge_kernel, "edge", [(3, LEV, 8, LAN)])(both)
    count = lax.axis_size("xy")
    pairs = [(q, count + q - 1) for q in range(1, count)]
    pairs += [(b, a) for a, b in pairs]
    halo = lax.ppermute(edge, ("zk", "xy"), pairs)
    send2, ef, nf, vf, dg, fr, pr, rc, mm, gr, br, bg = call(
        first_kernel, "first", [(4, 6) + cell] + [field] * 10 + [(4,) + cell]
    )(both, halo)
    got2 = lax.all_to_all(send2, "zc", 0, 0, tiled=False)
    send3, p1, bb, chain, u_red = call(
        second_kernel, "second", [(4, 5) + cell, field, field, (3, 8) + cell, (8,) + cell]
    )(got2, ef, nf, vf, fr, pr, rc, mm, gr, br, bg)
    got3 = lax.all_to_all(send3, "zc", 0, 0, tiled=False)
    (done,) = call(
        third_kernel,
        "third",
        [(LEV + LEV // 2, 16, LAN)],
        [(8,) + cell, (LEV + 4,) + cell, (LEV + 2,) + cell],
    )(got3, got2, ef, nf, vf, dg, fr, rc, mm, gr, bb, p1, chain, u_red, restriction_matrix())
    ends = lax.all_gather(done, "zk", axis=0, tiled=False)
    relaxed, coarse = call(last_kernel, "last", [(8, 32, LAN), (4, 16, LAN // 2)], ends="last")(ends)
    return relaxed, coarse


def solution(mesh):
    finer = Mesh(mesh.devices.reshape(4, 2, mesh.shape["xy"]), ("zc", "zk", "xy"))
    spec = P(("zc", "zk"), "xy", None)
    return jax.shard_map(shards, mesh=finer, in_specs=(spec,) * 4, out_specs=(spec,) * 2, check_vma=False)
```

```python
import jax
import jax.numpy as jnp
from jax import lax
from jax.experimental import pallas as pl
from jax.experimental.pallas import tpu as pltpu
from jax.sharding import Mesh
from jax.sharding import PartitionSpec as P

INTERPRET = False
SCOPED = 4 << 20
vertical_ratio = 100.0
absorption = 0.05

LEV = 16
HALF = 8
WIN = 24
LAN = 128
F32 = jnp.float32


def east_of(v):
    return pltpu.roll(v, WIN - 1, 0)


def west_of(v):
    return pltpu.roll(v, 1, 0)


def north_of(v):
    return pltpu.roll(v, LAN - 1, 1)


def south_of(v):
    return pltpu.roll(v, 1, 1)


def iotas():
    row = lax.broadcasted_iota(jnp.int32, (WIN, LAN), 0)
    lane = lax.broadcasted_iota(jnp.int32, (WIN, LAN), 1)
    red = ((row + lane) & 1) == 0
    return row, lane, red


def side_faces(w, last_lane):
    east = jnp.sqrt(w * east_of(w))
    north = jnp.where(last_lane, 0.0, jnp.sqrt(w * north_of(w)))
    return east, north


def horizontal(east, north, p):
    return (
        west_of(east * p)
        + east * east_of(p)
        + south_of(north * p)
        + north * north_of(p)
    )


def weigh_kernel(source, cond, fluid, pressure, out, cross, along, source_v, cond_v, fluid_v, sems):
    core = lax.axis_index("zk")
    copies = [
        pltpu.make_async_copy(cond, cond_v, sems.at[0]),
        pltpu.make_async_copy(fluid, fluid_v, sems.at[1]),
        pltpu.make_async_copy(source, source_v, sems.at[2]),
        pltpu.make_async_copy(pressure, out.at[2], sems.at[3]),
    ]
    for copy in copies:
        copy.start()
    for copy in copies:
        copy.wait()
    for l in range(HALF):
        real = fluid_v[l].astype(F32)
        out[0, l] = cond_v[l] * real
        out[1, l] = real * source_v[l]
    row8 = lax.broadcasted_iota(jnp.int32, (8, LAN), 0)
    for ref, high in ((cross, core), (along, 1 - core)):
        start = pl.multiple_of(high * 24, 8)
        keep = (row8 < 4) == (high == 0)
        for f in range(3):
            for l in range(4):
                one = out[f, l, pl.ds(start, 8), :]
                two = out[f, l + 4, pl.ds(start, 8), :]
                ref[f, l] = jnp.where(keep, one, pltpu.roll(two, 4, 0))


def first_kernel(both, cross, along, send, ef, nf, vf, dg, fr, pr, rc, mm, gr, br, bg):
    core = lax.axis_index("zk")
    row, lane, red = iotas()
    last_lane = lane == LAN - 1
    row8 = lax.broadcasted_iota(jnp.int32, (8, LAN), 0)
    from_near = (row8 < 4) == (core == 0)
    own_at = pl.multiple_of(core * 16, 8)
    near_at = pl.multiple_of(16 - 8 * core, 8)

    def window(f, l):
        own = both[l // 8, f, l % 8, pl.ds(own_at, 16), :]
        near = both[l // 8, f, l % 8, pl.ds(near_at, 8), :]
        straight = core == l // 8
        far = jnp.where(straight, along[f, l % 4], cross[f, l % 4])
        if l % 8 >= 4:
            far = pltpu.roll(far, 4, 0)
        return jnp.concatenate([own, jnp.where(from_near, near, far)], axis=0)

    w = None
    below = None
    for l in range(LEV):
        w_prev, w = w, window(0, l)
        east, north = side_faces(w, last_lane)
        ef[l] = east
        nf[l] = north
        west, south = west_of(east), south_of(north)
        if l > 0:
            below = vertical_ratio * jnp.sqrt(w * w_prev)
            vf[l] = below
        else:
            vf[l] = jnp.zeros_like(w)
            w0 = w
        fluid = jnp.where(w > 0.0, 1.0, 0.0)
        dg[l] = fluid * (absorption + (west + east + south + north)) + (1.0 - fluid)
        f = window(1, l)
        p = window(2, l)
        fr[l] = f
        pr[l] = p
    w15 = w
    bot = None
    for l in range(LEV):
        d = dg[l] + vf[l]
        if l < LEV - 1:
            d = d + vf[l + 1]
        dg[l] = d
        p = pr[l]
        b = fr[l] + horizontal(ef[l], nf[l], p)
        if l == 0:
            top_d, top_b = d, b
            continue
        v = vf[l]
        if l == 1:
            dd, bb, g = d, b, v
        else:
            dd = d - mult * v
            bb = b + mult * bb
            g = mult * g
        if l < LEV - 1:
            rcp = 1.0 / dd
            mult = vf[l + 1] * rcp
            grl = g * rcp
            rc[l] = rcp
            mm[l] = mult
            gr[l] = grl
            br[l] = bb
            top_d = top_d - g * grl
            top_b = top_b + grl * bb
    beta = gr[LEV - 2]
    gamma = mm[LEV - 2]
    far = vf[LEV - 1]
    bg[0] = jnp.where(red, south_of(far * gamma), far * beta)
    for l in range(LEV - 3, 0, -1):
        beta = gr[l] + mm[l] * beta
        gamma = mm[l] * gamma
    far = vf[1]
    bg[1] = jnp.where(red, south_of(far * gamma), far * beta)
    packed = jnp.where(red, top_b, south_of(bb))
    for peer in range(4):
        send[peer, 0] = top_d
        send[peer, 1] = g
        send[peer, 2] = dd
        send[peer, 3] = w0
        send[peer, 4] = w15
        send[peer, 5] = packed


def chain_solve(rj, mj, cj, right):
    acc = [right[0]]
    for j in range(1, 8):
        acc.append(right[j] + mj[j] * acc[j - 1])
    out = [None] * 8
    out[7] = acc[7] * rj[7]
    for j in range(6, -1, -1):
        out[j] = (acc[j] + cj[j + 1] * out[j + 1]) * rj[j]
    return out


def second_kernel(got, ef, nf, vf, fr, pr, rc, mm, gr, br, bg, send, p1, bb_out, chain, u_red):
    chip = lax.axis_index("zc")
    row, lane, red = iotas()
    pivot = None
    rj, mj, cj, right = [], [], [], []
    face = None
    for j in range(8):
        group, last = j // 2, j % 2
        if last == 0:
            up = got[group, 0]
            link = face if group > 0 else None
            if group > 0:
                up = up + face
            packed = got[group, 5]
            right.append(packed)
        else:
            up = got[group, 2]
            link = got[group, 1]
            if group < 3:
                face = vertical_ratio * jnp.sqrt(got[group, 4] * got[group + 1, 3])
                up = up + face
            right.append(north_of(packed))
        if link is None:
            mj.append(None)
            cj.append(None)
            pivot = up
        else:
            m = link * rj[-1]
            mj.append(m)
            cj.append(link)
            pivot = up - m * link
        rj.append(1.0 / pivot)
        chain[0, j] = rj[j]
        if j > 0:
            chain[1, j] = mj[j]
            chain[2, j] = cj[j]
        else:
            chain[1, j] = jnp.zeros((WIN, LAN), F32)
            chain[2, j] = jnp.zeros((WIN, LAN), F32)
    sol = chain_solve(rj, mj, cj, right)
    for j in range(8):
        u_red[j] = sol[j]
    low = u_red[2 * chip]
    high = u_red[2 * chip + 1]
    p1[0] = jnp.where(red, low, pr[0])
    p1[LEV - 1] = jnp.where(red, high, pr[LEV - 1])
    cur = high
    for l in range(LEV - 2, 0, -1):
        cur = br[l] * rc[l] + gr[l] * low + mm[l] * cur
        p1[l] = jnp.where(red, cur, pr[l])
    for l in range(LEV):
        b = fr[l] + horizontal(ef[l], nf[l], p1[l])
        if l == 0:
            top_b = b
            continue
        if l == 1:
            bb = b
        else:
            bb = b + mm[l - 1] * bb
        if l < LEV - 1:
            bb_out[l] = bb
            top_b = top_b + gr[l] * bb
    bb_out[0] = jnp.zeros((WIN, LAN), F32)
    bb_out[LEV - 1] = jnp.zeros((WIN, LAN), F32)
    alpha14 = bb_out[LEV - 2] * rc[LEV - 2]
    alpha = alpha14
    for l in range(LEV - 3, 0, -1):
        alpha = bb_out[l] * rc[l] + mm[l] * alpha
    packed = jnp.where(red, south_of(bb), top_b)
    up_mix = fr[LEV - 1] + vf[LEV - 1] * jnp.where(red, p1[LEV - 2], alpha14)
    down_mix = fr[0] + vf[1] * jnp.where(red, p1[1], alpha)
    for peer in range(4):
        send[peer, 0] = packed

        @pl.when(chip < peer)
        def _():
            send[peer, 1] = up_mix
            send[peer, 2] = bg[0]
            send[peer, 3] = vf[LEV - 1]

        @pl.when(chip >= peer)
        def _():
            send[peer, 1] = down_mix
            send[peer, 2] = bg[1]
            send[peer, 3] = vf[1]


def third_kernel(got3, got2, ef, nf, vf, dg, fr, rc, mm, gr, bb_in, p1, chain, u_red, out, u_all, full, res):
    chip = lax.axis_index("zc")
    row, lane, red = iotas()
    last_lane = lane == LAN - 1
    rj = [chain[0, j] for j in range(8)]
    mj = [chain[1, j] for j in range(8)]
    cj = [chain[2, j] for j in range(8)]
    right = []
    for group in range(4):
        packed = got3[group, 0]
        right += [packed, north_of(packed)]
    sol = chain_solve(rj, mj, cj, right)
    for j in range(8):
        u_all[j] = jnp.where(red, u_red[j], sol[j])
    low = u_all[2 * chip]
    high = u_all[2 * chip + 1]
    full[2] = low
    full[LEV + 1] = high
    cur = high
    for l in range(LEV - 2, 0, -1):
        cur = bb_in[l] * rc[l] + gr[l] * low + mm[l] * cur
        full[l + 2] = jnp.where(red, p1[l], cur)
    for l in range(LEV):
        out[l] = full[l + 2, 0:16, :]

    for side in (0, 1):
        near_chip = jnp.maximum(chip - 1, 0) if side == 0 else jnp.minimum(chip + 1, 3)
        there = chip > 0 if side == 0 else chip < 3
        mix = got3[near_chip, 1]
        pack = got3[near_chip, 2]
        face_far = got3[near_chip, 3]
        w_near = got2[near_chip, 4 if side == 0 else 3]
        w_own = got2[chip, 3 if side == 0 else 4]
        p_low = u_all[2 * near_chip]
        p_high = u_all[2 * near_chip + 1]
        inside = jnp.where(red, mix, mix + pack * p_low + north_of(pack) * p_high)
        p_near = p_high if side == 0 else p_low
        p_own = low if side == 0 else high
        w_near = jnp.where(there, w_near, 0.0)
        face_own = vertical_ratio * jnp.sqrt(w_near * w_own)
        east, north = side_faces(w_near, last_lane)
        fluid = jnp.where(w_near > 0.0, 1.0, 0.0)
        diag = fluid * (
            absorption + (west_of(east) + east + south_of(north) + north) + face_own + face_far
        ) + (1.0 - fluid)
        beyond = inside - (diag * p_near - (horizontal(east, north, p_near) + face_own * p_own))
        beyond = jnp.where(there, beyond, 0.0)
        if side == 0:
            res[0] = beyond
            face_low = face_own
            p_below = p_near
        else:
            res[LEV + 1] = beyond
            face_high = face_own
            p_above = p_near
    for l in range(LEV):
        p = full[l + 2]
        d = dg[l]
        if l == 0:
            d = d + face_low
            vert = face_low * p_below + vf[1] * full[3]
        elif l == LEV - 1:
            d = d + face_high
            vert = vf[l] * full[l + 1] + face_high * p_above
        else:
            vert = vf[l] * full[l + 1] + vf[l + 1] * full[l + 3]
        applied = d * p - (horizontal(ef[l], nf[l], p) + vert)
        res[l + 1] = fr[l] - applied
    weights = restriction_matrix()
    for big in range(LEV // 2):
        z = 2 * big
        s = 0.125 * (res[z] + 3.0 * res[z + 1] + 3.0 * res[z + 2] + res[z + 3])
        e = east_of(s)
        s = 0.125 * (west_of(s) + 3.0 * s + 3.0 * e + east_of(e))
        res[z] = jnp.dot(s, weights, precision=lax.Precision.HIGHEST, preferred_element_type=F32)
        out[LEV + big] = jnp.concatenate(
            [res[z, pl.ds(0, 8, stride=2), :], jnp.zeros((8, LAN), F32)], axis=0
        )


def last_kernel(both, relaxed, coarse):
    core = lax.axis_index("zk")
    for j in range(2):
        for l in range(8):
            relaxed[l, 16 * j : 16 * j + 16, :] = both[j, core * 8 + l]
        for big in range(4):
            coarse[big, 8 * j : 8 * j + 8, :] = both[j, LEV + core * 4 + big, 0:8, 0:64]


def restriction_matrix():
    fine = lax.broadcasted_iota(jnp.int32, (LAN, LAN), 0)
    big = lax.broadcasted_iota(jnp.int32, (LAN, LAN), 1)
    off = fine - 2 * big + 1
    inner = (off == 1) | (off == 2)
    outer = (off == 0) | (off == 3)
    return jnp.where(inner, 0.375, jnp.where(outer, 0.125, 0.0)).astype(F32)


def call(kernel, name, shapes, scratch=(), ends=""):
    vm = pl.BlockSpec(memory_space=pltpu.VMEM)
    main = pl.BlockSpec(memory_space=pltpu.HBM)

    def run(*args):
        if not INTERPRET:
            space = pltpu.HBM if ends == "first" else pltpu.VMEM
            args = [pltpu.with_memory_space_constraint(a, space) for a in args]
        plain = ends == "last" or INTERPRET
        return pl.pallas_call(
            kernel,
            out_shape=[jax.ShapeDtypeStruct(s, F32) if plain else pltpu.VMEM(s, F32) for s in shapes],
            in_specs=[main if ends == "first" else vm] * len(args),
            out_specs=[vm] * len(shapes),
            scratch_shapes=scratch,
            name=name,
            compiler_params=pltpu.CompilerParams(vmem_limit_bytes=SCOPED),
            interpret=INTERPRET,
        )(*args)

    return run


def shards(source, conductivity, fluid, pressure):
    cell = (WIN, LAN)
    field = (LEV, WIN, LAN)
    block = (HALF, 32, LAN)
    edge = (3, 4, 8, LAN)
    vmem = pltpu.VMEM
    mine, cross, along = call(
        weigh_kernel,
        "weigh",
        [(3,) + block, edge, edge],
        [vmem(block, F32), vmem(block, F32), vmem(block, jnp.int32), pltpu.SemaphoreType.DMA((4,))],
        ends="first",
    )(source, conductivity, fluid, pressure)
    count = lax.axis_size("xy")
    swap = [(q, count + q - 1) for q in range(1, count)]
    swap += [(b, a) for a, b in swap]
    shift = [(q, q + 1) for q in range(count - 1)] + [(count + q + 1, count + q) for q in range(count - 1)]
    cross = lax.ppermute(cross, ("zk", "xy"), swap)
    along = lax.ppermute(along, ("zk", "xy"), shift)
    both = lax.all_gather(mine, "zk", axis=0, tiled=False)
    send2, ef, nf, vf, dg, fr, pr, rc, mm, gr, br, bg = call(
        first_kernel, "first", [(4, 6) + cell] + [field] * 10 + [(2,) + cell]
    )(both, cross, along)
    got2 = lax.all_to_all(send2, "zc", 0, 0, tiled=False)
    send3, p1, bb, chain, u_red = call(
        second_kernel, "second", [(4, 4) + cell, field, field, (3, 8) + cell, (8,) + cell]
    )(got2, ef, nf, vf, fr, pr, rc, mm, gr, br, bg)
    got3 = lax.all_to_all(send3, "zc", 0, 0, tiled=False)
    (done,) = call(
        third_kernel,
        "third",
        [(LEV + LEV // 2, 16, LAN)],
        [vmem((8,) + cell, F32), vmem((LEV + 4,) + cell, F32), vmem((LEV + 2,) + cell, F32)],
    )(got3, got2, ef, nf, vf, dg, fr, rc, mm, gr, bb, p1, chain, u_red)
    ends = lax.all_gather(done, "zk", axis=0, tiled=False)
    relaxed, coarse = call(last_kernel, "last", [block, (4, 16, LAN // 2)], ends="last")(ends)
    return relaxed, coarse


def solution(mesh):
    finer = Mesh(mesh.devices.reshape(4, 2, mesh.shape["xy"]), ("zc", "zk", "xy"))
    spec = P(("zc", "zk"), "xy", None)
    return jax.shard_map(shards, mesh=finer, in_specs=(spec,) * 4, out_specs=(spec,) * 2, check_vma=False)
```

```python
import jax
import jax.numpy as jnp
from jax import lax
from jax.experimental import pallas as pl
from jax.experimental.pallas import tpu as pltpu
from jax.sharding import Mesh
from jax.sharding import PartitionSpec as P

INTERPRET = False
AXES = ("zc", "zk", "xy")
SCOPED = 4 << 20
vertical_ratio = 100.0
absorption = 0.05

LEV = 16
HALF = 8
WIN = 24
LAN = 128
F32 = jnp.float32


def east_of(v):
    return pltpu.roll(v, WIN - 1, 0)


def west_of(v):
    return pltpu.roll(v, 1, 0)


def north_of(v):
    return pltpu.roll(v, LAN - 1, 1)


def south_of(v):
    return pltpu.roll(v, 1, 1)


def iotas():
    row = lax.broadcasted_iota(jnp.int32, (WIN, LAN), 0)
    lane = lax.broadcasted_iota(jnp.int32, (WIN, LAN), 1)
    red = ((row + lane) & 1) == 0
    return row, lane, red


def side_faces(w, last_lane):
    east = jnp.sqrt(w * east_of(w))
    north = jnp.where(last_lane, 0.0, jnp.sqrt(w * north_of(w)))
    return east, north


def horizontal(east, north, p):
    return (
        west_of(east * p)
        + east * east_of(p)
        + south_of(north * p)
        + north * north_of(p)
    )


def weigh_kernel(source, cond, fluid, pressure, out, source_v, cond_v, fluid_v, sems):
    copies = [
        pltpu.make_async_copy(cond, cond_v, sems.at[0]),
        pltpu.make_async_copy(fluid, fluid_v, sems.at[1]),
        pltpu.make_async_copy(source, source_v, sems.at[2]),
        pltpu.make_async_copy(pressure, out.at[2], sems.at[3]),
    ]
    for copy in copies:
        copy.start()
    for copy in copies:
        copy.wait()
    for l in range(HALF):
        real = fluid_v[l].astype(F32)
        out[0, l] = cond_v[l] * real
        out[1, l] = real * source_v[l]


def edge_kernel(both, out):
    core = lax.axis_index("zk")
    start = pl.multiple_of(core * 24, 8)
    keep = (lax.broadcasted_iota(jnp.int32, (8, LAN), 0) < 4) == (core == 0)
    for f in range(3):
        for l in range(HALF):
            low = both[0, f, l, pl.ds(start, 8), :]
            high = both[1, f, l, pl.ds(start, 8), :]
            out[f, l] = jnp.where(keep, low, pltpu.roll(high, 4, 0))


def first_kernel(both, halo, send, ef, nf, vf, dg, fr, pr, rc, mm, gr, br, bg):
    core = lax.axis_index("zk")
    row, lane, red = iotas()
    last_lane = lane == LAN - 1
    row8 = lax.broadcasted_iota(jnp.int32, (8, LAN), 0)
    from_near = (row8 < 4) == (core == 0)
    own_at = pl.multiple_of(core * 16, 8)
    near_at = pl.multiple_of(16 - 8 * core, 8)
    block = lax.axis_index("xy")
    inside = jnp.where(core == 0, block > 0, block < lax.axis_size("xy") - 1)

    def window(f, l):
        own = both[l // 8, f, l % 8, pl.ds(own_at, 16), :]
        near = both[l // 8, f, l % 8, pl.ds(near_at, 8), :]
        far = jnp.where(inside, halo[1 - core, f, l % 8], 0.0)
        if l >= HALF:
            far = pltpu.roll(far, 4, 0)
        return jnp.concatenate([own, jnp.where(from_near, near, far)], axis=0)

    w = None
    below = None
    for l in range(LEV):
        w_prev, w = w, window(0, l)
        east, north = side_faces(w, last_lane)
        ef[l] = east
        nf[l] = north
        west, south = west_of(east), south_of(north)
        if l > 0:
            below = vertical_ratio * jnp.sqrt(w * w_prev)
            vf[l] = below
        else:
            vf[l] = jnp.zeros_like(w)
            w0 = w
        fluid = jnp.where(w > 0.0, 1.0, 0.0)
        dg[l] = fluid * (absorption + (west + east + south + north)) + (1.0 - fluid)
        f = window(1, l)
        p = window(2, l)
        fr[l] = f
        pr[l] = p
    w15 = w
    bot = None
    for l in range(LEV):
        d = dg[l] + vf[l]
        if l < LEV - 1:
            d = d + vf[l + 1]
        dg[l] = d
        p = pr[l]
        b = fr[l] + horizontal(ef[l], nf[l], p)
        if l == 0:
            top_d, top_b = d, b
            continue
        v = vf[l]
        if l == 1:
            dd, bb, g = d, b, v
        else:
            dd = d - mult * v
            bb = b + mult * bb
            g = mult * g
        if l < LEV - 1:
            rcp = 1.0 / dd
            mult = vf[l + 1] * rcp
            grl = g * rcp
            rc[l] = rcp
            mm[l] = mult
            gr[l] = grl
            br[l] = bb
            top_d = top_d - g * grl
            top_b = top_b + grl * bb
    beta = gr[LEV - 2]
    gamma = mm[LEV - 2]
    far = vf[LEV - 1]
    bg[0] = jnp.where(red, south_of(far * gamma), far * beta)
    for l in range(LEV - 3, 0, -1):
        beta = gr[l] + mm[l] * beta
        gamma = mm[l] * gamma
    far = vf[1]
    bg[1] = jnp.where(red, south_of(far * gamma), far * beta)
    packed = jnp.where(red, top_b, south_of(bb))
    for peer in range(4):
        send[peer, 0] = top_d
        send[peer, 1] = g
        send[peer, 2] = dd
        send[peer, 3] = w0
        send[peer, 4] = w15
        send[peer, 5] = packed


def chain_solve(rj, mj, cj, right):
    acc = [right[0]]
    for j in range(1, 8):
        acc.append(right[j] + mj[j] * acc[j - 1])
    out = [None] * 8
    out[7] = acc[7] * rj[7]
    for j in range(6, -1, -1):
        out[j] = (acc[j] + cj[j + 1] * out[j + 1]) * rj[j]
    return out


def second_kernel(got, ef, nf, vf, fr, pr, rc, mm, gr, br, bg, send, p1, bb_out, chain, u_red):
    chip = lax.axis_index("zc")
    row, lane, red = iotas()
    pivot = None
    rj, mj, cj, right = [], [], [], []
    face = None
    for j in range(8):
        group, last = j // 2, j % 2
        if last == 0:
            up = got[group, 0]
            link = face if group > 0 else None
            if group > 0:
                up = up + face
            packed = got[group, 5]
            right.append(packed)
        else:
            up = got[group, 2]
            link = got[group, 1]
            if group < 3:
                face = vertical_ratio * jnp.sqrt(got[group, 4] * got[group + 1, 3])
                up = up + face
            right.append(north_of(packed))
        if link is None:
            mj.append(None)
            cj.append(None)
            pivot = up
        else:
            m = link * rj[-1]
            mj.append(m)
            cj.append(link)
            pivot = up - m * link
        rj.append(1.0 / pivot)
        chain[0, j] = rj[j]
        if j > 0:
            chain[1, j] = mj[j]
            chain[2, j] = cj[j]
        else:
            chain[1, j] = jnp.zeros((WIN, LAN), F32)
            chain[2, j] = jnp.zeros((WIN, LAN), F32)
    sol = chain_solve(rj, mj, cj, right)
    for j in range(8):
        u_red[j] = sol[j]
    low = u_red[2 * chip]
    high = u_red[2 * chip + 1]
    p1[0] = jnp.where(red, low, pr[0])
    p1[LEV - 1] = jnp.where(red, high, pr[LEV - 1])
    cur = high
    for l in range(LEV - 2, 0, -1):
        cur = br[l] * rc[l] + gr[l] * low + mm[l] * cur
        p1[l] = jnp.where(red, cur, pr[l])
    for l in range(LEV):
        b = fr[l] + horizontal(ef[l], nf[l], p1[l])
        if l == 0:
            top_b = b
            continue
        if l == 1:
            bb = b
        else:
            bb = b + mm[l - 1] * bb
        if l < LEV - 1:
            bb_out[l] = bb
            top_b = top_b + gr[l] * bb
    bb_out[0] = jnp.zeros((WIN, LAN), F32)
    bb_out[LEV - 1] = jnp.zeros((WIN, LAN), F32)
    alpha14 = bb_out[LEV - 2] * rc[LEV - 2]
    alpha = alpha14
    for l in range(LEV - 3, 0, -1):
        alpha = bb_out[l] * rc[l] + mm[l] * alpha
    packed = jnp.where(red, south_of(bb), top_b)
    up_mix = fr[LEV - 1] + vf[LEV - 1] * jnp.where(red, p1[LEV - 2], alpha14)
    down_mix = fr[0] + vf[1] * jnp.where(red, p1[1], alpha)
    for peer in range(4):
        send[peer, 0] = packed

        @pl.when(chip < peer)
        def _():
            send[peer, 1] = up_mix
            send[peer, 2] = bg[0]
            send[peer, 3] = vf[LEV - 1]

        @pl.when(chip >= peer)
        def _():
            send[peer, 1] = down_mix
            send[peer, 2] = bg[1]
            send[peer, 3] = vf[1]


def third_kernel(got3, got2, ef, nf, vf, dg, fr, rc, mm, gr, bb_in, p1, chain, u_red, out, u_all, full, res):
    chip = lax.axis_index("zc")
    row, lane, red = iotas()
    last_lane = lane == LAN - 1
    rj = [chain[0, j] for j in range(8)]
    mj = [chain[1, j] for j in range(8)]
    cj = [chain[2, j] for j in range(8)]
    right = []
    for group in range(4):
        packed = got3[group, 0]
        right += [packed, north_of(packed)]
    sol = chain_solve(rj, mj, cj, right)
    for j in range(8):
        u_all[j] = jnp.where(red, u_red[j], sol[j])
    low = u_all[2 * chip]
    high = u_all[2 * chip + 1]
    full[2] = low
    full[LEV + 1] = high
    cur = high
    for l in range(LEV - 2, 0, -1):
        cur = bb_in[l] * rc[l] + gr[l] * low + mm[l] * cur
        full[l + 2] = jnp.where(red, p1[l], cur)
    for l in range(LEV):
        out[l] = full[l + 2, 0:16, :]

    for side in (0, 1):
        near_chip = jnp.maximum(chip - 1, 0) if side == 0 else jnp.minimum(chip + 1, 3)
        there = chip > 0 if side == 0 else chip < 3
        mix = got3[near_chip, 1]
        pack = got3[near_chip, 2]
        face_far = got3[near_chip, 3]
        w_near = got2[near_chip, 4 if side == 0 else 3]
        w_own = got2[chip, 3 if side == 0 else 4]
        p_low = u_all[2 * near_chip]
        p_high = u_all[2 * near_chip + 1]
        inside = jnp.where(red, mix, mix + pack * p_low + north_of(pack) * p_high)
        p_near = p_high if side == 0 else p_low
        p_own = low if side == 0 else high
        w_near = jnp.where(there, w_near, 0.0)
        face_own = vertical_ratio * jnp.sqrt(w_near * w_own)
        east, north = side_faces(w_near, last_lane)
        fluid = jnp.where(w_near > 0.0, 1.0, 0.0)
        diag = fluid * (
            absorption + (west_of(east) + east + south_of(north) + north) + face_own + face_far
        ) + (1.0 - fluid)
        beyond = inside - (diag * p_near - (horizontal(east, north, p_near) + face_own * p_own))
        beyond = jnp.where(there, beyond, 0.0)
        if side == 0:
            res[0] = beyond
            face_low = face_own
            p_below = p_near
        else:
            res[LEV + 1] = beyond
            face_high = face_own
            p_above = p_near
    for l in range(LEV):
        p = full[l + 2]
        d = dg[l]
        if l == 0:
            d = d + face_low
            vert = face_low * p_below + vf[1] * full[3]
        elif l == LEV - 1:
            d = d + face_high
            vert = vf[l] * full[l + 1] + face_high * p_above
        else:
            vert = vf[l] * full[l + 1] + vf[l + 1] * full[l + 3]
        applied = d * p - (horizontal(ef[l], nf[l], p) + vert)
        res[l + 1] = fr[l] - applied
    weights = restriction_matrix()
    for big in range(LEV // 2):
        z = 2 * big
        s = 0.125 * (res[z] + 3.0 * res[z + 1] + 3.0 * res[z + 2] + res[z + 3])
        e = east_of(s)
        s = 0.125 * (west_of(s) + 3.0 * s + 3.0 * e + east_of(e))
        res[z] = jnp.dot(s, weights, precision=lax.Precision.HIGHEST, preferred_element_type=F32)
        out[LEV + big] = jnp.concatenate(
            [res[z, pl.ds(0, 8, stride=2), :], jnp.zeros((8, LAN), F32)], axis=0
        )


def last_kernel(both, relaxed, coarse):
    core = lax.axis_index("zk")
    for j in range(2):
        for l in range(8):
            relaxed[l, 16 * j : 16 * j + 16, :] = both[j, core * 8 + l]
        for big in range(4):
            coarse[big, 8 * j : 8 * j + 8, :] = both[j, LEV + core * 4 + big, 0:8, 0:64]


def restriction_matrix():
    fine = lax.broadcasted_iota(jnp.int32, (LAN, LAN), 0)
    big = lax.broadcasted_iota(jnp.int32, (LAN, LAN), 1)
    off = fine - 2 * big + 1
    inner = (off == 1) | (off == 2)
    outer = (off == 0) | (off == 3)
    return jnp.where(inner, 0.375, jnp.where(outer, 0.125, 0.0)).astype(F32)


def call(kernel, name, shapes, scratch=(), ends=""):
    vm = pl.BlockSpec(memory_space=pltpu.VMEM)
    main = pl.BlockSpec(memory_space=pltpu.HBM)

    def run(*args):
        if not INTERPRET:
            space = pltpu.HBM if ends == "first" else pltpu.VMEM
            args = [pltpu.with_memory_space_constraint(a, space) for a in args]
        plain = ends == "last" or INTERPRET
        return pl.pallas_call(
            kernel,
            out_shape=[jax.ShapeDtypeStruct(s, F32) if plain else pltpu.VMEM(s, F32) for s in shapes],
            in_specs=[main if ends == "first" else vm] * len(args),
            out_specs=[vm] * len(shapes),
            scratch_shapes=scratch,
            name=name,
            compiler_params=pltpu.CompilerParams(vmem_limit_bytes=SCOPED),
            interpret=INTERPRET,
        )(*args)

    return run


def side_by_side():
    chips, cores, count = (lax.axis_size(axis) for axis in AXES)

    def number(chip, core, q):
        return (chip * cores + core) * count + q

    groups = [[number(c, 0, q), number(c, 1, q - 1)] for c in range(chips) for q in range(1, count)]
    for c in range(0, chips, 2):
        groups.append([number(c, 0, 0), number(c + 1, 0, 0)])
        groups.append([number(c, 1, count - 1), number(c + 1, 1, count - 1)])
    return groups


def shards(source, conductivity, fluid, pressure):
    cell = (WIN, LAN)
    field = (LEV, WIN, LAN)
    block = (HALF, 32, LAN)
    vmem = pltpu.VMEM
    (mine,) = call(
        weigh_kernel,
        "weigh",
        [(3,) + block],
        [vmem(block, F32), vmem(block, F32), vmem(block, jnp.int32), pltpu.SemaphoreType.DMA((4,))],
        ends="first",
    )(source, conductivity, fluid, pressure)
    both = lax.all_gather(mine, "zk", axis=0, tiled=False)
    (edge,) = call(edge_kernel, "edge", [(3, HALF, 8, LAN)])(both)
    halo = lax.all_gather(edge, AXES, axis=0, tiled=False, axis_index_groups=side_by_side())
    send2, ef, nf, vf, dg, fr, pr, rc, mm, gr, br, bg = call(
        first_kernel, "first", [(4, 6) + cell] + [field] * 10 + [(2,) + cell]
    )(both, halo)
    got2 = lax.all_to_all(send2, "zc", 0, 0, tiled=False)
    send3, p1, bb, chain, u_red = call(
        second_kernel, "second", [(4, 4) + cell, field, field, (3, 8) + cell, (8,) + cell]
    )(got2, ef, nf, vf, fr, pr, rc, mm, gr, br, bg)
    got3 = lax.all_to_all(send3, "zc", 0, 0, tiled=False)
    (done,) = call(
        third_kernel,
        "third",
        [(LEV + LEV // 2, 16, LAN)],
        [vmem((8,) + cell, F32), vmem((LEV + 4,) + cell, F32), vmem((LEV + 2,) + cell, F32)],
    )(got3, got2, ef, nf, vf, dg, fr, rc, mm, gr, bb, p1, chain, u_red)
    ends = lax.all_gather(done, "zk", axis=0, tiled=False)
    relaxed, coarse = call(last_kernel, "last", [block, (4, 16, LAN // 2)], ends="last")(ends)
    return relaxed, coarse


def solution(mesh):
    finer = Mesh(mesh.devices.reshape(4, 2, mesh.shape["xy"]), AXES)
    spec = P(("zc", "zk"), "xy", None)
    return jax.shard_map(shards, mesh=finer, in_specs=(spec,) * 4, out_specs=(spec,) * 2, check_vma=False)
```

```python
import jax
import jax.numpy as jnp
from jax import lax
from jax.experimental import pallas as pl
from jax.experimental.pallas import tpu as pltpu
from jax.sharding import Mesh
from jax.sharding import PartitionSpec as P

INTERPRET = False
AXES = ("zc", "zk", "xy")
SCOPED = 4 << 20
vertical_ratio = 100.0
absorption = 0.05

LEV = 16
HALF = 8
COMMON = 15
SENT = 18
WIN = 24
LAN = 128
F32 = jnp.float32


def east_of(v):
    return pltpu.roll(v, WIN - 1, 0)


def west_of(v):
    return pltpu.roll(v, 1, 0)


def north_of(v):
    return pltpu.roll(v, LAN - 1, 1)


def south_of(v):
    return pltpu.roll(v, 1, 1)


def iotas():
    row = lax.broadcasted_iota(jnp.int32, (WIN, LAN), 0)
    lane = lax.broadcasted_iota(jnp.int32, (WIN, LAN), 1)
    red = ((row + lane) & 1) == 0
    return row, lane, red


def side_faces(w, last_lane):
    east = jnp.sqrt(w * east_of(w))
    north = jnp.where(last_lane, 0.0, jnp.sqrt(w * north_of(w)))
    return east, north


def horizontal(east, north, p):
    return (
        west_of(east * p)
        + east * east_of(p)
        + south_of(north * p)
        + north * north_of(p)
    )


def weigh_kernel(source, cond, fluid, pressure, out, source_v, cond_v, fluid_v, sems):
    copies = [
        pltpu.make_async_copy(cond, cond_v, sems.at[0]),
        pltpu.make_async_copy(fluid, fluid_v, sems.at[1]),
        pltpu.make_async_copy(source, source_v, sems.at[2]),
        pltpu.make_async_copy(pressure, out.at[2], sems.at[3]),
    ]
    for copy in copies:
        copy.start()
    for copy in copies:
        copy.wait()
    for l in range(HALF):
        real = fluid_v[l].astype(F32)
        out[0, l] = cond_v[l] * real
        out[1, l] = real * source_v[l]


def edge_kernel(both, out):
    core = lax.axis_index("zk")
    start = pl.multiple_of(core * 24, 8)
    keep = (lax.broadcasted_iota(jnp.int32, (8, LAN), 0) < 4) == (core == 0)
    for f in range(3):
        for l in range(HALF):
            low = both[0, f, l, pl.ds(start, 8), :]
            high = both[1, f, l, pl.ds(start, 8), :]
            out[f, l] = jnp.where(keep, low, pltpu.roll(high, 4, 0))


def first_kernel(both, halo, send, ef, nf, vf, dg, fr, rc, mm, al, be, ga):
    core = lax.axis_index("zk")
    row, lane, red = iotas()
    last_lane = lane == LAN - 1
    row8 = lax.broadcasted_iota(jnp.int32, (8, LAN), 0)
    from_near = (row8 < 4) == (core == 0)
    own_at = pl.multiple_of(core * 16, 8)
    near_at = pl.multiple_of(16 - 8 * core, 8)
    block = lax.axis_index("xy")
    inside = jnp.where(core == 0, block > 0, block < lax.axis_size("xy") - 1)

    def window(f, l):
        own = both[l // 8, f, l % 8, pl.ds(own_at, 16), :]
        near = both[l // 8, f, l % 8, pl.ds(near_at, 8), :]
        far = jnp.where(inside, halo[1 - core, f, l % 8], 0.0)
        if l >= HALF:
            far = pltpu.roll(far, 4, 0)
        return jnp.concatenate([own, jnp.where(from_near, near, far)], axis=0)

    for l in range(LEV):
        w = window(0, l)
        east, north = side_faces(w, last_lane)
        ef[l] = east
        nf[l] = north
        if l == 0:
            w0 = w
            vf[0] = jnp.zeros_like(w)
        else:
            vf[l] = vertical_ratio * jnp.sqrt(w * w_below)
        w_below = w
        fluid = jnp.where(w > 0.0, 1.0, 0.0)
        dg[l] = fluid * (absorption + (west_of(east) + east + south_of(north) + north)) + (1.0 - fluid)
        fr[l] = window(1, l)
    w15 = w_below
    heat0 = fr[0] + horizontal(ef[0], nf[0], window(2, 0))
    d0 = dg[0] + vf[1]
    dg[0] = d0
    for l in range(1, LEV):
        d = dg[l] + vf[l]
        if l < LEV - 1:
            d = d + vf[l + 1]
        dg[l] = d
        b = fr[l] + horizontal(ef[l], nf[l], window(2, l))
        v = vf[l]
        if l == 1:
            dd, bb, g = d, b, v
        elif l < LEV - 1:
            dd = d - mult * v
            bb = b + mult * bb
            g = mult * g
        if l < LEV - 1:
            rcp = 1.0 / dd
            mult = vf[l + 1] * rcp
            rc[l] = rcp
            mm[l] = mult
            al[l] = bb * rcp
            be[l] = g * rcp
    heat15 = b
    alpha = jnp.where(red, al[LEV - 2], 0.0)
    beta = be[LEV - 2]
    gamma = mm[LEV - 2]
    al[LEV - 2] = alpha
    ga[LEV - 2] = gamma
    for l in range(LEV - 3, 0, -1):
        mult = mm[l]
        alpha = jnp.where(red, al[l] + mult * alpha, 0.0)
        beta = be[l] + mult * beta
        gamma = mult * gamma
        al[l] = alpha
        be[l] = beta
        ga[l] = gamma
    v1 = vf[1]
    v15 = vf[LEV - 1]
    self_low = v1 * be[1]
    self_high = v15 * ga[LEV - 2]
    e_tt, e_bb = ef[0], ef[LEV - 1]
    n_tt, n_bb = nf[0], nf[LEV - 1]
    e_tb = e_bt = n_tb = n_bt = jnp.zeros((WIN, LAN), F32)
    con_low = fr[0]
    con_high = fr[LEV - 1]
    for l in range(1, LEV - 1):
        beta, gamma, alpha = be[l], ga[l], al[l]
        east, north = ef[l], nf[l]
        there_b, there_g = east_of(beta), east_of(gamma)
        mine_b, mine_g = east * beta, east * gamma
        e_tt = e_tt + mine_b * there_b
        e_tb = e_tb + mine_b * there_g
        e_bt = e_bt + mine_g * there_b
        e_bb = e_bb + mine_g * there_g
        there_b, there_g = north_of(beta), north_of(gamma)
        mine_b, mine_g = north * beta, north * gamma
        n_tt = n_tt + mine_b * there_b
        n_tb = n_tb + mine_b * there_g
        n_bt = n_bt + mine_g * there_b
        n_bb = n_bb + mine_g * there_g
        b = fr[l] + horizontal(east, north, alpha)
        con_low = con_low + beta * b
        con_high = con_high + gamma * b
    own_low = v1 * al[1]
    own_high = v15 * al[LEV - 2]
    common = [d0 - self_low, v15 * be[LEV - 2], dg[LEV - 1] - self_high, w0, w15]
    common += [jnp.where(red, heat0 + own_low, con_low), jnp.where(red, heat15 + own_high, con_high)]
    common += [e_tt, e_tb, e_bt, e_bb, n_tt, n_tb, n_bt, n_bb]
    for k, value in enumerate(common):
        for peer in range(4):
            send[peer, k] = value
    upward = [v15, self_high, fr[LEV - 1] + own_high]
    downward = [v1, self_low, fr[0] + own_low]
    chip = lax.axis_index("zc")
    for peer in range(4):
        for k in range(3):
            send[peer, COMMON + k] = jnp.where(chip < peer, upward[k], downward[k])


def chain_factor(diag, link):
    rcp = [None] * 8
    for j in range(4):
        pivot = diag[j] if j == 0 else diag[j] - link[j] * link[j] * rcp[j - 1]
        rcp[j] = 1.0 / pivot
    for j in range(7, 4, -1):
        pivot = diag[j] if j == 7 else diag[j] - link[j + 1] * link[j + 1] * rcp[j + 1]
        rcp[j] = 1.0 / pivot
    rcp[4] = 1.0 / (diag[4] - link[4] * link[4] * rcp[3] - link[5] * link[5] * rcp[5])
    return rcp


def chain_solve(rcp, link, right):
    acc = list(right)
    for j in range(1, 4):
        acc[j] = acc[j] + link[j] * (rcp[j - 1] * acc[j - 1])
    for j in range(6, 4, -1):
        acc[j] = acc[j] + link[j + 1] * (rcp[j + 1] * acc[j + 1])
    out = [None] * 8
    out[4] = (acc[4] + link[4] * (rcp[3] * acc[3]) + link[5] * (rcp[5] * acc[5])) * rcp[4]
    for j in range(3, -1, -1):
        out[j] = (acc[j] + link[j + 1] * out[j + 1]) * rcp[j]
    for j in range(5, 8):
        out[j] = (acc[j] + link[j] * out[j - 1]) * rcp[j]
    return out


def second_kernel(got, ef, nf, vf, dg, fr, rc, mm, al, be, ga, out, ends, heat, full, res):
    chip = lax.axis_index("zc")
    row, lane, red = iotas()
    last_lane = lane == LAN - 1
    diag, link, right = [], [None], []
    for group in range(4):
        up, down = got[group, 0], got[group, 2]
        if group > 0:
            up = up + face
        if group < 3:
            face = vertical_ratio * jnp.sqrt(got[group, 4] * got[group + 1, 3])
            down = down + face
        diag += [up, down]
        link += [got[group, 1]] + ([face] if group < 3 else [])
        right += [got[group, 5], got[group, 6]]
    rcp = chain_factor(diag, link)
    reds = [jnp.where(red, v, 0.0) for v in chain_solve(rcp, link, right)]
    for group in range(4):
        t, b = reds[2 * group], reds[2 * group + 1]
        e_tt, e_tb, e_bt, e_bb, n_tt, n_tb, n_bt, n_bb = (got[group, 7 + k] for k in range(8))
        te, be_, tn, bn = east_of(t), east_of(b), north_of(t), north_of(b)
        right[2 * group] = right[2 * group] + (
            (e_tt * te + e_tb * be_)
            + (n_tt * tn + n_tb * bn)
            + west_of(e_tt * t + e_bt * b)
            + south_of(n_tt * t + n_bt * b)
        )
        right[2 * group + 1] = right[2 * group + 1] + (
            (e_bt * te + e_bb * be_)
            + (n_bt * tn + n_bb * bn)
            + west_of(e_tb * t + e_bb * b)
            + south_of(n_tb * t + n_bb * b)
        )
    blacks = chain_solve(rcp, link, right)
    for j in range(8):
        ends[j] = jnp.where(red, reds[j], blacks[j])
        heat[j] = right[j]
    low = ends[2 * chip]
    high = ends[2 * chip + 1]
    full[2] = low
    full[LEV + 1] = high
    bb = jnp.where(red, 0.0, vf[1] * low)
    for l in range(1, LEV - 1):
        p = jnp.where(red, al[l] + be[l] * low + ga[l] * high, 0.0)
        full[l + 2] = p
        b = fr[l] + horizontal(ef[l], nf[l], p)
        bb = b + (bb if l == 1 else mm[l - 1] * bb)
        res[l] = bb * rc[l]
    cur = high
    for l in range(LEV - 2, 0, -1):
        cur = res[l] + mm[l] * cur
        full[l + 2] = jnp.where(red, full[l + 2], cur)
    for l in range(LEV):
        out[l] = full[l + 2, 0:16, :]

    for side in (0, 1):
        near_chip = jnp.maximum(chip - 1, 0) if side == 0 else jnp.minimum(chip + 1, 3)
        there = chip > 0 if side == 0 else chip < 3
        end = 1 - side
        w_near = jnp.where(there, got[near_chip, 4 - side], 0.0)
        w_own = got[chip, 3 + side]
        p_near = ends[2 * near_chip + end]
        p_other = ends[2 * near_chip + side]
        p_own = low if side == 0 else high
        face_own = vertical_ratio * jnp.sqrt(w_near * w_own)
        face_far = got[near_chip, COMMON]
        east, north = side_faces(w_near, last_lane)
        fluid = jnp.where(w_near > 0.0, 1.0, 0.0)
        d = fluid * (
            absorption + (west_of(east) + east + south_of(north) + north) + face_own + face_far
        ) + (1.0 - fluid)
        known = jnp.where(red, got[near_chip, COMMON + 2] + horizontal(east, north, p_near), heat[2 * near_chip + end])
        inside = got[near_chip, 1] * p_other + got[near_chip, COMMON + 1] * p_near
        beyond = known + inside + face_own * p_own - d * p_near
        beyond = jnp.where(there, beyond, 0.0)
        if side == 0:
            res[0] = beyond
            face_low = face_own
            p_below = p_near
        else:
            res[LEV + 1] = beyond
            face_high = face_own
            p_above = p_near
    for l in range(LEV):
        p = full[l + 2]
        d = dg[l]
        if l == 0:
            d = d + face_low
            vert = face_low * p_below + vf[1] * full[3]
        elif l == LEV - 1:
            d = d + face_high
            vert = vf[l] * full[l + 1] + face_high * p_above
        else:
            vert = vf[l] * full[l + 1] + vf[l + 1] * full[l + 3]
        applied = d * p - (horizontal(ef[l], nf[l], p) + vert)
        res[l + 1] = fr[l] - applied
    weights = restriction_matrix()
    for big in range(LEV // 2):
        z = 2 * big
        s = 0.125 * (res[z] + 3.0 * res[z + 1] + 3.0 * res[z + 2] + res[z + 3])
        e = east_of(s)
        s = 0.125 * (west_of(s) + 3.0 * s + 3.0 * e + east_of(e))
        res[z] = jnp.dot(s, weights, precision=lax.Precision.HIGHEST, preferred_element_type=F32)
        out[LEV + big] = jnp.concatenate(
            [res[z, pl.ds(0, 8, stride=2), :], jnp.zeros((8, LAN), F32)], axis=0
        )


def last_kernel(both, relaxed, coarse):
    core = lax.axis_index("zk")
    for j in range(2):
        for l in range(8):
            relaxed[l, 16 * j : 16 * j + 16, :] = both[j, core * 8 + l]
        for big in range(4):
            coarse[big, 8 * j : 8 * j + 8, :] = both[j, LEV + core * 4 + big, 0:8, 0:64]


def restriction_matrix():
    fine = lax.broadcasted_iota(jnp.int32, (LAN, LAN), 0)
    big = lax.broadcasted_iota(jnp.int32, (LAN, LAN), 1)
    off = fine - 2 * big + 1
    inner = (off == 1) | (off == 2)
    outer = (off == 0) | (off == 3)
    return jnp.where(inner, 0.375, jnp.where(outer, 0.125, 0.0)).astype(F32)


def call(kernel, name, shapes, scratch=(), ends=""):
    vm = pl.BlockSpec(memory_space=pltpu.VMEM)
    main = pl.BlockSpec(memory_space=pltpu.HBM)

    def run(*args):
        if not INTERPRET:
            space = pltpu.HBM if ends == "first" else pltpu.VMEM
            args = [pltpu.with_memory_space_constraint(a, space) for a in args]
        plain = ends == "last" or INTERPRET
        return pl.pallas_call(
            kernel,
            out_shape=[jax.ShapeDtypeStruct(s, F32) if plain else pltpu.VMEM(s, F32) for s in shapes],
            in_specs=[main if ends == "first" else vm] * len(args),
            out_specs=[vm] * len(shapes),
            scratch_shapes=scratch,
            name=name,
            compiler_params=pltpu.CompilerParams(vmem_limit_bytes=SCOPED),
            interpret=INTERPRET,
        )(*args)

    return run


def side_by_side():
    chips, cores, count = (lax.axis_size(axis) for axis in AXES)

    def number(chip, core, q):
        return (chip * cores + core) * count + q

    groups = [[number(c, 0, q), number(c, 1, q - 1)] for c in range(chips) for q in range(1, count)]
    for c in range(0, chips, 2):
        groups.append([number(c, 0, 0), number(c + 1, 0, 0)])
        groups.append([number(c, 1, count - 1), number(c + 1, 1, count - 1)])
    return groups


def shards(source, conductivity, fluid, pressure):
    cell = (WIN, LAN)
    field = (LEV, WIN, LAN)
    block = (HALF, 32, LAN)
    vmem = pltpu.VMEM
    (mine,) = call(
        weigh_kernel,
        "weigh",
        [(3,) + block],
        [vmem(block, F32), vmem(block, F32), vmem(block, jnp.int32), pltpu.SemaphoreType.DMA((4,))],
        ends="first",
    )(source, conductivity, fluid, pressure)
    both = lax.all_gather(mine, "zk", axis=0, tiled=False)
    (edge,) = call(edge_kernel, "edge", [(3, HALF, 8, LAN)])(both)
    halo = lax.all_gather(edge, AXES, axis=0, tiled=False, axis_index_groups=side_by_side())
    send, *fields = call(first_kernel, "first", [(4, SENT) + cell] + [field] * 10)(both, halo)
    got = lax.all_to_all(send, "zc", 0, 0, tiled=False)
    (done,) = call(
        second_kernel,
        "second",
        [(LEV + LEV // 2, 16, LAN)],
        [vmem((8,) + cell, F32)] * 2 + [vmem((LEV + 4,) + cell, F32), vmem((LEV + 2,) + cell, F32)],
    )(got, *fields)
    ends = lax.all_gather(done, "zk", axis=0, tiled=False)
    relaxed, coarse = call(last_kernel, "last", [block, (4, 16, LAN // 2)], ends="last")(ends)
    return relaxed, coarse


def solution(mesh):
    finer = Mesh(mesh.devices.reshape(4, 2, mesh.shape["xy"]), AXES)
    spec = P(("zc", "zk"), "xy", None)
    return jax.shard_map(shards, mesh=finer, in_specs=(spec,) * 4, out_specs=(spec,) * 2, check_vma=False)
```

```python
import jax
import jax.numpy as jnp
from jax import lax
from jax.experimental import pallas as pl
from jax.experimental.pallas import tpu as pltpu
from jax.sharding import Mesh
from jax.sharding import PartitionSpec as P

INTERPRET = False
AXES = ("zc", "zk", "xy")
SCOPED = 4 << 20
vertical_ratio = 100.0
absorption = 0.05

LEV = 16
HALF = 8
ARRAYS = 16
OUTER = (0, 1, 2, 3, 4, 5, 6, 7, 8, 9, 10, 11, 11, 12, 12, 7)
ROLLED = (12, 14, 15)
SENT = ARRAYS * 16 + 13 * 8
WIN = 24
LAN = 128
F32 = jnp.float32


def east_of(v):
    return pltpu.roll(v, WIN - 1, 0)


def west_of(v):
    return pltpu.roll(v, 1, 0)


def north_of(v):
    return pltpu.roll(v, LAN - 1, 1)


def south_of(v):
    return pltpu.roll(v, 1, 1)


def iotas():
    row = lax.broadcasted_iota(jnp.int32, (WIN, LAN), 0)
    lane = lax.broadcasted_iota(jnp.int32, (WIN, LAN), 1)
    red = ((row + lane) & 1) == 0
    return row, lane, red


def side_faces(w, last_lane):
    east = jnp.sqrt(w * east_of(w))
    north = jnp.where(last_lane, 0.0, jnp.sqrt(w * north_of(w)))
    return east, north


def horizontal(east, north, p):
    return (
        west_of(east * p)
        + east * east_of(p)
        + south_of(north * p)
        + north * north_of(p)
    )


def weigh_kernel(source, cond, fluid, pressure, out, source_v, cond_v, fluid_v, sems):
    copies = [
        pltpu.make_async_copy(cond, cond_v, sems.at[0]),
        pltpu.make_async_copy(fluid, fluid_v, sems.at[1]),
        pltpu.make_async_copy(source, source_v, sems.at[2]),
        pltpu.make_async_copy(pressure, out.at[2], sems.at[3]),
    ]
    for copy in copies:
        copy.start()
    for copy in copies:
        copy.wait()
    for l in range(HALF):
        real = fluid_v[l].astype(F32)
        out[0, l] = cond_v[l] * real
        out[1, l] = real * source_v[l]


def edge_kernel(both, out):
    core = lax.axis_index("zk")
    start = pl.multiple_of(core * 24, 8)
    keep = (lax.broadcasted_iota(jnp.int32, (8, LAN), 0) < 4) == (core == 0)
    for f in range(3):
        for l in range(HALF):
            low = both[0, f, l, pl.ds(start, 8), :]
            high = both[1, f, l, pl.ds(start, 8), :]
            out[f, l] = jnp.where(keep, low, pltpu.roll(high, 4, 0))


def outer_rows(k):
    at = ARRAYS * 16 + 8 * OUTER[k]
    return slice(at, at + 8)


def received(got, group, k):
    outer = got[group, outer_rows(k), :]
    if k in ROLLED:
        outer = pltpu.roll(outer, 4, 0)
    return jnp.concatenate([got[group, 16 * k : 16 * k + 16, :], outer], axis=0)


def first_kernel(both, halo, send, ef, nf, vf, dg, fr, rc, mm, al, be, ga):
    core = lax.axis_index("zk")
    row, lane, red = iotas()
    last_lane = lane == LAN - 1
    row8 = lax.broadcasted_iota(jnp.int32, (8, LAN), 0)
    from_near = (row8 < 4) == (core == 0)
    own_at = pl.multiple_of(core * 16, 8)
    near_at = pl.multiple_of(16 - 8 * core, 8)
    block = lax.axis_index("xy")
    inside = jnp.where(core == 0, block > 0, block < lax.axis_size("xy") - 1)

    def window(f, l):
        own = both[l // 8, f, l % 8, pl.ds(own_at, 16), :]
        near = both[l // 8, f, l % 8, pl.ds(near_at, 8), :]
        far = jnp.where(inside, halo[1 - core, f, l % 8], 0.0)
        if l >= HALF:
            far = pltpu.roll(far, 4, 0)
        return jnp.concatenate([own, jnp.where(from_near, near, far)], axis=0)

    for l in range(LEV):
        w = window(0, l)
        east, north = side_faces(w, last_lane)
        ef[l] = east
        nf[l] = north
        if l == 0:
            w0 = w
            vf[0] = jnp.zeros_like(w)
        else:
            vf[l] = vertical_ratio * jnp.sqrt(w * w_below)
        w_below = w
        fluid = jnp.where(w > 0.0, 1.0, 0.0)
        dg[l] = fluid * (absorption + (west_of(east) + east + south_of(north) + north)) + (1.0 - fluid)
        fr[l] = window(1, l)
    w15 = w_below
    heat0 = fr[0] + horizontal(ef[0], nf[0], window(2, 0))
    d0 = dg[0] + vf[1]
    dg[0] = d0
    for l in range(1, LEV):
        d = dg[l] + vf[l]
        if l < LEV - 1:
            d = d + vf[l + 1]
        dg[l] = d
        b = fr[l] + horizontal(ef[l], nf[l], window(2, l))
        v = vf[l]
        if l == 1:
            dd, bb, g = d, b, v
        elif l < LEV - 1:
            dd = d - mult * v
            bb = b + mult * bb
            g = mult * g
        if l < LEV - 1:
            rcp = 1.0 / dd
            mult = vf[l + 1] * rcp
            rc[l] = rcp
            mm[l] = mult
            al[l] = bb * rcp
            be[l] = g * rcp
    heat15 = b
    alpha = jnp.where(red, al[LEV - 2], 0.0)
    beta = be[LEV - 2]
    gamma = mm[LEV - 2]
    al[LEV - 2] = alpha
    ga[LEV - 2] = gamma
    for l in range(LEV - 3, 0, -1):
        mult = mm[l]
        alpha = jnp.where(red, al[l] + mult * alpha, 0.0)
        beta = be[l] + mult * beta
        gamma = mult * gamma
        al[l] = alpha
        be[l] = beta
        ga[l] = gamma
    v1 = vf[1]
    v15 = vf[LEV - 1]
    self_low = v1 * be[1]
    self_high = v15 * ga[LEV - 2]
    e_tt, e_bb = ef[0], ef[LEV - 1]
    n_tt, n_bb = nf[0], nf[LEV - 1]
    e_tb = e_bt = n_tb = n_bt = jnp.zeros((WIN, LAN), F32)
    con_low = fr[0]
    con_high = fr[LEV - 1]
    for l in range(1, LEV - 1):
        beta, gamma, alpha = be[l], ga[l], al[l]
        east, north = ef[l], nf[l]
        there_b, there_g = east_of(beta), east_of(gamma)
        mine_b, mine_g = east * beta, east * gamma
        e_tt = e_tt + mine_b * there_b
        e_tb = e_tb + mine_b * there_g
        e_bt = e_bt + mine_g * there_b
        e_bb = e_bb + mine_g * there_g
        there_b, there_g = north_of(beta), north_of(gamma)
        mine_b, mine_g = north * beta, north * gamma
        n_tt = n_tt + mine_b * there_b
        n_tb = n_tb + mine_b * there_g
        n_bt = n_bt + mine_g * there_b
        n_bb = n_bb + mine_g * there_g
        b = fr[l] + horizontal(east, north, alpha)
        con_low = con_low + beta * b
        con_high = con_high + gamma * b
    own_low = v1 * al[1]
    own_high = v15 * al[LEV - 2]
    common = [d0 - self_low, v15 * be[LEV - 2], dg[LEV - 1] - self_high, w0, w15]
    common += [jnp.where(red, heat0 + own_low, con_low), jnp.where(red, heat15 + own_high, con_high)]
    common += [e_tt, e_tb, e_bt, e_bb, n_tt, n_tb, n_bt, n_bb]
    chip = lax.axis_index("zc")
    row8 = lax.broadcasted_iota(jnp.int32, (8, LAN), 0)
    upward = fr[LEV - 1] + own_high
    downward = fr[0] + own_low
    outer = [value[16:24] for value in common]
    inner = (row8 < 2) | (row8 > 5)
    for k in (11, 13):
        outer[k] = jnp.where(inner, outer[k], pltpu.roll(outer[k + 1], 4, 0))
    kept = (row8 < 2) | (row8 > 4)
    for peer in range(4):
        last = jnp.where(chip < peer, upward, downward)
        for k in range(ARRAYS):
            value = common[k] if k < ARRAYS - 1 else last
            send[peer, 16 * k : 16 * k + 16, :] = value[0:16]
            if k in ROLLED:
                continue
            tile = outer[k]
            if k == 7:
                tile = jnp.where(kept, tile, pltpu.roll(last[16:24], 4, 0))
            send[peer, outer_rows(k), :] = tile


def chain_factor(diag, link):
    rcp = [None] * 8
    for j in range(4):
        pivot = diag[j] if j == 0 else diag[j] - link[j] * link[j] * rcp[j - 1]
        rcp[j] = 1.0 / pivot
    for j in range(7, 4, -1):
        pivot = diag[j] if j == 7 else diag[j] - link[j + 1] * link[j + 1] * rcp[j + 1]
        rcp[j] = 1.0 / pivot
    rcp[4] = 1.0 / (diag[4] - link[4] * link[4] * rcp[3] - link[5] * link[5] * rcp[5])
    return rcp


def chain_solve(rcp, link, right):
    acc = list(right)
    for j in range(1, 4):
        acc[j] = acc[j] + link[j] * (rcp[j - 1] * acc[j - 1])
    for j in range(6, 4, -1):
        acc[j] = acc[j] + link[j + 1] * (rcp[j + 1] * acc[j + 1])
    out = [None] * 8
    out[4] = (acc[4] + link[4] * (rcp[3] * acc[3]) + link[5] * (rcp[5] * acc[5])) * rcp[4]
    for j in range(3, -1, -1):
        out[j] = (acc[j] + link[j + 1] * out[j + 1]) * rcp[j]
    for j in range(5, 8):
        out[j] = (acc[j] + link[j] * out[j - 1]) * rcp[j]
    return out


def second_kernel(got, ef, nf, vf, dg, fr, rc, mm, al, be, ga, out, ends, heat, full, res):
    chip = lax.axis_index("zc")
    row, lane, red = iotas()
    last_lane = lane == LAN - 1
    diag, link, right = [], [None], []
    for group in range(4):
        up, down = received(got, group, 0), received(got, group, 2)
        if group > 0:
            up = up + face
        if group < 3:
            face = vertical_ratio * jnp.sqrt(received(got, group, 4) * received(got, group + 1, 3))
            down = down + face
        diag += [up, down]
        link += [received(got, group, 1)] + ([face] if group < 3 else [])
        right += [received(got, group, 5), received(got, group, 6)]
    rcp = chain_factor(diag, link)
    reds = [jnp.where(red, v, 0.0) for v in chain_solve(rcp, link, right)]
    for group in range(4):
        t, b = reds[2 * group], reds[2 * group + 1]
        e_tt, e_tb, e_bt, e_bb, n_tt, n_tb, n_bt, n_bb = (received(got, group, 7 + k) for k in range(8))
        te, be_, tn, bn = east_of(t), east_of(b), north_of(t), north_of(b)
        right[2 * group] = right[2 * group] + (
            (e_tt * te + e_tb * be_)
            + (n_tt * tn + n_tb * bn)
            + west_of(e_tt * t + e_bt * b)
            + south_of(n_tt * t + n_bt * b)
        )
        right[2 * group + 1] = right[2 * group + 1] + (
            (e_bt * te + e_bb * be_)
            + (n_bt * tn + n_bb * bn)
            + west_of(e_tb * t + e_bb * b)
            + south_of(n_tb * t + n_bb * b)
        )
    blacks = chain_solve(rcp, link, right)
    for j in range(8):
        ends[j] = jnp.where(red, reds[j], blacks[j])
        heat[j] = right[j]
    low = ends[2 * chip]
    high = ends[2 * chip + 1]
    full[2] = low
    full[LEV + 1] = high
    bb = jnp.where(red, 0.0, vf[1] * low)
    for l in range(1, LEV - 1):
        p = jnp.where(red, al[l] + be[l] * low + ga[l] * high, 0.0)
        full[l + 2] = p
        b = fr[l] + horizontal(ef[l], nf[l], p)
        bb = b + (bb if l == 1 else mm[l - 1] * bb)
        res[l] = bb * rc[l]
    cur = high
    for l in range(LEV - 2, 0, -1):
        cur = res[l] + mm[l] * cur
        full[l + 2] = jnp.where(red, full[l + 2], cur)
    for l in range(LEV):
        out[l] = full[l + 2, 0:16, :]

    for side in (0, 1):
        near_chip = jnp.maximum(chip - 1, 0) if side == 0 else jnp.minimum(chip + 1, 3)
        there = chip > 0 if side == 0 else chip < 3
        end = 1 - side
        w_near = jnp.where(there, received(got, near_chip, 4 - side), 0.0)
        w_own = received(got, chip, 3 + side)
        p_near = ends[2 * near_chip + end]
        p_other = ends[2 * near_chip + side]
        p_own = low if side == 0 else high
        face_own = vertical_ratio * jnp.sqrt(w_near * w_own)
        east, north = side_faces(w_near, last_lane)
        known = jnp.where(
            red, received(got, near_chip, 15) + horizontal(east, north, p_near), heat[2 * near_chip + end]
        )
        d = received(got, near_chip, 2 - 2 * side) + face_own
        beyond = known + received(got, near_chip, 1) * p_other + face_own * p_own - d * p_near
        beyond = jnp.where(there, beyond, 0.0)
        if side == 0:
            res[0] = beyond
            face_low = face_own
            p_below = p_near
        else:
            res[LEV + 1] = beyond
            face_high = face_own
            p_above = p_near
    for l in range(LEV):
        p = full[l + 2]
        d = dg[l]
        if l == 0:
            d = d + face_low
            vert = face_low * p_below + vf[1] * full[3]
        elif l == LEV - 1:
            d = d + face_high
            vert = vf[l] * full[l + 1] + face_high * p_above
        else:
            vert = vf[l] * full[l + 1] + vf[l + 1] * full[l + 3]
        applied = d * p - (horizontal(ef[l], nf[l], p) + vert)
        res[l + 1] = fr[l] - applied
    weights = restriction_matrix()
    for big in range(LEV // 2):
        z = 2 * big
        s = 0.125 * (res[z] + 3.0 * res[z + 1] + 3.0 * res[z + 2] + res[z + 3])
        e = east_of(s)
        s = 0.125 * (west_of(s) + 3.0 * s + 3.0 * e + east_of(e))
        res[z] = jnp.dot(s, weights, precision=lax.Precision.HIGHEST, preferred_element_type=F32)
        out[LEV + big] = jnp.concatenate(
            [res[z, pl.ds(0, 8, stride=2), :], jnp.zeros((8, LAN), F32)], axis=0
        )


def last_kernel(both, relaxed, coarse):
    core = lax.axis_index("zk")
    for j in range(2):
        for l in range(8):
            relaxed[l, 16 * j : 16 * j + 16, :] = both[j, core * 8 + l]
        for big in range(4):
            coarse[big, 8 * j : 8 * j + 8, :] = both[j, LEV + core * 4 + big, 0:8, 0:64]


def restriction_matrix():
    fine = lax.broadcasted_iota(jnp.int32, (LAN, LAN), 0)
    big = lax.broadcasted_iota(jnp.int32, (LAN, LAN), 1)
    off = fine - 2 * big + 1
    inner = (off == 1) | (off == 2)
    outer = (off == 0) | (off == 3)
    return jnp.where(inner, 0.375, jnp.where(outer, 0.125, 0.0)).astype(F32)


def call(kernel, name, shapes, scratch=(), ends=""):
    vm = pl.BlockSpec(memory_space=pltpu.VMEM)
    main = pl.BlockSpec(memory_space=pltpu.HBM)

    def run(*args):
        if not INTERPRET:
            space = pltpu.HBM if ends == "first" else pltpu.VMEM
            args = [pltpu.with_memory_space_constraint(a, space) for a in args]
        plain = ends == "last" or INTERPRET
        return pl.pallas_call(
            kernel,
            out_shape=[jax.ShapeDtypeStruct(s, F32) if plain else pltpu.VMEM(s, F32) for s in shapes],
            in_specs=[main if ends == "first" else vm] * len(args),
            out_specs=[vm] * len(shapes),
            scratch_shapes=scratch,
            name=name,
            compiler_params=pltpu.CompilerParams(vmem_limit_bytes=SCOPED),
            interpret=INTERPRET,
        )(*args)

    return run


def side_by_side():
    chips, cores, count = (lax.axis_size(axis) for axis in AXES)

    def number(chip, core, q):
        return (chip * cores + core) * count + q

    groups = [[number(c, 0, q), number(c, 1, q - 1)] for c in range(chips) for q in range(1, count)]
    for c in range(0, chips, 2):
        groups.append([number(c, 0, 0), number(c + 1, 0, 0)])
        groups.append([number(c, 1, count - 1), number(c + 1, 1, count - 1)])
    return groups


def shards(source, conductivity, fluid, pressure):
    cell = (WIN, LAN)
    field = (LEV, WIN, LAN)
    block = (HALF, 32, LAN)
    vmem = pltpu.VMEM
    (mine,) = call(
        weigh_kernel,
        "weigh",
        [(3,) + block],
        [vmem(block, F32), vmem(block, F32), vmem(block, jnp.int32), pltpu.SemaphoreType.DMA((4,))],
        ends="first",
    )(source, conductivity, fluid, pressure)
    both = lax.all_gather(mine, "zk", axis=0, tiled=False)
    (edge,) = call(edge_kernel, "edge", [(3, HALF, 8, LAN)])(both)
    halo = lax.all_gather(edge, AXES, axis=0, tiled=False, axis_index_groups=side_by_side())
    send, *fields = call(first_kernel, "first", [(4, SENT, LAN)] + [field] * 10)(both, halo)
    got = lax.all_to_all(send, "zc", 0, 0, tiled=False)
    (done,) = call(
        second_kernel,
        "second",
        [(LEV + LEV // 2, 16, LAN)],
        [vmem((8,) + cell, F32)] * 2 + [vmem((LEV + 4,) + cell, F32), vmem((LEV + 2,) + cell, F32)],
    )(got, *fields)
    ends = lax.all_gather(done, "zk", axis=0, tiled=False)
    relaxed, coarse = call(last_kernel, "last", [block, (4, 16, LAN // 2)], ends="last")(ends)
    return relaxed, coarse


def solution(mesh):
    finer = Mesh(mesh.devices.reshape(4, 2, mesh.shape["xy"]), AXES)
    spec = P(("zc", "zk"), "xy", None)
    return jax.shard_map(shards, mesh=finer, in_specs=(spec,) * 4, out_specs=(spec,) * 2, check_vma=False)
```

```python
import jax
import jax.numpy as jnp
from jax import lax
from jax.experimental import pallas as pl
from jax.experimental.pallas import tpu as pltpu
from jax.sharding import Mesh
from jax.sharding import PartitionSpec as P

INTERPRET = False
AXES = ("zc", "zk", "xy")
SCOPED = 4 << 20
vertical_ratio = 100.0
absorption = 0.05

LEV = 16
HALF = 8
PLANES = 20
PIECES = 4
ARRAYS = 16
OWN = ARRAYS * 16 - 8
OUTER = (0, 1, 2, 3, 4, 5, 6, 7, 8, 9, 10, 11, 11, 12, 12, 7)
ROLLED = (12, 14, 15)
SENT = OWN + 13 * 8
WIN = 24
LAN = 128
F32 = jnp.float32


def east_of(v):
    return pltpu.roll(v, WIN - 1, 0)


def west_of(v):
    return pltpu.roll(v, 1, 0)


def north_of(v):
    return pltpu.roll(v, LAN - 1, 1)


def south_of(v):
    return pltpu.roll(v, 1, 1)


def iotas():
    row = lax.broadcasted_iota(jnp.int32, (WIN, LAN), 0)
    lane = lax.broadcasted_iota(jnp.int32, (WIN, LAN), 1)
    red = ((row + lane) & 1) == 0
    return row, lane, red


def black_mask(rows):
    row = lax.broadcasted_iota(jnp.int32, (rows, LAN), 0)
    lane = lax.broadcasted_iota(jnp.int32, (rows, LAN), 1)
    return ((row + lane) & 1) == 1


def side_faces(w, last_lane):
    east = jnp.sqrt(w * east_of(w))
    north = jnp.where(last_lane, 0.0, jnp.sqrt(w * north_of(w)))
    return east, north


def horizontal(east, north, p):
    return (
        west_of(east * p)
        + east * east_of(p)
        + south_of(north * p)
        + north * north_of(p)
    )


def weigh_kernel(source, cond, fluid, pressure, out, source_v, cond_v, fluid_v, pressure_v, sems):
    parts = [pl.ds(k * HALF // PIECES, HALF // PIECES) for k in range(PIECES)]
    copies = []
    for k, part in enumerate(parts):
        for n, (there, here) in enumerate(
            ((cond, cond_v), (fluid, fluid_v), (source, source_v), (pressure, pressure_v))
        ):
            copies.append(pltpu.make_async_copy(there.at[part], here.at[part], sems.at[k, n]))
    for copy in copies:
        copy.start()
    for copy in copies:
        copy.wait()
    black = black_mask(32)
    for l in range(HALF):
        real = fluid_v[l].astype(F32)
        out[l] = cond_v[l] * real
        out[HALF + l] = real * source_v[l]
    for l in range(0, HALF, 2):
        out[2 * HALF + l // 2] = jnp.where(black, pressure_v[l], pltpu.roll(pressure_v[l + 1], 1, 1))


def edge_kernel(both, out):
    core = lax.axis_index("zk")
    start = pl.multiple_of(core * 24, 8)
    keep = (lax.broadcasted_iota(jnp.int32, (8, LAN), 0) < 4) == (core == 0)
    for k in range(PLANES):
        low = both[0, k, pl.ds(start, 8), :]
        high = both[1, k, pl.ds(start, 8), :]
        out[k] = jnp.where(keep, low, pltpu.roll(high, 4, 0))


def outer_rows(k):
    at = OWN + 8 * OUTER[k]
    return slice(at, at + 8)


def received(got, group, k):
    outer = got[group, outer_rows(k), :]
    if k in ROLLED:
        outer = pltpu.roll(outer, 4, 0)
    if k == ARRAYS - 1:
        folded = got[group, OWN - 8 : OWN, :]
        return jnp.concatenate([folded, north_of(folded), outer], axis=0)
    return jnp.concatenate([got[group, 16 * k : 16 * k + 16, :], outer], axis=0)


def first_kernel(both, halo, send, ef, nf, vf, dg, fr, rc, mm, al, be, ga):
    core = lax.axis_index("zk")
    row, lane, red = iotas()
    last_lane = lane == LAN - 1
    row8 = lax.broadcasted_iota(jnp.int32, (8, LAN), 0)
    from_near = (row8 < 4) == (core == 0)
    own_at = pl.multiple_of(core * 16, 8)
    near_at = pl.multiple_of(16 - 8 * core, 8)
    block = lax.axis_index("xy")
    inside = jnp.where(core == 0, block > 0, block < lax.axis_size("xy") - 1)

    def window(f, l):
        k = f * HALF + l % HALF if f < 2 else 2 * HALF + l % HALF // 2
        own = both[l // HALF, k, pl.ds(own_at, 16), :]
        near = both[l // HALF, k, pl.ds(near_at, 8), :]
        far = jnp.where(inside, halo[1 - core, k], 0.0)
        if l >= HALF:
            far = pltpu.roll(far, 4, 0)
        value = jnp.concatenate([own, jnp.where(from_near, near, far)], axis=0)
        return north_of(value) if f == 2 and l % 2 == 1 else value

    for l in range(LEV):
        w = window(0, l)
        east, north = side_faces(w, last_lane)
        ef[l] = east
        nf[l] = north
        if l == 0:
            w0 = w
            vf[0] = jnp.zeros_like(w)
        else:
            vf[l] = vertical_ratio * jnp.sqrt(w * w_below)
        w_below = w
        fluid = jnp.where(w > 0.0, 1.0, 0.0)
        dg[l] = fluid * (absorption + (west_of(east) + east + south_of(north) + north)) + (1.0 - fluid)
        fr[l] = window(1, l)
    w15 = w_below
    heat0 = fr[0] + horizontal(ef[0], nf[0], window(2, 0))
    d0 = dg[0] + vf[1]
    dg[0] = d0
    for l in range(1, LEV):
        d = dg[l] + vf[l]
        if l < LEV - 1:
            d = d + vf[l + 1]
        dg[l] = d
        b = fr[l] + horizontal(ef[l], nf[l], window(2, l))
        v = vf[l]
        if l == 1:
            dd, bb, g = d, b, v
        elif l < LEV - 1:
            dd = d - mult * v
            bb = b + mult * bb
            g = mult * g
        if l < LEV - 1:
            rcp = 1.0 / dd
            mult = vf[l + 1] * rcp
            rc[l] = rcp
            mm[l] = mult
            al[l] = bb * rcp
            be[l] = g * rcp
    heat15 = b
    alpha = jnp.where(red, al[LEV - 2], 0.0)
    beta = be[LEV - 2]
    gamma = mm[LEV - 2]
    al[LEV - 2] = alpha
    ga[LEV - 2] = gamma
    for l in range(LEV - 3, 0, -1):
        mult = mm[l]
        alpha = jnp.where(red, al[l] + mult * alpha, 0.0)
        beta = be[l] + mult * beta
        gamma = mult * gamma
        al[l] = alpha
        be[l] = beta
        ga[l] = gamma
    v1 = vf[1]
    v15 = vf[LEV - 1]
    self_low = v1 * be[1]
    self_high = v15 * ga[LEV - 2]
    e_tt, e_bb = ef[0], ef[LEV - 1]
    n_tt, n_bb = nf[0], nf[LEV - 1]
    e_tb = e_bt = n_tb = n_bt = jnp.zeros((WIN, LAN), F32)
    con_low = fr[0]
    con_high = fr[LEV - 1]
    for l in range(1, LEV - 1):
        beta, gamma, alpha = be[l], ga[l], al[l]
        east, north = ef[l], nf[l]
        there_b, there_g = east_of(beta), east_of(gamma)
        mine_b, mine_g = east * beta, east * gamma
        e_tt = e_tt + mine_b * there_b
        e_tb = e_tb + mine_b * there_g
        e_bt = e_bt + mine_g * there_b
        e_bb = e_bb + mine_g * there_g
        there_b, there_g = north_of(beta), north_of(gamma)
        mine_b, mine_g = north * beta, north * gamma
        n_tt = n_tt + mine_b * there_b
        n_tb = n_tb + mine_b * there_g
        n_bt = n_bt + mine_g * there_b
        n_bb = n_bb + mine_g * there_g
        b = fr[l] + horizontal(east, north, alpha)
        con_low = con_low + beta * b
        con_high = con_high + gamma * b
    own_low = v1 * al[1]
    own_high = v15 * al[LEV - 2]
    common = [d0 - self_low, v15 * be[LEV - 2], dg[LEV - 1] - self_high, w0, w15]
    common += [jnp.where(red, heat0 + own_low, con_low), jnp.where(red, heat15 + own_high, con_high)]
    common += [e_tt, e_tb, e_bt, e_bb, n_tt, n_tb, n_bt, n_bb]
    chip = lax.axis_index("zc")
    row8 = lax.broadcasted_iota(jnp.int32, (8, LAN), 0)
    upward = fr[LEV - 1] + own_high
    downward = fr[0] + own_low
    outer = [value[16:24] for value in common]
    inner = (row8 < 2) | (row8 > 5)
    for k in (11, 13):
        outer[k] = jnp.where(inner, outer[k], pltpu.roll(outer[k + 1], 4, 0))
    kept = (row8 < 2) | (row8 > 4)
    for peer in range(4):
        last = jnp.where(chip < peer, upward, downward)
        for k in range(ARRAYS):
            if k < ARRAYS - 1:
                send[peer, 16 * k : 16 * k + 16, :] = common[k][0:16]
            else:
                send[peer, OWN - 8 : OWN, :] = jnp.where(red[0:8], last[0:8], south_of(last[8:16]))
            if k in ROLLED:
                continue
            tile = outer[k]
            if k == 7:
                tile = jnp.where(kept, tile, pltpu.roll(last[16:24], 4, 0))
            send[peer, outer_rows(k), :] = tile


def chain_factor(diag, link):
    rcp = [None] * 8
    for j in range(4):
        pivot = diag[j] if j == 0 else diag[j] - link[j] * link[j] * rcp[j - 1]
        rcp[j] = 1.0 / pivot
    for j in range(7, 4, -1):
        pivot = diag[j] if j == 7 else diag[j] - link[j + 1] * link[j + 1] * rcp[j + 1]
        rcp[j] = 1.0 / pivot
    rcp[4] = 1.0 / (diag[4] - link[4] * link[4] * rcp[3] - link[5] * link[5] * rcp[5])
    return rcp


def chain_solve(rcp, link, right):
    acc = list(right)
    for j in range(1, 4):
        acc[j] = acc[j] + link[j] * (rcp[j - 1] * acc[j - 1])
    for j in range(6, 4, -1):
        acc[j] = acc[j] + link[j + 1] * (rcp[j + 1] * acc[j + 1])
    out = [None] * 8
    out[4] = (acc[4] + link[4] * (rcp[3] * acc[3]) + link[5] * (rcp[5] * acc[5])) * rcp[4]
    for j in range(3, -1, -1):
        out[j] = (acc[j] + link[j + 1] * out[j + 1]) * rcp[j]
    for j in range(5, 8):
        out[j] = (acc[j] + link[j] * out[j - 1]) * rcp[j]
    return out


def second_kernel(got, ef, nf, vf, dg, fr, rc, mm, al, be, ga, keep, give, out, ends, heat, full, res):
    chip = lax.axis_index("zc")
    row, lane, red = iotas()
    last_lane = lane == LAN - 1
    diag, link, right = [], [None], []
    for group in range(4):
        up, down = received(got, group, 0), received(got, group, 2)
        if group > 0:
            up = up + face
        if group < 3:
            face = vertical_ratio * jnp.sqrt(received(got, group, 4) * received(got, group + 1, 3))
            down = down + face
        diag += [up, down]
        link += [received(got, group, 1)] + ([face] if group < 3 else [])
        right += [received(got, group, 5), received(got, group, 6)]
    rcp = chain_factor(diag, link)
    reds = [jnp.where(red, v, 0.0) for v in chain_solve(rcp, link, right)]
    for group in range(4):
        t, b = reds[2 * group], reds[2 * group + 1]
        e_tt, e_tb, e_bt, e_bb, n_tt, n_tb, n_bt, n_bb = (received(got, group, 7 + k) for k in range(8))
        te, be_, tn, bn = east_of(t), east_of(b), north_of(t), north_of(b)
        right[2 * group] = right[2 * group] + (
            (e_tt * te + e_tb * be_)
            + (n_tt * tn + n_tb * bn)
            + west_of(e_tt * t + e_bt * b)
            + south_of(n_tt * t + n_bt * b)
        )
        right[2 * group + 1] = right[2 * group + 1] + (
            (e_bt * te + e_bb * be_)
            + (n_bt * tn + n_bb * bn)
            + west_of(e_tb * t + e_bb * b)
            + south_of(n_tb * t + n_bb * b)
        )
    blacks = chain_solve(rcp, link, right)
    for j in range(8):
        ends[j] = jnp.where(red, reds[j], blacks[j])
        heat[j] = right[j]
    low = ends[2 * chip]
    high = ends[2 * chip + 1]
    full[2] = low
    full[LEV + 1] = high
    bb = jnp.where(red, 0.0, vf[1] * low)
    for l in range(1, LEV - 1):
        p = jnp.where(red, al[l] + be[l] * low + ga[l] * high, 0.0)
        full[l + 2] = p
        b = fr[l] + horizontal(ef[l], nf[l], p)
        bb = b + (bb if l == 1 else mm[l - 1] * bb)
        res[l] = bb * rc[l]
    cur = high
    for l in range(LEV - 2, 0, -1):
        cur = res[l] + mm[l] * cur
        full[l + 2] = jnp.where(red, full[l + 2], cur)
    for l in range(LEV):
        out[l // HALF, l % HALF] = full[l + 2, 0:16, :]

    for side in (0, 1):
        near_chip = jnp.maximum(chip - 1, 0) if side == 0 else jnp.minimum(chip + 1, 3)
        there = chip > 0 if side == 0 else chip < 3
        end = 1 - side
        w_near = jnp.where(there, received(got, near_chip, 4 - side), 0.0)
        w_own = received(got, chip, 3 + side)
        p_near = ends[2 * near_chip + end]
        p_other = ends[2 * near_chip + side]
        p_own = low if side == 0 else high
        face_own = vertical_ratio * jnp.sqrt(w_near * w_own)
        east, north = side_faces(w_near, last_lane)
        known = jnp.where(
            red, received(got, near_chip, 15) + horizontal(east, north, p_near), heat[2 * near_chip + end]
        )
        d = received(got, near_chip, 2 - 2 * side) + face_own
        beyond = known + received(got, near_chip, 1) * p_other + face_own * p_own - d * p_near
        beyond = jnp.where(there, beyond, 0.0)
        if side == 0:
            res[0] = beyond
            face_low = face_own
            p_below = p_near
        else:
            res[LEV + 1] = beyond
            face_high = face_own
            p_above = p_near
    for l in range(LEV):
        p = full[l + 2]
        d = dg[l]
        if l == 0:
            d = d + face_low
            vert = face_low * p_below + vf[1] * full[3]
        elif l == LEV - 1:
            d = d + face_high
            vert = vf[l] * full[l + 1] + face_high * p_above
        else:
            vert = vf[l] * full[l + 1] + vf[l + 1] * full[l + 3]
        applied = d * p - (horizontal(ef[l], nf[l], p) + vert)
        res[l + 1] = fr[l] - applied
    weights = restriction_matrix()
    for big in range(LEV // 2):
        z = 2 * big
        s = 0.125 * (res[z] + 3.0 * res[z + 1] + 3.0 * res[z + 2] + res[z + 3])
        e = east_of(s)
        s = 0.125 * (west_of(s) + 3.0 * s + 3.0 * e + east_of(e))
        res[z] = jnp.dot(s, weights, precision=lax.Precision.HIGHEST, preferred_element_type=F32)
        pair = res[z, pl.ds(0, 8, stride=2), :]
        out[big // 4, HALF + big % 4] = jnp.concatenate([pair, pair], axis=0)
    core = lax.axis_index("zk")
    keep[...] = out[core]
    give[...] = out[1 - core]


def last_kernel(both, keep, relaxed, coarse, mine, sems):
    core = lax.axis_index("zk")
    other = 1 - core
    copies = []
    for k in range(PIECES):
        part = pl.ds(k * HALF // PIECES, HALF // PIECES)
        for n, (side, here) in enumerate(((core, keep), (other, both.at[other]))):
            there = relaxed.at[part, pl.ds(pl.multiple_of(side * 16, 8), 16), :]
            copies.append(pltpu.make_async_copy(here.at[part], there, sems.at[k, n]))
    for copy in copies:
        copy.start()
    for big in range(4):
        mine[big, pl.ds(pl.multiple_of(core * 8, 8), 8), :] = keep[HALF + big, 0:8, 0:64]
        mine[big, pl.ds(pl.multiple_of(other * 8, 8), 8), :] = both[other, HALF + big, 0:8, 0:64]
    copies.append(pltpu.make_async_copy(mine, coarse, sems.at[PIECES, 0]))
    copies[-1].start()
    for copy in copies:
        copy.wait()


def restriction_matrix():
    fine = lax.broadcasted_iota(jnp.int32, (LAN, LAN), 0)
    big = lax.broadcasted_iota(jnp.int32, (LAN, LAN), 1)
    off = fine - 2 * big + 1
    inner = (off == 1) | (off == 2)
    outer = (off == 0) | (off == 3)
    return jnp.where(inner, 0.375, jnp.where(outer, 0.125, 0.0)).astype(F32)


def call(kernel, name, shapes, scratch=(), ends=""):
    vm = pl.BlockSpec(memory_space=pltpu.VMEM)
    main = pl.BlockSpec(memory_space=pltpu.HBM)

    def run(*args):
        if not INTERPRET:
            space = pltpu.HBM if ends == "first" else pltpu.VMEM
            args = [pltpu.with_memory_space_constraint(a, space) for a in args]
        plain = ends == "last" or INTERPRET
        return pl.pallas_call(
            kernel,
            out_shape=[jax.ShapeDtypeStruct(s, F32) if plain else pltpu.VMEM(s, F32) for s in shapes],
            in_specs=[main if ends == "first" else vm] * len(args),
            out_specs=[main if ends == "last" else vm] * len(shapes),
            scratch_shapes=scratch,
            name=name,
            compiler_params=pltpu.CompilerParams(vmem_limit_bytes=SCOPED),
            interpret=INTERPRET,
        )(*args)

    return run


def side_by_side():
    chips, cores, count = (lax.axis_size(axis) for axis in AXES)

    def number(chip, core, q):
        return (chip * cores + core) * count + q

    groups = [[number(c, 0, q), number(c, 1, q - 1)] for c in range(chips) for q in range(1, count)]
    for c in range(0, chips, 2):
        groups.append([number(c, 0, 0), number(c + 1, 0, 0)])
        groups.append([number(c, 1, count - 1), number(c + 1, 1, count - 1)])
    return groups


def shards(source, conductivity, fluid, pressure):
    cell = (WIN, LAN)
    field = (LEV, WIN, LAN)
    block = (HALF, 32, LAN)
    vmem = pltpu.VMEM
    (mine,) = call(
        weigh_kernel,
        "weigh",
        [(PLANES, 32, LAN)],
        [vmem(block, t) for t in (F32, F32, jnp.int32, F32)] + [pltpu.SemaphoreType.DMA((PIECES, 4))],
        ends="first",
    )(source, conductivity, fluid, pressure)
    both = lax.all_gather(mine, "zk", axis=0, tiled=False)
    (edge,) = call(edge_kernel, "edge", [(PLANES, 8, LAN)])(both)
    halo = lax.all_gather(edge, AXES, axis=0, tiled=False, axis_index_groups=side_by_side())
    send, *fields = call(first_kernel, "first", [(4, SENT, LAN)] + [field] * 10)(both, halo)
    got = lax.all_to_all(send, "zc", 0, 0, tiled=False)
    part = (HALF + HALF // 2, 16, LAN)
    keep, give = call(
        second_kernel,
        "second",
        [part, part],
        [vmem((2,) + part, F32)]
        + [vmem((8,) + cell, F32)] * 2
        + [vmem((LEV + 4,) + cell, F32), vmem((LEV + 2,) + cell, F32)],
    )(got, *fields)
    ends = lax.all_gather(give, "zk", axis=0, tiled=False)
    coarse = (HALF // 2, 16, LAN // 2)
    relaxed, coarse = call(
        last_kernel,
        "last",
        [block, coarse],
        [vmem(coarse, F32), pltpu.SemaphoreType.DMA((PIECES + 1, 2))],
        ends="last",
    )(ends, keep)
    return relaxed, coarse


def solution(mesh):
    finer = Mesh(mesh.devices.reshape(4, 2, mesh.shape["xy"]), AXES)
    spec = P(("zc", "zk"), "xy", None)
    return jax.shard_map(shards, mesh=finer, in_specs=(spec,) * 4, out_specs=(spec,) * 2, check_vma=False)
```

```python
import jax
import jax.numpy as jnp
from jax import lax
from jax.experimental import pallas as pl
from jax.experimental.pallas import tpu as pltpu
from jax.sharding import Mesh
from jax.sharding import PartitionSpec as P

INTERPRET = False
AXES = ("zc", "zk", "xy")
SCOPED = 4 << 20
vertical_ratio = 100.0
absorption = 0.05

LEV = 16
HALF = 8
PLANES = 20
ARRAYS = 16
OWN = ARRAYS * 16 - 8
OUTER = (0, 1, 2, 3, 4, 5, 6, 7, 8, 9, 10, 11, 11, 12, 12, 7)
ROLLED = (12, 14, 15)
SENT = OWN + 13 * 8
WIN = 24
LAN = 128
F32 = jnp.float32


def east_of(v):
    return pltpu.roll(v, WIN - 1, 0)


def west_of(v):
    return pltpu.roll(v, 1, 0)


def north_of(v):
    return pltpu.roll(v, LAN - 1, 1)


def south_of(v):
    return pltpu.roll(v, 1, 1)


def iotas():
    row = lax.broadcasted_iota(jnp.int32, (WIN, LAN), 0)
    lane = lax.broadcasted_iota(jnp.int32, (WIN, LAN), 1)
    red = ((row + lane) & 1) == 0
    return row, lane, red


def side_faces(w, last_lane):
    east = jnp.sqrt(w * east_of(w))
    north = jnp.where(last_lane, 0.0, jnp.sqrt(w * north_of(w)))
    return east, north


def horizontal(east, north, p):
    return (
        west_of(east * p)
        + east * east_of(p)
        + south_of(north * p)
        + north * north_of(p)
    )


def weigh_kernel(source, cond, fluid, pressure, out, source_v, cond_v, fluid_v, pressure_v, sems):
    copies = [
        pltpu.make_async_copy(cond, cond_v, sems.at[0]),
        pltpu.make_async_copy(fluid, fluid_v, sems.at[1]),
        pltpu.make_async_copy(source, source_v, sems.at[2]),
        pltpu.make_async_copy(pressure, pressure_v, sems.at[3]),
    ]
    for copy in copies:
        copy.start()
    for copy in copies:
        copy.wait()
    for l in range(HALF):
        real = fluid_v[l].astype(F32)
        out[l] = cond_v[l] * real
        out[HALF + l] = real * source_v[l]
    row = lax.broadcasted_iota(jnp.int32, (32, LAN), 0)
    lane = lax.broadcasted_iota(jnp.int32, (32, LAN), 1)
    black = ((row + lane) & 1) == 1
    for l in range(0, HALF, 2):
        out[2 * HALF + l // 2] = jnp.where(black, pressure_v[l], south_of(pressure_v[l + 1]))


def edge_kernel(both, out):
    core = lax.axis_index("zk")
    start = pl.multiple_of(core * 24, 8)
    keep = (lax.broadcasted_iota(jnp.int32, (8, LAN), 0) < 4) == (core == 0)
    for k in range(PLANES):
        low = both[0, k, pl.ds(start, 8), :]
        high = both[1, k, pl.ds(start, 8), :]
        out[k] = jnp.where(keep, low, pltpu.roll(high, 4, 0))


def outer_rows(k):
    at = OWN + 8 * OUTER[k]
    return slice(at, at + 8)


def received(got, group, k):
    outer = got[group, outer_rows(k), :]
    if k in ROLLED:
        outer = pltpu.roll(outer, 4, 0)
    if k == ARRAYS - 1:
        folded = got[group, OWN - 8 : OWN, :]
        return jnp.concatenate([folded, north_of(folded), outer], axis=0)
    return jnp.concatenate([got[group, 16 * k : 16 * k + 16, :], outer], axis=0)


def first_kernel(both, halo, send, ef, nf, vf, dg, fr, rc, mm, al, be, ga):
    core = lax.axis_index("zk")
    row, lane, red = iotas()
    last_lane = lane == LAN - 1
    row8 = lax.broadcasted_iota(jnp.int32, (8, LAN), 0)
    from_near = (row8 < 4) == (core == 0)
    own_at = pl.multiple_of(core * 16, 8)
    near_at = pl.multiple_of(16 - 8 * core, 8)
    block = lax.axis_index("xy")
    inside = jnp.where(core == 0, block > 0, block < lax.axis_size("xy") - 1)

    def window(k, l):
        own = both[l // HALF, k, pl.ds(own_at, 16), :]
        near = both[l // HALF, k, pl.ds(near_at, 8), :]
        far = jnp.where(inside, halo[1 - core, k], 0.0)
        if l >= HALF:
            far = pltpu.roll(far, 4, 0)
        return jnp.concatenate([own, jnp.where(from_near, near, far)], axis=0)

    w = window(0, 0)
    w0 = w
    below = None
    for l in range(LEV):
        east, north = side_faces(w, last_lane)
        ef[l] = east
        nf[l] = north
        south = south_of(north)
        d = absorption + (west_of(east) + east + south + north)
        fluid = w > 0.0
        if below is not None:
            d = d + below
        v = below
        if l < LEV - 1:
            w_next = window((l + 1) % HALF, l + 1)
            below = vertical_ratio * jnp.sqrt(w_next * w)
            vf[l + 1] = below
            d = d + below
            w = w_next
        d = jnp.where(fluid, d, 1.0)
        dg[l] = d
        f = window(HALF + l % HALF, l)
        fr[l] = f
        if l % 2 == 0:
            old = window(2 * HALF + l % HALF // 2, l)
            old_up = north_of(old)
            b = f + ((west_of(east * old) + east * east_of(old)) + (south * south_of(old) + north * old_up))
        else:
            b = f + ((west_of(east * old_up) + east * east_of(old_up)) + (south * old + north * north_of(old_up)))
        if l == 0:
            heat0, d0 = b, d
            continue
        if l == 1:
            dd, bb, g = d, b, v
        elif l < LEV - 1:
            dd = d - mult * v
            bb = b + mult * bb
            g = mult * g
        if l < LEV - 1:
            rcp = 1.0 / dd
            mult = below * rcp
            rc[l] = rcp
            mm[l] = mult
            al[l] = bb * rcp
            be[l] = g * rcp
    heat15, d15, w15 = b, d, w
    e_tt, e_bb = ef[0], ef[LEV - 1]
    n_tt, n_bb = nf[0], nf[LEV - 1]
    e_tb = e_bt = n_tb = n_bt = jnp.zeros((WIN, LAN), F32)
    con_low = fr[0]
    con_high = fr[LEV - 1]
    for l in range(LEV - 2, 0, -1):
        mult = mm[l]
        if l == LEV - 2:
            alpha, beta, gamma = al[l], be[l], mult
            high_share = beta
        else:
            alpha = al[l] + mult * alpha
            beta = be[l] + mult * beta
            gamma = mult * gamma
        alpha = jnp.where(red, alpha, 0.0)
        al[l] = alpha
        be[l] = beta
        ga[l] = gamma
        east, north = ef[l], nf[l]
        there_b, there_g = east_of(beta), east_of(gamma)
        mine_b, mine_g = east * beta, east * gamma
        e_tt = e_tt + mine_b * there_b
        e_tb = e_tb + mine_b * there_g
        e_bt = e_bt + mine_g * there_b
        e_bb = e_bb + mine_g * there_g
        b = fr[l] + horizontal(east, north, alpha)
        con_low = con_low + beta * b
        con_high = con_high + gamma * b
    for l in range(LEV - 2, 0, -1):
        alpha, beta, gamma, east, north = al[l], be[l], ga[l], ef[l], nf[l]
        there_b, there_g = north_of(beta), north_of(gamma)
        mine_b, mine_g = north * beta, north * gamma
        n_tt = n_tt + mine_b * there_b
        n_tb = n_tb + mine_b * there_g
        n_bt = n_bt + mine_g * there_b
        n_bb = n_bb + mine_g * there_g
    v1 = vf[1]
    v15 = vf[LEV - 1]
    self_low = v1 * be[1]
    self_high = v15 * ga[LEV - 2]
    own_low = v1 * al[1]
    own_high = v15 * al[LEV - 2]
    common = [d0 - self_low, v15 * be[LEV - 2], d15 - self_high, w0, w15]
    common += [jnp.where(red, heat0 + own_low, con_low), jnp.where(red, heat15 + own_high, con_high)]
    common += [e_tt, e_tb, e_bt, e_bb, n_tt, n_tb, n_bt, n_bb]
    chip = lax.axis_index("zc")
    row8 = lax.broadcasted_iota(jnp.int32, (8, LAN), 0)
    upward = fr[LEV - 1] + own_high
    downward = fr[0] + own_low
    outer = [value[16:24] for value in common]
    inner = (row8 < 2) | (row8 > 5)
    for k in (11, 13):
        outer[k] = jnp.where(inner, outer[k], pltpu.roll(outer[k + 1], 4, 0))
    kept = (row8 < 2) | (row8 > 4)
    for peer in range(4):
        last = jnp.where(chip < peer, upward, downward)
        for k in range(ARRAYS):
            if k < ARRAYS - 1:
                send[peer, 16 * k : 16 * k + 16, :] = common[k][0:16]
            else:
                send[peer, OWN - 8 : OWN, :] = jnp.where(red[0:8], last[0:8], south_of(last[8:16]))
            if k in ROLLED:
                continue
            tile = outer[k]
            if k == 7:
                tile = jnp.where(kept, tile, pltpu.roll(last[16:24], 4, 0))
            send[peer, outer_rows(k), :] = tile


def chain_factor(diag, link):
    rcp = [None] * 8
    for j in range(4):
        pivot = diag[j] if j == 0 else diag[j] - link[j] * link[j] * rcp[j - 1]
        rcp[j] = 1.0 / pivot
    for j in range(7, 4, -1):
        pivot = diag[j] if j == 7 else diag[j] - link[j + 1] * link[j + 1] * rcp[j + 1]
        rcp[j] = 1.0 / pivot
    rcp[4] = 1.0 / (diag[4] - link[4] * link[4] * rcp[3] - link[5] * link[5] * rcp[5])
    return rcp


def chain_solve(rcp, link, right):
    acc = list(right)
    for j in range(1, 4):
        acc[j] = acc[j] + link[j] * (rcp[j - 1] * acc[j - 1])
    for j in range(6, 4, -1):
        acc[j] = acc[j] + link[j + 1] * (rcp[j + 1] * acc[j + 1])
    out = [None] * 8
    out[4] = (acc[4] + link[4] * (rcp[3] * acc[3]) + link[5] * (rcp[5] * acc[5])) * rcp[4]
    for j in range(3, -1, -1):
        out[j] = (acc[j] + link[j + 1] * out[j + 1]) * rcp[j]
    for j in range(5, 8):
        out[j] = (acc[j] + link[j] * out[j - 1]) * rcp[j]
    return out


def second_kernel(got, ef, nf, vf, dg, fr, rc, mm, al, be, ga, keep, give, out, ends, heat, full, res):
    chip = lax.axis_index("zc")
    row, lane, red = iotas()
    last_lane = lane == LAN - 1
    diag, link, right = [], [None], []
    for group in range(4):
        up, down = received(got, group, 0), received(got, group, 2)
        if group > 0:
            up = up + face
        if group < 3:
            face = vertical_ratio * jnp.sqrt(received(got, group, 4) * received(got, group + 1, 3))
            down = down + face
        diag += [up, down]
        link += [received(got, group, 1)] + ([face] if group < 3 else [])
        right += [received(got, group, 5), received(got, group, 6)]
    rcp = chain_factor(diag, link)
    reds = [jnp.where(red, v, 0.0) for v in chain_solve(rcp, link, right)]
    for group in range(4):
        t, b = reds[2 * group], reds[2 * group + 1]
        e_tt, e_tb, e_bt, e_bb, n_tt, n_tb, n_bt, n_bb = (received(got, group, 7 + k) for k in range(8))
        te, be_, tn, bn = east_of(t), east_of(b), north_of(t), north_of(b)
        right[2 * group] = right[2 * group] + (
            (e_tt * te + e_tb * be_)
            + (n_tt * tn + n_tb * bn)
            + west_of(e_tt * t + e_bt * b)
            + south_of(n_tt * t + n_bt * b)
        )
        right[2 * group + 1] = right[2 * group + 1] + (
            (e_bt * te + e_bb * be_)
            + (n_bt * tn + n_bb * bn)
            + west_of(e_tb * t + e_bb * b)
            + south_of(n_tb * t + n_bb * b)
        )
    blacks = chain_solve(rcp, link, right)
    for j in range(8):
        ends[j] = jnp.where(red, reds[j], blacks[j])
        heat[j] = right[j]
    low = ends[2 * chip]
    high = ends[2 * chip + 1]
    full[2] = low
    full[LEV + 1] = high
    bb = jnp.where(red, 0.0, vf[1] * low)
    for l in range(1, LEV - 1):
        p = jnp.where(red, al[l] + be[l] * low + ga[l] * high, 0.0)
        full[l + 2] = p
        b = fr[l] + horizontal(ef[l], nf[l], p)
        bb = b + (bb if l == 1 else mm[l - 1] * bb)
        res[l] = bb * rc[l]
    cur = high
    for l in range(LEV - 2, 0, -1):
        cur = res[l] + mm[l] * cur
        full[l + 2] = jnp.where(red, full[l + 2], cur)
    for l in range(LEV):
        out[l // HALF, l % HALF] = full[l + 2, 0:16, :]

    for side in (0, 1):
        near_chip = jnp.maximum(chip - 1, 0) if side == 0 else jnp.minimum(chip + 1, 3)
        there = chip > 0 if side == 0 else chip < 3
        end = 1 - side
        w_near = jnp.where(there, received(got, near_chip, 4 - side), 0.0)
        w_own = received(got, chip, 3 + side)
        p_near = ends[2 * near_chip + end]
        p_other = ends[2 * near_chip + side]
        p_own = low if side == 0 else high
        face_own = vertical_ratio * jnp.sqrt(w_near * w_own)
        east, north = side_faces(w_near, last_lane)
        known = jnp.where(
            red, received(got, near_chip, 15) + horizontal(east, north, p_near), heat[2 * near_chip + end]
        )
        d = received(got, near_chip, 2 - 2 * side) + face_own
        beyond = known + received(got, near_chip, 1) * p_other + face_own * p_own - d * p_near
        beyond = jnp.where(there, beyond, 0.0)
        if side == 0:
            res[0] = beyond
            face_low = face_own
            p_below = p_near
        else:
            res[LEV + 1] = beyond
            face_high = face_own
            p_above = p_near
    for l in range(LEV):
        p = full[l + 2]
        d = dg[l]
        if l == 0:
            d = d + face_low
            vert = face_low * p_below + vf[1] * full[3]
        elif l == LEV - 1:
            d = d + face_high
            vert = vf[l] * full[l + 1] + face_high * p_above
        else:
            vert = vf[l] * full[l + 1] + vf[l + 1] * full[l + 3]
        applied = d * p - (horizontal(ef[l], nf[l], p) + vert)
        res[l + 1] = fr[l] - applied
    weights = restriction_matrix()
    for big in range(LEV // 2):
        z = 2 * big
        s = 0.125 * (res[z] + 3.0 * res[z + 1] + 3.0 * res[z + 2] + res[z + 3])
        e = east_of(s)
        s = 0.125 * (west_of(s) + 3.0 * s + 3.0 * e + east_of(e))
        res[z] = jnp.dot(s, weights, precision=lax.Precision.HIGHEST, preferred_element_type=F32)
        pair = res[z, pl.ds(0, 8, stride=2), :]
        out[big // 4, HALF + big % 4] = jnp.concatenate([pair, pair], axis=0)
    core = lax.axis_index("zk")
    keep[...] = out[core]
    give[...] = out[1 - core]


def last_kernel(both, keep, relaxed, coarse):
    core = lax.axis_index("zk")
    other = 1 - core
    for side, of in ((core, lambda k: keep[k]), (other, lambda k: both[other, k])):
        at = pl.multiple_of(side * 16, 8)
        for l in range(HALF):
            relaxed[l, pl.ds(at, 16), :] = of(l)
        at = pl.multiple_of(side * 8, 8)
        for big in range(4):
            coarse[big, pl.ds(at, 8), :] = of(HALF + big)[0:8, 0:64]


def restriction_matrix():
    fine = lax.broadcasted_iota(jnp.int32, (LAN, LAN), 0)
    big = lax.broadcasted_iota(jnp.int32, (LAN, LAN), 1)
    off = fine - 2 * big + 1
    inner = (off == 1) | (off == 2)
    outer = (off == 0) | (off == 3)
    return jnp.where(inner, 0.375, jnp.where(outer, 0.125, 0.0)).astype(F32)


def call(kernel, name, shapes, scratch=(), ends=""):
    vm = pl.BlockSpec(memory_space=pltpu.VMEM)
    main = pl.BlockSpec(memory_space=pltpu.HBM)

    def run(*args):
        if not INTERPRET:
            space = pltpu.HBM if ends == "first" else pltpu.VMEM
            args = [pltpu.with_memory_space_constraint(a, space) for a in args]
        plain = ends == "last" or INTERPRET
        return pl.pallas_call(
            kernel,
            out_shape=[jax.ShapeDtypeStruct(s, F32) if plain else pltpu.VMEM(s, F32) for s in shapes],
            in_specs=[main if ends == "first" else vm] * len(args),
            out_specs=[vm] * len(shapes),
            scratch_shapes=scratch,
            name=name,
            compiler_params=pltpu.CompilerParams(vmem_limit_bytes=SCOPED),
            interpret=INTERPRET,
        )(*args)

    return run


def side_by_side():
    chips, cores, count = (lax.axis_size(axis) for axis in AXES)

    def number(chip, core, q):
        return (chip * cores + core) * count + q

    groups = [[number(c, 0, q), number(c, 1, q - 1)] for c in range(chips) for q in range(1, count)]
    for c in range(0, chips, 2):
        groups.append([number(c, 0, 0), number(c + 1, 0, 0)])
        groups.append([number(c, 1, count - 1), number(c + 1, 1, count - 1)])
    return groups


def shards(source, conductivity, fluid, pressure):
    cell = (WIN, LAN)
    field = (LEV, WIN, LAN)
    block = (HALF, 32, LAN)
    vmem = pltpu.VMEM
    (mine,) = call(
        weigh_kernel,
        "weigh",
        [(PLANES, 32, LAN)],
        [vmem(block, t) for t in (F32, F32, jnp.int32, F32)] + [pltpu.SemaphoreType.DMA((4,))],
        ends="first",
    )(source, conductivity, fluid, pressure)
    both = lax.all_gather(mine, "zk", axis=0, tiled=False)
    (edge,) = call(edge_kernel, "edge", [(PLANES, 8, LAN)])(both)
    halo = lax.all_gather(edge, AXES, axis=0, tiled=False, axis_index_groups=side_by_side())
    send, *fields = call(first_kernel, "first", [(4, SENT, LAN)] + [field] * 10)(both, halo)
    got = lax.all_to_all(send, "zc", 0, 0, tiled=False)
    part = (HALF + HALF // 2, 16, LAN)
    keep, give = call(
        second_kernel,
        "second",
        [part, part],
        [vmem((2,) + part, F32)]
        + [vmem((8,) + cell, F32)] * 2
        + [vmem((LEV + 4,) + cell, F32), vmem((LEV + 2,) + cell, F32)],
    )(got, *fields)
    ends = lax.all_gather(give, "zk", axis=0, tiled=False)
    coarse = (HALF // 2, 16, LAN // 2)
    relaxed, coarse = call(
        last_kernel,
        "last",
        [block, coarse],
        ends="last",
    )(ends, keep)
    return relaxed, coarse


def solution(mesh):
    finer = Mesh(mesh.devices.reshape(4, 2, mesh.shape["xy"]), AXES)
    spec = P(("zc", "zk"), "xy", None)
    return jax.shard_map(shards, mesh=finer, in_specs=(spec,) * 4, out_specs=(spec,) * 2, check_vma=False)
```

```python
import jax
import jax.numpy as jnp
from jax import lax
from jax.experimental import pallas as pl
from jax.experimental.pallas import tpu as pltpu
from jax.sharding import Mesh
from jax.sharding import PartitionSpec as P

INTERPRET = False
AXES = ("zc", "zk", "xy")
SCOPED = 4 << 20
vertical_ratio = 100.0
absorption = 0.05

LEV = 16
HALF = 8
ARRAYS = 16
OWN = ARRAYS * 16 - 8
OUTER = (0, 1, 2, 3, 4, 5, None, 6, 7, 8, 9, 10, 10, 11, 11, 6)
ROLLED = (12, 14, 15)
SENT = OWN + 12 * 8
WIN = 24
LAN = 128
F32 = jnp.float32


def east_of(v):
    return pltpu.roll(v, WIN - 1, 0)


def west_of(v):
    return pltpu.roll(v, 1, 0)


def north_of(v):
    return pltpu.roll(v, LAN - 1, 1)


def south_of(v):
    return pltpu.roll(v, 1, 1)


def iotas():
    row = lax.broadcasted_iota(jnp.int32, (WIN, LAN), 0)
    lane = lax.broadcasted_iota(jnp.int32, (WIN, LAN), 1)
    red = ((row + lane) & 1) == 0
    return row, lane, red


def side_faces(w, last_lane):
    east = jnp.sqrt(w * east_of(w))
    north = jnp.where(last_lane, 0.0, jnp.sqrt(w * north_of(w)))
    return east, north


def horizontal(east, north, p):
    return (
        west_of(east * p)
        + east * east_of(p)
        + south_of(north * p)
        + north * north_of(p)
    )


def weigh_kernel(source, cond, fluid, pressure, out, source_v, cond_v, fluid_v, sems):
    copies = [
        pltpu.make_async_copy(cond, cond_v, sems.at[0]),
        pltpu.make_async_copy(fluid, fluid_v, sems.at[1]),
        pltpu.make_async_copy(source, source_v, sems.at[2]),
        pltpu.make_async_copy(pressure, out.at[2], sems.at[3]),
    ]
    for copy in copies:
        copy.start()
    for copy in copies:
        copy.wait()
    for l in range(HALF):
        real = fluid_v[l].astype(F32)
        out[0, l] = cond_v[l] * real
        out[1, l] = real * source_v[l]


def edge_kernel(both, out):
    core = lax.axis_index("zk")
    start = pl.multiple_of(core * 24, 8)
    keep = (lax.broadcasted_iota(jnp.int32, (8, LAN), 0) < 4) == (core == 0)
    for f in range(3):
        for l in range(HALF):
            low = both[0, f, l, pl.ds(start, 8), :]
            high = both[1, f, l, pl.ds(start, 8), :]
            out[f, l] = jnp.where(keep, low, pltpu.roll(high, 4, 0))


def outer_rows(k):
    at = OWN + 8 * OUTER[k]
    return slice(at, at + 8)


def received(got, group, k):
    if k == 6:
        east = pltpu.roll(got[group, outer_rows(8), :], 6, 0)
        west = pltpu.roll(got[group, outer_rows(9), :], 3, 0)
        outer = jnp.where(lax.broadcasted_iota(jnp.int32, (8, LAN), 0) < 3, east, west)
    else:
        outer = got[group, outer_rows(k), :]
    if k in ROLLED:
        outer = pltpu.roll(outer, 4, 0)
    if k == ARRAYS - 1:
        folded = got[group, OWN - 8 : OWN, :]
        return jnp.concatenate([folded, pltpu.roll(folded, 7, 0), outer], axis=0)
    return jnp.concatenate([got[group, 16 * k : 16 * k + 16, :], outer], axis=0)


def first_kernel(both, halo, send, ef, nf, vf, dg, fr, rc, mm, al, be, ga):
    core = lax.axis_index("zk")
    row, lane, red = iotas()
    last_lane = lane == LAN - 1
    row8 = lax.broadcasted_iota(jnp.int32, (8, LAN), 0)
    from_near = (row8 < 4) == (core == 0)
    own_at = pl.multiple_of(core * 16, 8)
    near_at = pl.multiple_of(16 - 8 * core, 8)
    block = lax.axis_index("xy")
    inside = jnp.where(core == 0, block > 0, block < lax.axis_size("xy") - 1)

    def window(f, l):
        own = both[l // 8, f, l % 8, pl.ds(own_at, 16), :]
        near = both[l // 8, f, l % 8, pl.ds(near_at, 8), :]
        far = jnp.where(inside, halo[1 - core, f, l % 8], 0.0)
        if l >= HALF:
            far = pltpu.roll(far, 4, 0)
        return jnp.concatenate([own, jnp.where(from_near, near, far)], axis=0)

    for l in range(LEV):
        w = window(0, l)
        east, north = side_faces(w, last_lane)
        ef[l] = east
        nf[l] = north
        if l == 0:
            w0 = w
            vf[0] = jnp.zeros_like(w)
        else:
            vf[l] = vertical_ratio * jnp.sqrt(w * w_below)
        w_below = w
        fluid = jnp.where(w > 0.0, 1.0, 0.0)
        dg[l] = fluid * (absorption + (west_of(east) + east + south_of(north) + north)) + (1.0 - fluid)
        fr[l] = window(1, l)
    w15 = w_below
    heat0 = fr[0] + horizontal(ef[0], nf[0], window(2, 0))
    d0 = dg[0] + vf[1]
    dg[0] = d0
    for l in range(1, LEV):
        d = dg[l] + vf[l]
        if l < LEV - 1:
            d = d + vf[l + 1]
        dg[l] = d
        b = fr[l] + horizontal(ef[l], nf[l], window(2, l))
        v = vf[l]
        if l == 1:
            dd, bb, g = d, b, v
        elif l < LEV - 1:
            dd = d - mult * v
            bb = b + mult * bb
            g = mult * g
        if l < LEV - 1:
            rcp = 1.0 / dd
            mult = vf[l + 1] * rcp
            rc[l] = rcp
            mm[l] = mult
            al[l] = bb * rcp
            be[l] = g * rcp
    heat15 = b
    alpha = jnp.where(red, al[LEV - 2], 0.0)
    beta = be[LEV - 2]
    gamma = mm[LEV - 2]
    al[LEV - 2] = alpha
    ga[LEV - 2] = gamma
    for l in range(LEV - 3, 0, -1):
        mult = mm[l]
        alpha = jnp.where(red, al[l] + mult * alpha, 0.0)
        beta = be[l] + mult * beta
        gamma = mult * gamma
        al[l] = alpha
        be[l] = beta
        ga[l] = gamma
    v1 = vf[1]
    v15 = vf[LEV - 1]
    self_low = v1 * be[1]
    self_high = v15 * ga[LEV - 2]
    e_tt, e_bb = ef[0], ef[LEV - 1]
    n_tt, n_bb = nf[0], nf[LEV - 1]
    e_tb = e_bt = n_tb = n_bt = jnp.zeros((WIN, LAN), F32)
    con_low = fr[0]
    con_high = fr[LEV - 1]
    for l in range(1, LEV - 1):
        beta, gamma, alpha = be[l], ga[l], al[l]
        east, north = ef[l], nf[l]
        there_b, there_g = east_of(beta), east_of(gamma)
        mine_b, mine_g = east * beta, east * gamma
        e_tt = e_tt + mine_b * there_b
        e_tb = e_tb + mine_b * there_g
        e_bt = e_bt + mine_g * there_b
        e_bb = e_bb + mine_g * there_g
        there_b, there_g = north_of(beta), north_of(gamma)
        mine_b, mine_g = north * beta, north * gamma
        n_tt = n_tt + mine_b * there_b
        n_tb = n_tb + mine_b * there_g
        n_bt = n_bt + mine_g * there_b
        n_bb = n_bb + mine_g * there_g
        b = fr[l] + horizontal(east, north, alpha)
        con_low = con_low + beta * b
        con_high = con_high + gamma * b
    own_low = v1 * al[1]
    own_high = v15 * al[LEV - 2]
    common = [d0 - self_low, v15 * be[LEV - 2], dg[LEV - 1] - self_high, w0, w15]
    common += [jnp.where(red, heat0 + own_low, con_low), jnp.where(red, heat15 + own_high, con_high)]
    common += [e_tt, e_tb, e_bt, e_bb, n_tt, n_tb, n_bt, n_bb]
    chip = lax.axis_index("zc")
    row8 = lax.broadcasted_iota(jnp.int32, (8, LAN), 0)
    upward = fr[LEV - 1] + own_high
    downward = fr[0] + own_low
    outer = [value[16:24] for value in common]
    inner = (row8 < 2) | (row8 > 5)
    for k in (11, 13):
        outer[k] = jnp.where(inner, outer[k], pltpu.roll(outer[k + 1], 4, 0))
    kept = (row8 < 2) | (row8 > 4)
    outer[8] = jnp.where(kept, outer[8], pltpu.roll(outer[6], 2, 0))
    outer[9] = jnp.where(kept, outer[9], pltpu.roll(outer[6], 5, 0))
    for peer in range(4):
        last = jnp.where(chip < peer, upward, downward)
        for k in range(ARRAYS):
            if k < ARRAYS - 1:
                send[peer, 16 * k : 16 * k + 16, :] = common[k][0:16]
            else:
                send[peer, OWN - 8 : OWN, :] = jnp.where(red[0:8], last[0:8], pltpu.roll(last[8:16], 1, 0))
            if k in ROLLED or k == 6:
                continue
            tile = outer[k]
            if k == 7:
                tile = jnp.where(kept, tile, pltpu.roll(last[16:24], 4, 0))
            send[peer, outer_rows(k), :] = tile


def chain_factor(diag, link):
    rcp = [None] * 8
    for j in range(4):
        pivot = diag[j] if j == 0 else diag[j] - link[j] * link[j] * rcp[j - 1]
        rcp[j] = 1.0 / pivot
    for j in range(7, 4, -1):
        pivot = diag[j] if j == 7 else diag[j] - link[j + 1] * link[j + 1] * rcp[j + 1]
        rcp[j] = 1.0 / pivot
    rcp[4] = 1.0 / (diag[4] - link[4] * link[4] * rcp[3] - link[5] * link[5] * rcp[5])
    return rcp


def chain_solve(rcp, link, right):
    acc = list(right)
    for j in range(1, 4):
        acc[j] = acc[j] + link[j] * (rcp[j - 1] * acc[j - 1])
    for j in range(6, 4, -1):
        acc[j] = acc[j] + link[j + 1] * (rcp[j + 1] * acc[j + 1])
    out = [None] * 8
    out[4] = (acc[4] + link[4] * (rcp[3] * acc[3]) + link[5] * (rcp[5] * acc[5])) * rcp[4]
    for j in range(3, -1, -1):
        out[j] = (acc[j] + link[j + 1] * out[j + 1]) * rcp[j]
    for j in range(5, 8):
        out[j] = (acc[j] + link[j] * out[j - 1]) * rcp[j]
    return out


def second_kernel(got, ef, nf, vf, dg, fr, rc, mm, al, be, ga, keep, give, out, ends, heat, full, res):
    chip = lax.axis_index("zc")
    row, lane, red = iotas()
    last_lane = lane == LAN - 1
    diag, link, right = [], [None], []
    for group in range(4):
        up, down = received(got, group, 0), received(got, group, 2)
        if group > 0:
            up = up + face
        if group < 3:
            face = vertical_ratio * jnp.sqrt(received(got, group, 4) * received(got, group + 1, 3))
            down = down + face
        diag += [up, down]
        link += [received(got, group, 1)] + ([face] if group < 3 else [])
        right += [received(got, group, 5), received(got, group, 6)]
    rcp = chain_factor(diag, link)
    reds = [jnp.where(red, v, 0.0) for v in chain_solve(rcp, link, right)]
    for group in range(4):
        t, b = reds[2 * group], reds[2 * group + 1]
        e_tt, e_tb, e_bt, e_bb, n_tt, n_tb, n_bt, n_bb = (received(got, group, 7 + k) for k in range(8))
        te, be_, tn, bn = east_of(t), east_of(b), north_of(t), north_of(b)
        right[2 * group] = right[2 * group] + (
            (e_tt * te + e_tb * be_)
            + (n_tt * tn + n_tb * bn)
            + west_of(e_tt * t + e_bt * b)
            + south_of(n_tt * t + n_bt * b)
        )
        right[2 * group + 1] = right[2 * group + 1] + (
            (e_bt * te + e_bb * be_)
            + (n_bt * tn + n_bb * bn)
            + west_of(e_tb * t + e_bb * b)
            + south_of(n_tb * t + n_bb * b)
        )
    blacks = chain_solve(rcp, link, right)
    for j in range(8):
        ends[j] = jnp.where(red, reds[j], blacks[j])
        heat[j] = right[j]
    low = ends[2 * chip]
    high = ends[2 * chip + 1]
    full[2] = low
    full[LEV + 1] = high
    bb = jnp.where(red, 0.0, vf[1] * low)
    for l in range(1, LEV - 1):
        p = jnp.where(red, al[l] + be[l] * low + ga[l] * high, 0.0)
        full[l + 2] = p
        b = fr[l] + horizontal(ef[l], nf[l], p)
        bb = b + (bb if l == 1 else mm[l - 1] * bb)
        res[l] = bb * rc[l]
    cur = high
    for l in range(LEV - 2, 0, -1):
        cur = res[l] + mm[l] * cur
        full[l + 2] = jnp.where(red, full[l + 2], cur)
    for l in range(LEV):
        out[l // HALF, l % HALF] = full[l + 2, 0:16, :]

    for side in (0, 1):
        near_chip = jnp.maximum(chip - 1, 0) if side == 0 else jnp.minimum(chip + 1, 3)
        there = chip > 0 if side == 0 else chip < 3
        end = 1 - side
        w_near = jnp.where(there, received(got, near_chip, 4 - side), 0.0)
        w_own = received(got, chip, 3 + side)
        p_near = ends[2 * near_chip + end]
        p_other = ends[2 * near_chip + side]
        p_own = low if side == 0 else high
        face_own = vertical_ratio * jnp.sqrt(w_near * w_own)
        east, north = side_faces(w_near, last_lane)
        known = jnp.where(
            red, received(got, near_chip, 15) + horizontal(east, north, p_near), heat[2 * near_chip + end]
        )
        d = received(got, near_chip, 2 - 2 * side) + face_own
        beyond = known + received(got, near_chip, 1) * p_other + face_own * p_own - d * p_near
        beyond = jnp.where(there, beyond, 0.0)
        if side == 0:
            res[0] = beyond
            face_low = face_own
            p_below = p_near
        else:
            res[LEV + 1] = beyond
            face_high = face_own
            p_above = p_near
    for l in range(LEV):
        p = full[l + 2]
        d = dg[l]
        if l == 0:
            d = d + face_low
            vert = face_low * p_below + vf[1] * full[3]
        elif l == LEV - 1:
            d = d + face_high
            vert = vf[l] * full[l + 1] + face_high * p_above
        else:
            vert = vf[l] * full[l + 1] + vf[l + 1] * full[l + 3]
        applied = d * p - (horizontal(ef[l], nf[l], p) + vert)
        res[l + 1] = fr[l] - applied
    weights = restriction_matrix()
    for big in range(LEV // 2):
        z = 2 * big
        s = 0.125 * (res[z] + 3.0 * res[z + 1] + 3.0 * res[z + 2] + res[z + 3])
        e = east_of(s)
        s = 0.125 * (west_of(s) + 3.0 * s + 3.0 * e + east_of(e))
        res[z] = jnp.dot(s, weights, precision=lax.Precision.HIGHEST, preferred_element_type=F32)
        pair = res[z, pl.ds(0, 8, stride=2), :]
        out[big // 4, HALF + big % 4] = jnp.concatenate([pair, pair], axis=0)
    core = lax.axis_index("zk")
    keep[...] = out[core]
    give[...] = out[1 - core]


def last_kernel(both, keep, relaxed, coarse):
    core = lax.axis_index("zk")
    other = 1 - core
    for side, of in ((core, lambda k: keep[k]), (other, lambda k: both[other, k])):
        at = pl.multiple_of(side * 16, 8)
        for l in range(HALF):
            relaxed[l, pl.ds(at, 16), :] = of(l)
        at = pl.multiple_of(side * 8, 8)
        for big in range(4):
            coarse[big, pl.ds(at, 8), :] = of(HALF + big)[0:8, 0:64]


def restriction_matrix():
    fine = lax.broadcasted_iota(jnp.int32, (LAN, LAN), 0)
    big = lax.broadcasted_iota(jnp.int32, (LAN, LAN), 1)
    off = fine - 2 * big + 1
    inner = (off == 1) | (off == 2)
    outer = (off == 0) | (off == 3)
    return jnp.where(inner, 0.375, jnp.where(outer, 0.125, 0.0)).astype(F32)


def call(kernel, name, shapes, scratch=(), ends=""):
    vm = pl.BlockSpec(memory_space=pltpu.VMEM)
    main = pl.BlockSpec(memory_space=pltpu.HBM)

    def run(*args):
        if not INTERPRET:
            space = pltpu.HBM if ends == "first" else pltpu.VMEM
            args = [pltpu.with_memory_space_constraint(a, space) for a in args]
        plain = ends == "last" or INTERPRET
        return pl.pallas_call(
            kernel,
            out_shape=[jax.ShapeDtypeStruct(s, F32) if plain else pltpu.VMEM(s, F32) for s in shapes],
            in_specs=[main if ends == "first" else vm] * len(args),
            out_specs=[vm] * len(shapes),
            scratch_shapes=scratch,
            name=name,
            compiler_params=pltpu.CompilerParams(vmem_limit_bytes=SCOPED),
            interpret=INTERPRET,
        )(*args)

    return run


def side_by_side():
    chips, cores, count = (lax.axis_size(axis) for axis in AXES)

    def number(chip, core, q):
        return (chip * cores + core) * count + q

    groups = [[number(c, 0, q), number(c, 1, q - 1)] for c in range(chips) for q in range(1, count)]
    for c in range(0, chips, 2):
        groups.append([number(c, 0, 0), number(c + 1, 0, 0)])
        groups.append([number(c, 1, count - 1), number(c + 1, 1, count - 1)])
    return groups


def shards(source, conductivity, fluid, pressure):
    cell = (WIN, LAN)
    field = (LEV, WIN, LAN)
    block = (HALF, 32, LAN)
    vmem = pltpu.VMEM
    (mine,) = call(
        weigh_kernel,
        "weigh",
        [(3,) + block],
        [vmem(block, F32), vmem(block, F32), vmem(block, jnp.int32), pltpu.SemaphoreType.DMA((4,))],
        ends="first",
    )(source, conductivity, fluid, pressure)
    both = lax.all_gather(mine, "zk", axis=0, tiled=False)
    (edge,) = call(edge_kernel, "edge", [(3, HALF, 8, LAN)])(both)
    halo = lax.all_gather(edge, AXES, axis=0, tiled=False, axis_index_groups=side_by_side())
    send, *fields = call(first_kernel, "first", [(4, SENT, LAN)] + [field] * 10)(both, halo)
    got = lax.all_to_all(send, "zc", 0, 0, tiled=False)
    part = (HALF + HALF // 2, 16, LAN)
    keep, give = call(
        second_kernel,
        "second",
        [part, part],
        [vmem((2,) + part, F32)]
        + [vmem((8,) + cell, F32)] * 2
        + [vmem((LEV + 4,) + cell, F32), vmem((LEV + 2,) + cell, F32)],
    )(got, *fields)
    ends = lax.all_gather(give, "zk", axis=0, tiled=False)
    coarse = (HALF // 2, 16, LAN // 2)
    relaxed, coarse = call(
        last_kernel,
        "last",
        [block, coarse],
        ends="last",
    )(ends, keep)
    return relaxed, coarse


def solution(mesh):
    finer = Mesh(mesh.devices.reshape(4, 2, mesh.shape["xy"]), AXES)
    spec = P(("zc", "zk"), "xy", None)
    return jax.shard_map(shards, mesh=finer, in_specs=(spec,) * 4, out_specs=(spec,) * 2, check_vma=False)
```

```python
import jax
import jax.numpy as jnp
from jax import lax
from jax.experimental import pallas as pl
from jax.experimental.pallas import tpu as pltpu
from jax.sharding import Mesh
from jax.sharding import PartitionSpec as P

INTERPRET = False
AXES = ("zc", "zk", "xy")
SCOPED = 4 << 20
vertical_ratio = 100.0
absorption = 0.05

LEV = 16
HALF = 8
PLANES = 20
ARRAYS = 16
OWN = ARRAYS * 16 - 8
OUTER = (0, 1, 2, 3, 4, 5, None, 6, 7, 8, 9, 10, 10, 11, 11, 6)
ROLLED = (12, 14, 15)
SENT = OWN + 12 * 8
WIN = 24
LAN = 128
F32 = jnp.float32


def east_of(v):
    return pltpu.roll(v, WIN - 1, 0)


def west_of(v):
    return pltpu.roll(v, 1, 0)


def north_of(v):
    return pltpu.roll(v, LAN - 1, 1)


def south_of(v):
    return pltpu.roll(v, 1, 1)


def iotas():
    row = lax.broadcasted_iota(jnp.int32, (WIN, LAN), 0)
    lane = lax.broadcasted_iota(jnp.int32, (WIN, LAN), 1)
    red = ((row + lane) & 1) == 0
    return row, lane, red


def side_faces(w, last_lane):
    east = jnp.sqrt(w * east_of(w))
    north = jnp.where(last_lane, 0.0, jnp.sqrt(w * north_of(w)))
    return east, north


def horizontal(east, north, p):
    return (
        west_of(east * p)
        + east * east_of(p)
        + south_of(north * p)
        + north * north_of(p)
    )


def row_down(tile):
    row = lax.broadcasted_iota(jnp.int32, (8, LAN), 0)
    return jnp.where((row & 3) == 0, pltpu.roll(tile, 5, 0), pltpu.roll(tile, 1, 0))


def row_up(tile):
    row = lax.broadcasted_iota(jnp.int32, (8, LAN), 0)
    return jnp.where((row & 3) == 3, pltpu.roll(tile, 3, 0), pltpu.roll(tile, 7, 0))


def weigh_kernel(source, cond, fluid, pressure, out, source_v, cond_v, fluid_v, pressure_v, sems):
    copies = [
        pltpu.make_async_copy(cond, cond_v, sems.at[0]),
        pltpu.make_async_copy(fluid, fluid_v, sems.at[1]),
        pltpu.make_async_copy(source, source_v, sems.at[2]),
        pltpu.make_async_copy(pressure, pressure_v, sems.at[3]),
    ]
    for copy in copies:
        copy.start()
    for copy in copies:
        copy.wait()
    for l in range(HALF):
        real = fluid_v[l].astype(F32)
        out[l] = cond_v[l] * real
        out[HALF + l] = real * source_v[l]
    row = lax.broadcasted_iota(jnp.int32, (8, LAN), 0)
    lane = lax.broadcasted_iota(jnp.int32, (8, LAN), 1)
    black = ((row + lane) & 1) == 1
    for l in range(0, HALF, 2):
        for t in range(0, 32, 8):
            tile = slice(t, t + 8)
            out[2 * HALF + l // 2, tile, :] = jnp.where(black, pressure_v[l, tile, :], row_down(pressure_v[l + 1, tile, :]))


def edge_kernel(both, out):
    core = lax.axis_index("zk")
    start = pl.multiple_of(core * 24, 8)
    keep = (lax.broadcasted_iota(jnp.int32, (8, LAN), 0) < 4) == (core == 0)
    for k in range(PLANES):
        low = both[0, k, pl.ds(start, 8), :]
        high = both[1, k, pl.ds(start, 8), :]
        out[k] = jnp.where(keep, low, pltpu.roll(high, 4, 0))


def outer_rows(k):
    at = OWN + 8 * OUTER[k]
    return slice(at, at + 8)


def received(got, group, k):
    if k == 6:
        east = pltpu.roll(got[group, outer_rows(8), :], 6, 0)
        west = pltpu.roll(got[group, outer_rows(9), :], 3, 0)
        outer = jnp.where(lax.broadcasted_iota(jnp.int32, (8, LAN), 0) < 3, east, west)
    else:
        outer = got[group, outer_rows(k), :]
    if k in ROLLED:
        outer = pltpu.roll(outer, 4, 0)
    if k == ARRAYS - 1:
        folded = got[group, OWN - 8 : OWN, :]
        return jnp.concatenate([folded, pltpu.roll(folded, 7, 0), outer], axis=0)
    return jnp.concatenate([got[group, 16 * k : 16 * k + 16, :], outer], axis=0)


def first_kernel(both, halo, send, ef, nf, vf, dg, fr, rc, mm, al, be, ga):
    core = lax.axis_index("zk")
    row, lane, red = iotas()
    last_lane = lane == LAN - 1
    row8 = lax.broadcasted_iota(jnp.int32, (8, LAN), 0)
    from_near = (row8 < 4) == (core == 0)
    own_at = pl.multiple_of(core * 16, 8)
    near_at = pl.multiple_of(16 - 8 * core, 8)
    block = lax.axis_index("xy")
    inside = jnp.where(core == 0, block > 0, block < lax.axis_size("xy") - 1)

    def window(f, l):
        k = f * HALF + l % HALF if f < 2 else 2 * HALF + l % HALF // 2
        own = both[l // HALF, k, pl.ds(own_at, 16), :]
        near = both[l // HALF, k, pl.ds(near_at, 8), :]
        far = jnp.where(inside, halo[1 - core, k], 0.0)
        if l >= HALF:
            far = pltpu.roll(far, 4, 0)
        tiles = [own[0:8], own[8:16], jnp.where(from_near, near, far)]
        if f == 2 and l % 2 == 1:
            tiles = [row_up(tile) for tile in tiles]
        return jnp.concatenate(tiles, axis=0)

    for l in range(LEV):
        w = window(0, l)
        east, north = side_faces(w, last_lane)
        ef[l] = east
        nf[l] = north
        if l == 0:
            w0 = w
            vf[0] = jnp.zeros_like(w)
        else:
            vf[l] = vertical_ratio * jnp.sqrt(w * w_below)
        w_below = w
        fluid = jnp.where(w > 0.0, 1.0, 0.0)
        dg[l] = fluid * (absorption + (west_of(east) + east + south_of(north) + north)) + (1.0 - fluid)
        fr[l] = window(1, l)
    w15 = w_below
    heat0 = fr[0] + horizontal(ef[0], nf[0], window(2, 0))
    d0 = dg[0] + vf[1]
    dg[0] = d0
    for l in range(1, LEV):
        d = dg[l] + vf[l]
        if l < LEV - 1:
            d = d + vf[l + 1]
        dg[l] = d
        b = fr[l] + horizontal(ef[l], nf[l], window(2, l))
        v = vf[l]
        if l == 1:
            dd, bb, g = d, b, v
        elif l < LEV - 1:
            dd = d - mult * v
            bb = b + mult * bb
            g = mult * g
        if l < LEV - 1:
            rcp = 1.0 / dd
            mult = vf[l + 1] * rcp
            rc[l] = rcp
            mm[l] = mult
            al[l] = bb * rcp
            be[l] = g * rcp
    heat15 = b
    alpha = jnp.where(red, al[LEV - 2], 0.0)
    beta = be[LEV - 2]
    gamma = mm[LEV - 2]
    al[LEV - 2] = alpha
    ga[LEV - 2] = gamma
    for l in range(LEV - 3, 0, -1):
        mult = mm[l]
        alpha = jnp.where(red, al[l] + mult * alpha, 0.0)
        beta = be[l] + mult * beta
        gamma = mult * gamma
        al[l] = alpha
        be[l] = beta
        ga[l] = gamma
    v1 = vf[1]
    v15 = vf[LEV - 1]
    self_low = v1 * be[1]
    self_high = v15 * ga[LEV - 2]
    e_tt, e_bb = ef[0], ef[LEV - 1]
    n_tt, n_bb = nf[0], nf[LEV - 1]
    e_tb = e_bt = n_tb = n_bt = jnp.zeros((WIN, LAN), F32)
    con_low = fr[0]
    con_high = fr[LEV - 1]
    for l in range(1, LEV - 1):
        beta, gamma, alpha = be[l], ga[l], al[l]
        east, north = ef[l], nf[l]
        there_b, there_g = east_of(beta), east_of(gamma)
        mine_b, mine_g = east * beta, east * gamma
        e_tt = e_tt + mine_b * there_b
        e_tb = e_tb + mine_b * there_g
        e_bt = e_bt + mine_g * there_b
        e_bb = e_bb + mine_g * there_g
        there_b, there_g = north_of(beta), north_of(gamma)
        mine_b, mine_g = north * beta, north * gamma
        n_tt = n_tt + mine_b * there_b
        n_tb = n_tb + mine_b * there_g
        n_bt = n_bt + mine_g * there_b
        n_bb = n_bb + mine_g * there_g
        b = fr[l] + horizontal(east, north, alpha)
        con_low = con_low + beta * b
        con_high = con_high + gamma * b
    own_low = v1 * al[1]
    own_high = v15 * al[LEV - 2]
    common = [d0 - self_low, v15 * be[LEV - 2], dg[LEV - 1] - self_high, w0, w15]
    common += [jnp.where(red, heat0 + own_low, con_low), jnp.where(red, heat15 + own_high, con_high)]
    common += [e_tt, e_tb, e_bt, e_bb, n_tt, n_tb, n_bt, n_bb]
    chip = lax.axis_index("zc")
    row8 = lax.broadcasted_iota(jnp.int32, (8, LAN), 0)
    upward = fr[LEV - 1] + own_high
    downward = fr[0] + own_low
    outer = [value[16:24] for value in common]
    inner = (row8 < 2) | (row8 > 5)
    for k in (11, 13):
        outer[k] = jnp.where(inner, outer[k], pltpu.roll(outer[k + 1], 4, 0))
    kept = (row8 < 2) | (row8 > 4)
    outer[8] = jnp.where(kept, outer[8], pltpu.roll(outer[6], 2, 0))
    outer[9] = jnp.where(kept, outer[9], pltpu.roll(outer[6], 5, 0))
    for peer in range(4):
        last = jnp.where(chip < peer, upward, downward)
        for k in range(ARRAYS):
            if k < ARRAYS - 1:
                send[peer, 16 * k : 16 * k + 16, :] = common[k][0:16]
            else:
                send[peer, OWN - 8 : OWN, :] = jnp.where(red[0:8], last[0:8], pltpu.roll(last[8:16], 1, 0))
            if k in ROLLED or k == 6:
                continue
            tile = outer[k]
            if k == 7:
                tile = jnp.where(kept, tile, pltpu.roll(last[16:24], 4, 0))
            send[peer, outer_rows(k), :] = tile


def chain_factor(diag, link):
    rcp = [None] * 8
    for j in range(4):
        pivot = diag[j] if j == 0 else diag[j] - link[j] * link[j] * rcp[j - 1]
        rcp[j] = 1.0 / pivot
    for j in range(7, 4, -1):
        pivot = diag[j] if j == 7 else diag[j] - link[j + 1] * link[j + 1] * rcp[j + 1]
        rcp[j] = 1.0 / pivot
    rcp[4] = 1.0 / (diag[4] - link[4] * link[4] * rcp[3] - link[5] * link[5] * rcp[5])
    return rcp


def chain_solve(rcp, link, right):
    acc = list(right)
    for j in range(1, 4):
        acc[j] = acc[j] + link[j] * (rcp[j - 1] * acc[j - 1])
    for j in range(6, 4, -1):
        acc[j] = acc[j] + link[j + 1] * (rcp[j + 1] * acc[j + 1])
    out = [None] * 8
    out[4] = (acc[4] + link[4] * (rcp[3] * acc[3]) + link[5] * (rcp[5] * acc[5])) * rcp[4]
    for j in range(3, -1, -1):
        out[j] = (acc[j] + link[j + 1] * out[j + 1]) * rcp[j]
    for j in range(5, 8):
        out[j] = (acc[j] + link[j] * out[j - 1]) * rcp[j]
    return out


def second_kernel(got, ef, nf, vf, dg, fr, rc, mm, al, be, ga, keep, give, out, ends, heat, full, res):
    chip = lax.axis_index("zc")
    row, lane, red = iotas()
    last_lane = lane == LAN - 1
    diag, link, right = [], [None], []
    for group in range(4):
        up, down = received(got, group, 0), received(got, group, 2)
        if group > 0:
            up = up + face
        if group < 3:
            face = vertical_ratio * jnp.sqrt(received(got, group, 4) * received(got, group + 1, 3))
            down = down + face
        diag += [up, down]
        link += [received(got, group, 1)] + ([face] if group < 3 else [])
        right += [received(got, group, 5), received(got, group, 6)]
    rcp = chain_factor(diag, link)
    reds = [jnp.where(red, v, 0.0) for v in chain_solve(rcp, link, right)]
    for group in range(4):
        t, b = reds[2 * group], reds[2 * group + 1]
        e_tt, e_tb, e_bt, e_bb, n_tt, n_tb, n_bt, n_bb = (received(got, group, 7 + k) for k in range(8))
        te, be_, tn, bn = east_of(t), east_of(b), north_of(t), north_of(b)
        right[2 * group] = right[2 * group] + (
            (e_tt * te + e_tb * be_)
            + (n_tt * tn + n_tb * bn)
            + west_of(e_tt * t + e_bt * b)
            + south_of(n_tt * t + n_bt * b)
        )
        right[2 * group + 1] = right[2 * group + 1] + (
            (e_bt * te + e_bb * be_)
            + (n_bt * tn + n_bb * bn)
            + west_of(e_tb * t + e_bb * b)
            + south_of(n_tb * t + n_bb * b)
        )
    blacks = chain_solve(rcp, link, right)
    for j in range(8):
        ends[j] = jnp.where(red, reds[j], blacks[j])
        heat[j] = right[j]
    low = ends[2 * chip]
    high = ends[2 * chip + 1]
    full[2] = low
    full[LEV + 1] = high
    bb = jnp.where(red, 0.0, vf[1] * low)
    for l in range(1, LEV - 1):
        p = jnp.where(red, al[l] + be[l] * low + ga[l] * high, 0.0)
        full[l + 2] = p
        b = fr[l] + horizontal(ef[l], nf[l], p)
        bb = b + (bb if l == 1 else mm[l - 1] * bb)
        res[l] = bb * rc[l]
    cur = high
    for l in range(LEV - 2, 0, -1):
        cur = res[l] + mm[l] * cur
        full[l + 2] = jnp.where(red, full[l + 2], cur)
    for l in range(LEV):
        out[l // HALF, l % HALF] = full[l + 2, 0:16, :]

    for side in (0, 1):
        near_chip = jnp.maximum(chip - 1, 0) if side == 0 else jnp.minimum(chip + 1, 3)
        there = chip > 0 if side == 0 else chip < 3
        end = 1 - side
        w_near = jnp.where(there, received(got, near_chip, 4 - side), 0.0)
        w_own = received(got, chip, 3 + side)
        p_near = ends[2 * near_chip + end]
        p_other = ends[2 * near_chip + side]
        p_own = low if side == 0 else high
        face_own = vertical_ratio * jnp.sqrt(w_near * w_own)
        east, north = side_faces(w_near, last_lane)
        known = jnp.where(
            red, received(got, near_chip, 15) + horizontal(east, north, p_near), heat[2 * near_chip + end]
        )
        d = received(got, near_chip, 2 - 2 * side) + face_own
        beyond = known + received(got, near_chip, 1) * p_other + face_own * p_own - d * p_near
        beyond = jnp.where(there, beyond, 0.0)
        if side == 0:
            res[0] = beyond
            face_low = face_own
            p_below = p_near
        else:
            res[LEV + 1] = beyond
            face_high = face_own
            p_above = p_near
    for l in range(LEV):
        p = full[l + 2]
        d = dg[l]
        if l == 0:
            d = d + face_low
            vert = face_low * p_below + vf[1] * full[3]
        elif l == LEV - 1:
            d = d + face_high
            vert = vf[l] * full[l + 1] + face_high * p_above
        else:
            vert = vf[l] * full[l + 1] + vf[l + 1] * full[l + 3]
        applied = d * p - (horizontal(ef[l], nf[l], p) + vert)
        res[l + 1] = fr[l] - applied
    weights = restriction_matrix()
    for big in range(LEV // 2):
        z = 2 * big
        s = 0.125 * (res[z] + 3.0 * res[z + 1] + 3.0 * res[z + 2] + res[z + 3])
        e = east_of(s)
        s = 0.125 * (west_of(s) + 3.0 * s + 3.0 * e + east_of(e))
        res[z] = jnp.dot(s, weights, precision=lax.Precision.HIGHEST, preferred_element_type=F32)
        pair = res[z, pl.ds(0, 8, stride=2), :]
        out[big // 4, HALF + big % 4] = jnp.concatenate([pair, pair], axis=0)
    core = lax.axis_index("zk")
    keep[...] = out[core]
    give[...] = out[1 - core]


def last_kernel(both, keep, relaxed, coarse):
    core = lax.axis_index("zk")
    other = 1 - core
    for side, of in ((core, lambda k: keep[k]), (other, lambda k: both[other, k])):
        at = pl.multiple_of(side * 16, 8)
        for l in range(HALF):
            relaxed[l, pl.ds(at, 16), :] = of(l)
        at = pl.multiple_of(side * 8, 8)
        for big in range(4):
            coarse[big, pl.ds(at, 8), :] = of(HALF + big)[0:8, 0:64]


def restriction_matrix():
    fine = lax.broadcasted_iota(jnp.int32, (LAN, LAN), 0)
    big = lax.broadcasted_iota(jnp.int32, (LAN, LAN), 1)
    off = fine - 2 * big + 1
    inner = (off == 1) | (off == 2)
    outer = (off == 0) | (off == 3)
    return jnp.where(inner, 0.375, jnp.where(outer, 0.125, 0.0)).astype(F32)


def call(kernel, name, shapes, scratch=(), ends=""):
    vm = pl.BlockSpec(memory_space=pltpu.VMEM)
    main = pl.BlockSpec(memory_space=pltpu.HBM)

    def run(*args):
        if not INTERPRET:
            space = pltpu.HBM if ends == "first" else pltpu.VMEM
            args = [pltpu.with_memory_space_constraint(a, space) for a in args]
        plain = ends == "last" or INTERPRET
        return pl.pallas_call(
            kernel,
            out_shape=[jax.ShapeDtypeStruct(s, F32) if plain else pltpu.VMEM(s, F32) for s in shapes],
            in_specs=[main if ends == "first" else vm] * len(args),
            out_specs=[vm] * len(shapes),
            scratch_shapes=scratch,
            name=name,
            compiler_params=pltpu.CompilerParams(vmem_limit_bytes=SCOPED),
            interpret=INTERPRET,
        )(*args)

    return run


def side_by_side():
    chips, cores, count = (lax.axis_size(axis) for axis in AXES)

    def number(chip, core, q):
        return (chip * cores + core) * count + q

    groups = [[number(c, 0, q), number(c, 1, q - 1)] for c in range(chips) for q in range(1, count)]
    for c in range(0, chips, 2):
        groups.append([number(c, 0, 0), number(c + 1, 0, 0)])
        groups.append([number(c, 1, count - 1), number(c + 1, 1, count - 1)])
    return groups


def shards(source, conductivity, fluid, pressure):
    cell = (WIN, LAN)
    field = (LEV, WIN, LAN)
    block = (HALF, 32, LAN)
    vmem = pltpu.VMEM
    (mine,) = call(
        weigh_kernel,
        "weigh",
        [(PLANES, 32, LAN)],
        [vmem(block, t) for t in (F32, F32, jnp.int32, F32)] + [pltpu.SemaphoreType.DMA((4,))],
        ends="first",
    )(source, conductivity, fluid, pressure)
    both = lax.all_gather(mine, "zk", axis=0, tiled=False)
    (edge,) = call(edge_kernel, "edge", [(PLANES, 8, LAN)])(both)
    halo = lax.all_gather(edge, AXES, axis=0, tiled=False, axis_index_groups=side_by_side())
    send, *fields = call(first_kernel, "first", [(4, SENT, LAN)] + [field] * 10)(both, halo)
    got = lax.all_to_all(send, "zc", 0, 0, tiled=False)
    part = (HALF + HALF // 2, 16, LAN)
    keep, give = call(
        second_kernel,
        "second",
        [part, part],
        [vmem((2,) + part, F32)]
        + [vmem((8,) + cell, F32)] * 2
        + [vmem((LEV + 4,) + cell, F32), vmem((LEV + 2,) + cell, F32)],
    )(got, *fields)
    ends = lax.all_gather(give, "zk", axis=0, tiled=False)
    coarse = (HALF // 2, 16, LAN // 2)
    relaxed, coarse = call(
        last_kernel,
        "last",
        [block, coarse],
        ends="last",
    )(ends, keep)
    return relaxed, coarse


def solution(mesh):
    finer = Mesh(mesh.devices.reshape(4, 2, mesh.shape["xy"]), AXES)
    spec = P(("zc", "zk"), "xy", None)
    return jax.shard_map(shards, mesh=finer, in_specs=(spec,) * 4, out_specs=(spec,) * 2, check_vma=False)
```

```python
import jax
import jax.numpy as jnp
from jax import lax
from jax.experimental import pallas as pl
from jax.experimental.pallas import tpu as pltpu
from jax.sharding import Mesh
from jax.sharding import PartitionSpec as P

INTERPRET = False
AXES = ("zc", "zk", "xy")
SCOPED = 4 << 20
vertical_ratio = 100.0
absorption = 0.05

LEV = 16
HALF = 8
PLANES = 20
ARRAYS = 16
OWN = ARRAYS * 16 - 8
OUTER = (0, 1, 2, 3, 4, 5, None, 6, 7, 8, 9, 10, 10, 11, 11, 6)
ROLLED = (12, 14, 15)
SENT = OWN + 12 * 8
WIN = 24
LAN = 128
F32 = jnp.float32


def east_of(v):
    return pltpu.roll(v, WIN - 1, 0)


def west_of(v):
    return pltpu.roll(v, 1, 0)


def north_of(v):
    return pltpu.roll(v, LAN - 1, 1)


def south_of(v):
    return pltpu.roll(v, 1, 1)


def iotas():
    row = lax.broadcasted_iota(jnp.int32, (WIN, LAN), 0)
    lane = lax.broadcasted_iota(jnp.int32, (WIN, LAN), 1)
    red = ((row + lane) & 1) == 0
    return row, lane, red


def side_faces(w, last_lane):
    east = jnp.sqrt(w * east_of(w))
    north = jnp.where(last_lane, 0.0, jnp.sqrt(w * north_of(w)))
    return east, north


def horizontal(east, north, p):
    return (
        west_of(east * p)
        + east * east_of(p)
        + south_of(north * p)
        + north * north_of(p)
    )


def row_down(tile):
    row = lax.broadcasted_iota(jnp.int32, (8, LAN), 0)
    return jnp.where((row & 3) == 0, pltpu.roll(tile, 5, 0), pltpu.roll(tile, 1, 0))


def row_up(tile):
    row = lax.broadcasted_iota(jnp.int32, (8, LAN), 0)
    return jnp.where((row & 3) == 3, pltpu.roll(tile, 3, 0), pltpu.roll(tile, 7, 0))


def weigh_kernel(source, cond, fluid, pressure, out, source_v, cond_v, fluid_v, pressure_v, sems):
    copies = [
        pltpu.make_async_copy(cond, cond_v, sems.at[0]),
        pltpu.make_async_copy(fluid, fluid_v, sems.at[1]),
        pltpu.make_async_copy(source, source_v, sems.at[2]),
        pltpu.make_async_copy(pressure, pressure_v, sems.at[3]),
    ]
    for copy in copies:
        copy.start()
    for copy in copies:
        copy.wait()
    for l in range(HALF):
        real = fluid_v[l].astype(F32)
        out[l] = cond_v[l] * real
        out[HALF + l] = real * source_v[l]
    row = lax.broadcasted_iota(jnp.int32, (8, LAN), 0)
    lane = lax.broadcasted_iota(jnp.int32, (8, LAN), 1)
    black = ((row + lane) & 1) == 1
    for l in range(0, HALF, 2):
        for t in range(0, 32, 8):
            tile = slice(t, t + 8)
            out[2 * HALF + l // 2, tile, :] = jnp.where(black, pressure_v[l, tile, :], row_down(pressure_v[l + 1, tile, :]))


def edge_kernel(both, out):
    core = lax.axis_index("zk")
    start = pl.multiple_of(core * 24, 8)
    keep = (lax.broadcasted_iota(jnp.int32, (8, LAN), 0) < 4) == (core == 0)
    for k in range(PLANES):
        low = both[0, k, pl.ds(start, 8), :]
        high = both[1, k, pl.ds(start, 8), :]
        out[k] = jnp.where(keep, low, pltpu.roll(high, 4, 0))


def outer_rows(k):
    at = OWN + 8 * OUTER[k]
    return slice(at, at + 8)


def received(got, group, k):
    if k == 6:
        east = pltpu.roll(got[group, outer_rows(8), :], 6, 0)
        west = pltpu.roll(got[group, outer_rows(9), :], 3, 0)
        outer = jnp.where(lax.broadcasted_iota(jnp.int32, (8, LAN), 0) < 3, east, west)
    else:
        outer = got[group, outer_rows(k), :]
    if k in ROLLED:
        outer = pltpu.roll(outer, 4, 0)
    if k == ARRAYS - 1:
        folded = got[group, OWN - 8 : OWN, :]
        return jnp.concatenate([folded, pltpu.roll(folded, 7, 0), outer], axis=0)
    return jnp.concatenate([got[group, 16 * k : 16 * k + 16, :], outer], axis=0)


def first_kernel(both, halo, send, ef, nf, vf, dg, fr, rc, mm, al, be, ga):
    core = lax.axis_index("zk")
    row, lane, red = iotas()
    last_lane = lane == LAN - 1
    row8 = lax.broadcasted_iota(jnp.int32, (8, LAN), 0)
    from_near = (row8 < 4) == (core == 0)
    own_at = pl.multiple_of(core * 16, 8)
    near_at = pl.multiple_of(16 - 8 * core, 8)
    block = lax.axis_index("xy")
    inside = jnp.where(core == 0, block > 0, block < lax.axis_size("xy") - 1)

    def window(f, l):
        k = f * HALF + l % HALF if f < 2 else 2 * HALF + l % HALF // 2
        own = both[l // HALF, k, pl.ds(own_at, 16), :]
        near = both[l // HALF, k, pl.ds(near_at, 8), :]
        far = jnp.where(inside, halo[1 - core, k], 0.0)
        if l >= HALF:
            far = pltpu.roll(far, 4, 0)
        tiles = [own[0:8], own[8:16], jnp.where(from_near, near, far)]
        if f == 2 and l % 2 == 1:
            tiles = [row_up(tile) for tile in tiles]
        return jnp.concatenate(tiles, axis=0)

    for l in range(LEV):
        w = window(0, l)
        east, north = side_faces(w, last_lane)
        ef[l] = east
        nf[l] = north
        if l == 0:
            w0 = w
            vf[0] = jnp.zeros_like(w)
        else:
            vf[l] = vertical_ratio * jnp.sqrt(w * w_below)
        w_below = w
        fluid = jnp.where(w > 0.0, 1.0, 0.0)
        dg[l] = fluid * (absorption + (west_of(east) + east + south_of(north) + north)) + (1.0 - fluid)
        fr[l] = window(1, l)
    w15 = w_below
    heat0 = fr[0] + horizontal(ef[0], nf[0], window(2, 0))
    d0 = dg[0] + vf[1]
    dg[0] = d0
    for l in range(1, LEV):
        d = dg[l] + vf[l]
        if l < LEV - 1:
            d = d + vf[l + 1]
        dg[l] = d
        b = fr[l] + horizontal(ef[l], nf[l], window(2, l))
        v = vf[l]
        if l == 1:
            dd, bb, g = d, b, v
        elif l < LEV - 1:
            dd = d - mult * v
            bb = b + mult * bb
            g = mult * g
        if l < LEV - 1:
            rcp = 1.0 / dd
            mult = vf[l + 1] * rcp
            rc[l] = rcp
            mm[l] = mult
            al[l] = bb * rcp
            be[l] = g * rcp
    heat15 = b
    alpha = jnp.where(red, al[LEV - 2], 0.0)
    beta = be[LEV - 2]
    gamma = mm[LEV - 2]
    al[LEV - 2] = alpha
    ga[LEV - 2] = gamma
    for l in range(LEV - 3, 0, -1):
        mult = mm[l]
        alpha = jnp.where(red, al[l] + mult * alpha, 0.0)
        beta = be[l] + mult * beta
        gamma = mult * gamma
        al[l] = alpha
        be[l] = beta
        ga[l] = gamma
    v1 = vf[1]
    v15 = vf[LEV - 1]
    self_low = v1 * be[1]
    self_high = v15 * ga[LEV - 2]
    e_tt, e_bb = ef[0], ef[LEV - 1]
    n_tt, n_bb = nf[0], nf[LEV - 1]
    e_tb = e_bt = n_tb = n_bt = jnp.zeros((WIN, LAN), F32)
    con_low = fr[0]
    con_high = fr[LEV - 1]
    for l in range(1, LEV - 1):
        beta, gamma, alpha = be[l], ga[l], al[l]
        east, north = ef[l], nf[l]
        there_b, there_g = east_of(beta), east_of(gamma)
        mine_b, mine_g = east * beta, east * gamma
        e_tt = e_tt + mine_b * there_b
        e_tb = e_tb + mine_b * there_g
        e_bt = e_bt + mine_g * there_b
        e_bb = e_bb + mine_g * there_g
        there_b, there_g = north_of(beta), north_of(gamma)
        mine_b, mine_g = north * beta, north * gamma
        n_tt = n_tt + mine_b * there_b
        n_tb = n_tb + mine_b * there_g
        n_bt = n_bt + mine_g * there_b
        n_bb = n_bb + mine_g * there_g
        b = fr[l] + horizontal(east, north, alpha)
        con_low = con_low + beta * b
        con_high = con_high + gamma * b
    own_low = v1 * al[1]
    own_high = v15 * al[LEV - 2]
    common = [d0 - self_low, v15 * be[LEV - 2], dg[LEV - 1] - self_high, w0, w15]
    common += [jnp.where(red, heat0 + own_low, con_low), jnp.where(red, heat15 + own_high, con_high)]
    common += [e_tt, e_tb, e_bt, e_bb, n_tt, n_tb, n_bt, n_bb]
    chip = lax.axis_index("zc")
    row8 = lax.broadcasted_iota(jnp.int32, (8, LAN), 0)
    upward = fr[LEV - 1] + own_high
    downward = fr[0] + own_low
    outer = [value[16:24] for value in common]
    inner = (row8 < 2) | (row8 > 5)
    for k in (11, 13):
        outer[k] = jnp.where(inner, outer[k], pltpu.roll(outer[k + 1], 4, 0))
    kept = (row8 < 2) | (row8 > 4)
    outer[8] = jnp.where(kept, outer[8], pltpu.roll(outer[6], 2, 0))
    outer[9] = jnp.where(kept, outer[9], pltpu.roll(outer[6], 5, 0))
    for peer in range(4):
        last = jnp.where(chip < peer, upward, downward)
        for k in range(ARRAYS):
            if k < ARRAYS - 1:
                send[peer, 16 * k : 16 * k + 16, :] = common[k][0:16]
            else:
                send[peer, OWN - 8 : OWN, :] = jnp.where(red[0:8], last[0:8], pltpu.roll(last[8:16], 1, 0))
            if k in ROLLED or k == 6:
                continue
            tile = outer[k]
            if k == 7:
                tile = jnp.where(kept, tile, pltpu.roll(last[16:24], 4, 0))
            send[peer, outer_rows(k), :] = tile


def chain_factor(diag, link):
    rcp = [None] * 8
    for j in range(4):
        pivot = diag[j] if j == 0 else diag[j] - link[j] * link[j] * rcp[j - 1]
        rcp[j] = 1.0 / pivot
    for j in range(7, 4, -1):
        pivot = diag[j] if j == 7 else diag[j] - link[j + 1] * link[j + 1] * rcp[j + 1]
        rcp[j] = 1.0 / pivot
    rcp[4] = 1.0 / (diag[4] - link[4] * link[4] * rcp[3] - link[5] * link[5] * rcp[5])
    return rcp


def chain_solve(rcp, link, right):
    acc = list(right)
    for j in range(1, 4):
        acc[j] = acc[j] + link[j] * (rcp[j - 1] * acc[j - 1])
    for j in range(6, 4, -1):
        acc[j] = acc[j] + link[j + 1] * (rcp[j + 1] * acc[j + 1])
    out = [None] * 8
    out[4] = (acc[4] + link[4] * (rcp[3] * acc[3]) + link[5] * (rcp[5] * acc[5])) * rcp[4]
    for j in range(3, -1, -1):
        out[j] = (acc[j] + link[j + 1] * out[j + 1]) * rcp[j]
    for j in range(5, 8):
        out[j] = (acc[j] + link[j] * out[j - 1]) * rcp[j]
    return out


def second_kernel(got, ef, nf, vf, dg, fr, rc, mm, al, be, ga, keep, give, out, ends, heat, full, res):
    chip = lax.axis_index("zc")
    row, lane, red = iotas()
    last_lane = lane == LAN - 1
    diag, link, right = [], [None], []
    for group in range(4):
        up, down = received(got, group, 0), received(got, group, 2)
        if group > 0:
            up = up + face
        if group < 3:
            face = vertical_ratio * jnp.sqrt(received(got, group, 4) * received(got, group + 1, 3))
            down = down + face
        diag += [up, down]
        link += [received(got, group, 1)] + ([face] if group < 3 else [])
        right += [received(got, group, 5), received(got, group, 6)]
    rcp = chain_factor(diag, link)
    reds = [jnp.where(red, v, 0.0) for v in chain_solve(rcp, link, right)]
    for group in range(4):
        t, b = reds[2 * group], reds[2 * group + 1]
        e_tt, e_tb, e_bt, e_bb, n_tt, n_tb, n_bt, n_bb = (received(got, group, 7 + k) for k in range(8))
        te, be_, tn, bn = east_of(t), east_of(b), north_of(t), north_of(b)
        right[2 * group] = right[2 * group] + (
            (e_tt * te + e_tb * be_)
            + (n_tt * tn + n_tb * bn)
            + west_of(e_tt * t + e_bt * b)
            + south_of(n_tt * t + n_bt * b)
        )
        right[2 * group + 1] = right[2 * group + 1] + (
            (e_bt * te + e_bb * be_)
            + (n_bt * tn + n_bb * bn)
            + west_of(e_tb * t + e_bb * b)
            + south_of(n_tb * t + n_bb * b)
        )
    blacks = chain_solve(rcp, link, right)
    for j in range(8):
        ends[j] = jnp.where(red, reds[j], blacks[j])
        heat[j] = right[j]
    low = ends[2 * chip]
    high = ends[2 * chip + 1]
    full[2] = low
    full[LEV + 1] = high
    bb = jnp.where(red, 0.0, vf[1] * low)
    for l in range(1, LEV - 1):
        p = jnp.where(red, al[l] + be[l] * low + ga[l] * high, 0.0)
        full[l + 2] = p
        b = fr[l] + horizontal(ef[l], nf[l], p)
        bb = b + (bb if l == 1 else mm[l - 1] * bb)
        res[l] = bb * rc[l]
    cur = high
    for l in range(LEV - 2, 0, -1):
        cur = res[l] + mm[l] * cur
        full[l + 2] = jnp.where(red, full[l + 2], cur)
    for l in range(LEV):
        out[l // HALF, l % HALF] = full[l + 2, 0:16, :]

    for side in (0, 1):
        near_chip = jnp.maximum(chip - 1, 0) if side == 0 else jnp.minimum(chip + 1, 3)
        there = chip > 0 if side == 0 else chip < 3
        end = 1 - side
        w_near = jnp.where(there, received(got, near_chip, 4 - side), 0.0)
        w_own = received(got, chip, 3 + side)
        p_near = ends[2 * near_chip + end]
        p_other = ends[2 * near_chip + side]
        p_own = low if side == 0 else high
        face_own = vertical_ratio * jnp.sqrt(w_near * w_own)
        east, north = side_faces(w_near, last_lane)
        known = jnp.where(
            red, received(got, near_chip, 15) + horizontal(east, north, p_near), heat[2 * near_chip + end]
        )
        d = received(got, near_chip, 2 - 2 * side) + face_own
        beyond = known + received(got, near_chip, 1) * p_other + face_own * p_own - d * p_near
        beyond = jnp.where(there, beyond, 0.0)
        if side == 0:
            res[0] = beyond
            face_low = face_own
            p_below = p_near
        else:
            res[LEV + 1] = beyond
            face_high = face_own
            p_above = p_near
    for l in range(LEV):
        p = full[l + 2]
        d = dg[l]
        if l == 0:
            d = d + face_low
            vert = face_low * p_below + vf[1] * full[3]
        elif l == LEV - 1:
            d = d + face_high
            vert = vf[l] * full[l + 1] + face_high * p_above
        else:
            vert = vf[l] * full[l + 1] + vf[l + 1] * full[l + 3]
        applied = d * p - (horizontal(ef[l], nf[l], p) + vert)
        res[l + 1] = fr[l] - applied
    for big in range(LEV // 2):
        z = 2 * big
        s = 0.125 * (res[z] + 3.0 * res[z + 1] + 3.0 * res[z + 2] + res[z + 3])
        e = east_of(s)
        res[big] = 0.125 * (west_of(s) + 3.0 * s + 3.0 * e + east_of(e))
    flat = res[0:8].reshape(8 * WIN, LAN)
    flat = jnp.dot(flat, restriction_matrix(), precision=lax.Precision.HIGHEST, preferred_element_type=F32)
    res[8:16] = flat.reshape(8, WIN, LAN)
    for big in range(LEV // 2):
        pair = res[8 + big, pl.ds(0, 8, stride=2), :]
        out[big // 4, HALF + big % 4] = jnp.concatenate([pair, pair], axis=0)
    core = lax.axis_index("zk")
    keep[...] = out[core]
    give[...] = out[1 - core]


def last_kernel(both, keep, relaxed, coarse):
    core = lax.axis_index("zk")
    other = 1 - core
    for side, of in ((core, lambda k: keep[k]), (other, lambda k: both[other, k])):
        at = pl.multiple_of(side * 16, 8)
        for l in range(HALF):
            relaxed[l, pl.ds(at, 16), :] = of(l)
        at = pl.multiple_of(side * 8, 8)
        for big in range(4):
            coarse[big, pl.ds(at, 8), :] = of(HALF + big)[0:8, 0:64]


def restriction_matrix():
    fine = lax.broadcasted_iota(jnp.int32, (LAN, LAN), 0)
    big = lax.broadcasted_iota(jnp.int32, (LAN, LAN), 1)
    off = fine - 2 * big + 1
    inner = (off == 1) | (off == 2)
    outer = (off == 0) | (off == 3)
    return jnp.where(inner, 0.375, jnp.where(outer, 0.125, 0.0)).astype(F32)


def call(kernel, name, shapes, scratch=(), ends=""):
    vm = pl.BlockSpec(memory_space=pltpu.VMEM)
    main = pl.BlockSpec(memory_space=pltpu.HBM)

    def run(*args):
        if not INTERPRET:
            space = pltpu.HBM if ends == "first" else pltpu.VMEM
            args = [pltpu.with_memory_space_constraint(a, space) for a in args]
        plain = ends == "last" or INTERPRET
        return pl.pallas_call(
            kernel,
            out_shape=[jax.ShapeDtypeStruct(s, F32) if plain else pltpu.VMEM(s, F32) for s in shapes],
            in_specs=[main if ends == "first" else vm] * len(args),
            out_specs=[vm] * len(shapes),
            scratch_shapes=scratch,
            name=name,
            compiler_params=pltpu.CompilerParams(vmem_limit_bytes=SCOPED),
            interpret=INTERPRET,
        )(*args)

    return run


def side_by_side():
    chips, cores, count = (lax.axis_size(axis) for axis in AXES)

    def number(chip, core, q):
        return (chip * cores + core) * count + q

    groups = [[number(c, 0, q), number(c, 1, q - 1)] for c in range(chips) for q in range(1, count)]
    for c in range(0, chips, 2):
        groups.append([number(c, 0, 0), number(c + 1, 0, 0)])
        groups.append([number(c, 1, count - 1), number(c + 1, 1, count - 1)])
    return groups


def shards(source, conductivity, fluid, pressure):
    cell = (WIN, LAN)
    field = (LEV, WIN, LAN)
    block = (HALF, 32, LAN)
    vmem = pltpu.VMEM
    (mine,) = call(
        weigh_kernel,
        "weigh",
        [(PLANES, 32, LAN)],
        [vmem(block, t) for t in (F32, F32, jnp.int32, F32)] + [pltpu.SemaphoreType.DMA((4,))],
        ends="first",
    )(source, conductivity, fluid, pressure)
    both = lax.all_gather(mine, "zk", axis=0, tiled=False)
    (edge,) = call(edge_kernel, "edge", [(PLANES, 8, LAN)])(both)
    halo = lax.all_gather(edge, AXES, axis=0, tiled=False, axis_index_groups=side_by_side())
    send, *fields = call(first_kernel, "first", [(4, SENT, LAN)] + [field] * 10)(both, halo)
    got = lax.all_to_all(send, "zc", 0, 0, tiled=False)
    part = (HALF + HALF // 2, 16, LAN)
    keep, give = call(
        second_kernel,
        "second",
        [part, part],
        [vmem((2,) + part, F32)]
        + [vmem((8,) + cell, F32)] * 2
        + [vmem((LEV + 4,) + cell, F32), vmem((LEV + 2,) + cell, F32)],
    )(got, *fields)
    ends = lax.all_gather(give, "zk", axis=0, tiled=False)
    coarse = (HALF // 2, 16, LAN // 2)
    relaxed, coarse = call(
        last_kernel,
        "last",
        [block, coarse],
        ends="last",
    )(ends, keep)
    return relaxed, coarse


def solution(mesh):
    finer = Mesh(mesh.devices.reshape(4, 2, mesh.shape["xy"]), AXES)
    spec = P(("zc", "zk"), "xy", None)
    return jax.shard_map(shards, mesh=finer, in_specs=(spec,) * 4, out_specs=(spec,) * 2, check_vma=False)
```

```python
import jax
import jax.numpy as jnp
from jax import lax
from jax.experimental import pallas as pl
from jax.experimental.pallas import tpu as pltpu
from jax.sharding import Mesh
from jax.sharding import PartitionSpec as P

INTERPRET = False
AXES = ("zc", "zk", "xy")
SCOPED = 4 << 20
vertical_ratio = 100.0
absorption = 0.05

LEV = 16
HALF = 8
PLANES = 20
ARRAYS = 16
OWN = ARRAYS * 16 - 8
OUTER = (0, 1, 2, 3, 4, 5, None, 6, 7, 8, 9, 10, 10, 11, 11, 6)
ROLLED = (12, 14, 15)
SENT = OWN + 12 * 8
WIN = 24
LAN = 128
F32 = jnp.float32


def east_of(v):
    return pltpu.roll(v, WIN - 1, 0)


def west_of(v):
    return pltpu.roll(v, 1, 0)


def north_of(v):
    return pltpu.roll(v, LAN - 1, 1)


def south_of(v):
    return pltpu.roll(v, 1, 1)


def iotas():
    row = lax.broadcasted_iota(jnp.int32, (WIN, LAN), 0)
    lane = lax.broadcasted_iota(jnp.int32, (WIN, LAN), 1)
    red = ((row + lane) & 1) == 0
    return row, lane, red


def side_faces(w, last_lane):
    east = jnp.sqrt(w * east_of(w))
    north = jnp.where(last_lane, 0.0, jnp.sqrt(w * north_of(w)))
    return east, north


def horizontal(east, north, p):
    return (
        west_of(east * p)
        + east * east_of(p)
        + south_of(north * p)
        + north * north_of(p)
    )


def row_down(tile):
    row = lax.broadcasted_iota(jnp.int32, (8, LAN), 0)
    return jnp.where((row & 3) == 0, pltpu.roll(tile, 5, 0), pltpu.roll(tile, 1, 0))


def row_up(tile):
    row = lax.broadcasted_iota(jnp.int32, (8, LAN), 0)
    return jnp.where((row & 3) == 3, pltpu.roll(tile, 3, 0), pltpu.roll(tile, 7, 0))


def weigh_kernel(source, cond, fluid, pressure, out, source_v, cond_v, fluid_v, pressure_v, sems):
    copies = [
        pltpu.make_async_copy(cond, cond_v, sems.at[0]),
        pltpu.make_async_copy(fluid, fluid_v, sems.at[1]),
        pltpu.make_async_copy(source, source_v, sems.at[2]),
        pltpu.make_async_copy(pressure, pressure_v, sems.at[3]),
    ]
    for copy in copies:
        copy.start()
    for copy in copies:
        copy.wait()
    for l in range(HALF):
        real = fluid_v[l].astype(F32)
        out[l] = cond_v[l] * real
        out[HALF + l] = real * source_v[l]
    row = lax.broadcasted_iota(jnp.int32, (8, LAN), 0)
    lane = lax.broadcasted_iota(jnp.int32, (8, LAN), 1)
    black = ((row + lane) & 1) == 1
    for l in range(0, HALF, 2):
        for t in range(0, 32, 8):
            tile = slice(t, t + 8)
            out[2 * HALF + l // 2, tile, :] = jnp.where(black, pressure_v[l, tile, :], row_down(pressure_v[l + 1, tile, :]))


def edge_kernel(both, out):
    core = lax.axis_index("zk")
    start = pl.multiple_of(core * 24, 8)
    keep = (lax.broadcasted_iota(jnp.int32, (8, LAN), 0) < 4) == (core == 0)
    for k in range(PLANES):
        low = both[0, k, pl.ds(start, 8), :]
        high = both[1, k, pl.ds(start, 8), :]
        out[k] = jnp.where(keep, low, pltpu.roll(high, 4, 0))


def outer_rows(k):
    at = OWN + 8 * OUTER[k]
    return slice(at, at + 8)


def received(got, group, k):
    if k == 6:
        east = pltpu.roll(got[group, outer_rows(8), :], 6, 0)
        west = pltpu.roll(got[group, outer_rows(9), :], 3, 0)
        outer = jnp.where(lax.broadcasted_iota(jnp.int32, (8, LAN), 0) < 3, east, west)
    else:
        outer = got[group, outer_rows(k), :]
    if k in ROLLED:
        outer = pltpu.roll(outer, 4, 0)
    if k == ARRAYS - 1:
        folded = got[group, OWN - 8 : OWN, :]
        return jnp.concatenate([folded, pltpu.roll(folded, 7, 0), outer], axis=0)
    return jnp.concatenate([got[group, 16 * k : 16 * k + 16, :], outer], axis=0)


def first_kernel(both, halo, send, ef, nf, vf, dg, fr, rc, mm, al, be, ga):
    core = lax.axis_index("zk")
    row, lane, red = iotas()
    last_lane = lane == LAN - 1
    row8 = lax.broadcasted_iota(jnp.int32, (8, LAN), 0)
    from_near = (row8 < 4) == (core == 0)
    own_at = pl.multiple_of(core * 16, 8)
    near_at = pl.multiple_of(16 - 8 * core, 8)
    block = lax.axis_index("xy")
    inside = jnp.where(core == 0, block > 0, block < lax.axis_size("xy") - 1)

    def window(f, l):
        k = f * HALF + l % HALF if f < 2 else 2 * HALF + l % HALF // 2
        own = both[l // HALF, k, pl.ds(own_at, 16), :]
        near = both[l // HALF, k, pl.ds(near_at, 8), :]
        far = jnp.where(inside, halo[1 - core, k], 0.0)
        if l >= HALF:
            far = pltpu.roll(far, 4, 0)
        tiles = [own[0:8], own[8:16], jnp.where(from_near, near, far)]
        if f == 2 and l % 2 == 1:
            tiles = [row_up(tile) for tile in tiles]
        return jnp.concatenate(tiles, axis=0)

    for l in range(LEV):
        w = window(0, l)
        east, north = side_faces(w, last_lane)
        ef[l] = east
        nf[l] = north
        if l == 0:
            w0 = w
            vf[0] = jnp.zeros_like(w)
        else:
            vf[l] = vertical_ratio * jnp.sqrt(w * w_below)
        w_below = w
        fluid = jnp.where(w > 0.0, 1.0, 0.0)
        dg[l] = fluid * (absorption + (west_of(east) + east + south_of(north) + north)) + (1.0 - fluid)
        fr[l] = window(1, l)
    w15 = w_below
    heat0 = fr[0] + horizontal(ef[0], nf[0], window(2, 0))
    d0 = dg[0] + vf[1]
    dg[0] = d0
    for l in range(1, LEV):
        d = dg[l] + vf[l]
        if l < LEV - 1:
            d = d + vf[l + 1]
        dg[l] = d
        b = fr[l] + horizontal(ef[l], nf[l], window(2, l))
        v = vf[l]
        if l == 1:
            dd, bb, g = d, b, v
        elif l < LEV - 1:
            dd = d - mult * v
            bb = b + mult * bb
            g = mult * g
        if l < LEV - 1:
            rcp = 1.0 / dd
            mult = vf[l + 1] * rcp
            rc[l] = rcp
            mm[l] = mult
            al[l] = bb * rcp
            be[l] = g * rcp
    heat15 = b
    alpha = jnp.where(red, al[LEV - 2], 0.0)
    beta = be[LEV - 2]
    gamma = mm[LEV - 2]
    al[LEV - 2] = alpha
    ga[LEV - 2] = gamma
    for l in range(LEV - 3, 0, -1):
        mult = mm[l]
        alpha = jnp.where(red, al[l] + mult * alpha, 0.0)
        beta = be[l] + mult * beta
        gamma = mult * gamma
        al[l] = alpha
        be[l] = beta
        ga[l] = gamma
    v1 = vf[1]
    v15 = vf[LEV - 1]
    self_low = v1 * be[1]
    self_high = v15 * ga[LEV - 2]
    e_tt, e_bb = ef[0], ef[LEV - 1]
    n_tt, n_bb = nf[0], nf[LEV - 1]
    e_tb = e_bt = n_tb = n_bt = jnp.zeros((WIN, LAN), F32)
    con_low = fr[0]
    con_high = fr[LEV - 1]
    for l in range(1, LEV - 1):
        beta, gamma, alpha = be[l], ga[l], al[l]
        east, north = ef[l], nf[l]
        there_b, there_g = east_of(beta), east_of(gamma)
        mine_b, mine_g = east * beta, east * gamma
        e_tt = e_tt + mine_b * there_b
        e_tb = e_tb + mine_b * there_g
        e_bt = e_bt + mine_g * there_b
        e_bb = e_bb + mine_g * there_g
        there_b, there_g = north_of(beta), north_of(gamma)
        mine_b, mine_g = north * beta, north * gamma
        n_tt = n_tt + mine_b * there_b
        n_tb = n_tb + mine_b * there_g
        n_bt = n_bt + mine_g * there_b
        n_bb = n_bb + mine_g * there_g
        b = fr[l] + horizontal(east, north, alpha)
        con_low = con_low + beta * b
        con_high = con_high + gamma * b
    own_low = v1 * al[1]
    own_high = v15 * al[LEV - 2]
    common = [d0 - self_low, v15 * be[LEV - 2], dg[LEV - 1] - self_high, w0, w15]
    common += [jnp.where(red, heat0 + own_low, con_low), jnp.where(red, heat15 + own_high, con_high)]
    common += [e_tt, e_tb, e_bt, e_bb, n_tt, n_tb, n_bt, n_bb]
    chip = lax.axis_index("zc")
    row8 = lax.broadcasted_iota(jnp.int32, (8, LAN), 0)
    upward = fr[LEV - 1] + own_high
    downward = fr[0] + own_low
    outer = [value[16:24] for value in common]
    inner = (row8 < 2) | (row8 > 5)
    for k in (11, 13):
        outer[k] = jnp.where(inner, outer[k], pltpu.roll(outer[k + 1], 4, 0))
    kept = (row8 < 2) | (row8 > 4)
    outer[8] = jnp.where(kept, outer[8], pltpu.roll(outer[6], 2, 0))
    outer[9] = jnp.where(kept, outer[9], pltpu.roll(outer[6], 5, 0))
    for peer in range(4):
        last = jnp.where(chip < peer, upward, downward)
        for k in range(ARRAYS):
            if k < ARRAYS - 1:
                send[peer, 16 * k : 16 * k + 16, :] = common[k][0:16]
            else:
                send[peer, OWN - 8 : OWN, :] = jnp.where(red[0:8], last[0:8], pltpu.roll(last[8:16], 1, 0))
            if k in ROLLED or k == 6:
                continue
            tile = outer[k]
            if k == 7:
                tile = jnp.where(kept, tile, pltpu.roll(last[16:24], 4, 0))
            send[peer, outer_rows(k), :] = tile


def chain_factor(diag, link):
    rcp = [None] * 8
    for j in range(4):
        pivot = diag[j] if j == 0 else diag[j] - link[j] * link[j] * rcp[j - 1]
        rcp[j] = 1.0 / pivot
    for j in range(7, 4, -1):
        pivot = diag[j] if j == 7 else diag[j] - link[j + 1] * link[j + 1] * rcp[j + 1]
        rcp[j] = 1.0 / pivot
    rcp[4] = 1.0 / (diag[4] - link[4] * link[4] * rcp[3] - link[5] * link[5] * rcp[5])
    return rcp


def chain_solve(rcp, link, right):
    acc = list(right)
    for j in range(1, 4):
        acc[j] = acc[j] + link[j] * (rcp[j - 1] * acc[j - 1])
    for j in range(6, 4, -1):
        acc[j] = acc[j] + link[j + 1] * (rcp[j + 1] * acc[j + 1])
    out = [None] * 8
    out[4] = (acc[4] + link[4] * (rcp[3] * acc[3]) + link[5] * (rcp[5] * acc[5])) * rcp[4]
    for j in range(3, -1, -1):
        out[j] = (acc[j] + link[j + 1] * out[j + 1]) * rcp[j]
    for j in range(5, 8):
        out[j] = (acc[j] + link[j] * out[j - 1]) * rcp[j]
    return out


def second_kernel(got, ef, nf, vf, dg, fr, rc, mm, al, be, ga, keep, give, out, ends, heat, full, res):
    chip = lax.axis_index("zc")
    row, lane, red = iotas()
    last_lane = lane == LAN - 1
    diag, link, right = [], [None], []
    for group in range(4):
        up, down = received(got, group, 0), received(got, group, 2)
        if group > 0:
            up = up + face
        if group < 3:
            face = vertical_ratio * jnp.sqrt(received(got, group, 4) * received(got, group + 1, 3))
            down = down + face
        diag += [up, down]
        link += [received(got, group, 1)] + ([face] if group < 3 else [])
        right += [received(got, group, 5), received(got, group, 6)]
    rcp = chain_factor(diag, link)
    reds = [jnp.where(red, v, 0.0) for v in chain_solve(rcp, link, right)]
    for group in range(4):
        t, b = reds[2 * group], reds[2 * group + 1]
        e_tt, e_tb, e_bt, e_bb, n_tt, n_tb, n_bt, n_bb = (received(got, group, 7 + k) for k in range(8))
        te, be_, tn, bn = east_of(t), east_of(b), north_of(t), north_of(b)
        right[2 * group] = right[2 * group] + (
            (e_tt * te + e_tb * be_)
            + (n_tt * tn + n_tb * bn)
            + west_of(e_tt * t + e_bt * b)
            + south_of(n_tt * t + n_bt * b)
        )
        right[2 * group + 1] = right[2 * group + 1] + (
            (e_bt * te + e_bb * be_)
            + (n_bt * tn + n_bb * bn)
            + west_of(e_tb * t + e_bb * b)
            + south_of(n_tb * t + n_bb * b)
        )
    blacks = chain_solve(rcp, link, right)
    for j in range(8):
        ends[j] = jnp.where(red, reds[j], blacks[j])
        heat[j] = right[j]
    low = ends[2 * chip]
    high = ends[2 * chip + 1]
    full[2] = low
    full[LEV + 1] = high
    bb = jnp.where(red, 0.0, vf[1] * low)
    for l in range(1, LEV - 1):
        p = jnp.where(red, al[l] + be[l] * low + ga[l] * high, 0.0)
        full[l + 2] = p
        b = fr[l] + horizontal(ef[l], nf[l], p)
        bb = b + (bb if l == 1 else mm[l - 1] * bb)
        res[l] = bb * rc[l]
    cur = high
    for l in range(LEV - 2, 0, -1):
        cur = res[l] + mm[l] * cur
        full[l + 2] = jnp.where(red, full[l + 2], cur)
    for l in range(LEV):
        out[l // HALF, l % HALF] = full[l + 2, 0:16, :]

    for side in (0, 1):
        near_chip = jnp.maximum(chip - 1, 0) if side == 0 else jnp.minimum(chip + 1, 3)
        there = chip > 0 if side == 0 else chip < 3
        end = 1 - side
        w_near = jnp.where(there, received(got, near_chip, 4 - side), 0.0)
        w_own = received(got, chip, 3 + side)
        p_near = ends[2 * near_chip + end]
        p_other = ends[2 * near_chip + side]
        p_own = low if side == 0 else high
        face_own = vertical_ratio * jnp.sqrt(w_near * w_own)
        east, north = side_faces(w_near, last_lane)
        known = jnp.where(
            red, received(got, near_chip, 15) + horizontal(east, north, p_near), heat[2 * near_chip + end]
        )
        d = received(got, near_chip, 2 - 2 * side) + face_own
        beyond = known + received(got, near_chip, 1) * p_other + face_own * p_own - d * p_near
        beyond = jnp.where(there, beyond, 0.0)
        if side == 0:
            res[0] = beyond
            face_low = face_own
            p_below = p_near
        else:
            res[LEV + 1] = beyond
            face_high = face_own
            p_above = p_near
    for l in range(LEV):
        p = full[l + 2]
        d = dg[l]
        if l == 0:
            d = d + face_low
            vert = face_low * p_below + vf[1] * full[3]
        elif l == LEV - 1:
            d = d + face_high
            vert = vf[l] * full[l + 1] + face_high * p_above
        else:
            vert = vf[l] * full[l + 1] + vf[l + 1] * full[l + 3]
        applied = d * p - (horizontal(ef[l], nf[l], p) + vert)
        res[l + 1] = fr[l] - applied
    for big in range(LEV // 2):
        z = 2 * big
        s = 0.125 * (res[z] + 3.0 * res[z + 1] + 3.0 * res[z + 2] + res[z + 3])
        e = east_of(s)
        res[big] = 0.125 * (west_of(s) + 3.0 * s + 3.0 * e + east_of(e))
    flat = jnp.concatenate([res[big, pl.ds(0, 8, stride=2), :] for big in range(LEV // 2)], axis=0)
    flat = jnp.dot(flat, restriction_matrix(), precision=lax.Precision.HIGHEST, preferred_element_type=F32)
    for big in range(LEV // 2):
        pair = flat[8 * big : 8 * big + 8]
        out[big // 4, HALF + big % 4] = jnp.concatenate([pair, pair], axis=0)
    core = lax.axis_index("zk")
    keep[...] = out[core]
    give[...] = out[1 - core]


def last_kernel(both, keep, relaxed, coarse):
    core = lax.axis_index("zk")
    other = 1 - core
    for side, of in ((core, lambda k: keep[k]), (other, lambda k: both[other, k])):
        at = pl.multiple_of(side * 16, 8)
        for l in range(HALF):
            relaxed[l, pl.ds(at, 16), :] = of(l)
        at = pl.multiple_of(side * 8, 8)
        for big in range(4):
            coarse[big, pl.ds(at, 8), :] = of(HALF + big)[0:8, 0:64]


def restriction_matrix():
    fine = lax.broadcasted_iota(jnp.int32, (LAN, LAN), 0)
    big = lax.broadcasted_iota(jnp.int32, (LAN, LAN), 1)
    off = fine - 2 * big + 1
    inner = (off == 1) | (off == 2)
    outer = (off == 0) | (off == 3)
    return jnp.where(inner, 0.375, jnp.where(outer, 0.125, 0.0)).astype(F32)


def call(kernel, name, shapes, scratch=(), ends=""):
    vm = pl.BlockSpec(memory_space=pltpu.VMEM)
    main = pl.BlockSpec(memory_space=pltpu.HBM)

    def run(*args):
        if not INTERPRET:
            space = pltpu.HBM if ends == "first" else pltpu.VMEM
            args = [pltpu.with_memory_space_constraint(a, space) for a in args]
        plain = ends == "last" or INTERPRET
        return pl.pallas_call(
            kernel,
            out_shape=[jax.ShapeDtypeStruct(s, F32) if plain else pltpu.VMEM(s, F32) for s in shapes],
            in_specs=[main if ends == "first" else vm] * len(args),
            out_specs=[vm] * len(shapes),
            scratch_shapes=scratch,
            name=name,
            compiler_params=pltpu.CompilerParams(vmem_limit_bytes=SCOPED),
            interpret=INTERPRET,
        )(*args)

    return run


def side_by_side():
    chips, cores, count = (lax.axis_size(axis) for axis in AXES)

    def number(chip, core, q):
        return (chip * cores + core) * count + q

    groups = [[number(c, 0, q), number(c, 1, q - 1)] for c in range(chips) for q in range(1, count)]
    for c in range(0, chips, 2):
        groups.append([number(c, 0, 0), number(c + 1, 0, 0)])
        groups.append([number(c, 1, count - 1), number(c + 1, 1, count - 1)])
    return groups


def shards(source, conductivity, fluid, pressure):
    cell = (WIN, LAN)
    field = (LEV, WIN, LAN)
    block = (HALF, 32, LAN)
    vmem = pltpu.VMEM
    (mine,) = call(
        weigh_kernel,
        "weigh",
        [(PLANES, 32, LAN)],
        [vmem(block, t) for t in (F32, F32, jnp.int32, F32)] + [pltpu.SemaphoreType.DMA((4,))],
        ends="first",
    )(source, conductivity, fluid, pressure)
    both = lax.all_gather(mine, "zk", axis=0, tiled=False)
    (edge,) = call(edge_kernel, "edge", [(PLANES, 8, LAN)])(both)
    halo = lax.all_gather(edge, AXES, axis=0, tiled=False, axis_index_groups=side_by_side())
    send, *fields = call(first_kernel, "first", [(4, SENT, LAN)] + [field] * 10)(both, halo)
    got = lax.all_to_all(send, "zc", 0, 0, tiled=False)
    part = (HALF + HALF // 2, 16, LAN)
    keep, give = call(
        second_kernel,
        "second",
        [part, part],
        [vmem((2,) + part, F32)]
        + [vmem((8,) + cell, F32)] * 2
        + [vmem((LEV + 4,) + cell, F32), vmem((LEV + 2,) + cell, F32)],
    )(got, *fields)
    ends = lax.all_gather(give, "zk", axis=0, tiled=False)
    coarse = (HALF // 2, 16, LAN // 2)
    relaxed, coarse = call(
        last_kernel,
        "last",
        [block, coarse],
        ends="last",
    )(ends, keep)
    return relaxed, coarse


def solution(mesh):
    finer = Mesh(mesh.devices.reshape(4, 2, mesh.shape["xy"]), AXES)
    spec = P(("zc", "zk"), "xy", None)
    return jax.shard_map(shards, mesh=finer, in_specs=(spec,) * 4, out_specs=(spec,) * 2, check_vma=False)
```
